32 devices in a mesh: net: 2 (over core), dp: 2 (over x), depth: 8 (over z, y).
Axes of the slice: x: 2, y: 2, z: 4, core: 2. Of those that a mesh axis runs over, the one named last changes fastest.
Arguments:
- features: bfloat16 [2, 2, 16, 64, 16, 128], P('net', 'dp', None, 'depth'), may hold values from -16 to 16
- labels: int32 [2, 64, 16, 128], P('dp', 'depth'), may hold values from 0 to 7
- masks: int32 [2, 2, 64, 16, 128], P('net', 'dp', 'depth'), may hold values 0 or 1
- conv_kernel: bfloat16 [2, 27, 16, 16], P('net'), may hold values from -0.3125 to 0.3125
- conv_bias: float32 [2, 16], P('net'), may hold values from -3 to 3
- head_weight: bfloat16 [2, 8, 16], P('net'), may hold values from -1.5 to 1.5
- head_bias: float32 [2, 8], P('net'), may hold values from -3 to 3
Outputs:
- grad_input: bfloat16 [2, 2, 16, 64, 16, 128], P('net', 'dp', None, 'depth')
- grad_kernel: float32 [2, 27, 16, 16], P('net')
- grad_bias: float32 [2, 16], P('net')
- grad_head: float32 [2, 8, 16], P('net')
- grad_head_bias: float32 [2, 8], P('net')
The draws below stay inside these ranges and needn't reach their ends.
All inputs are finite; a program needn't handle non-finite values. No bound on the sum of `masks` on one device may be relied on, other than what follows from the above.
Results may differ from the reference program's by a relative error of at most 0.0063.
Values may be sent and summed in bfloat16 or wider, within the bound.
No kernel may reach another device: no remote copies, remote signals or barrier semaphores. Data moves between devices by JAX's collectives and lax.ppermute only.
A program may use at most 64 MiB of HBM per device.

```python
import jax
import jax.numpy as jnp
from jax import lax

CH = 16
CLASSES = 8
HH = 16
WW = 128
NETS = 2
CROPS = 2
DEPTH = 64
VOXELS = 262144


def draw_features(key, part):
    base_key, scale_key = jax.random.split(key)
    full_shape = (NETS, CROPS, CH, DEPTH, HH, WW)
    base_draw = jnp.clip(jax.random.normal(base_key, full_shape, jnp.float32), -6.0, 6.0)
    factor = jnp.exp(jax.random.uniform(scale_key, (NETS, CROPS, CH, DEPTH, 1, 1), jnp.float32, -0.35, 0.35))
    plane_pos = jnp.arange(DEPTH, dtype=jnp.float32) / DEPTH
    rising = 0.6 * jnp.exp(jnp.log(3.0) * plane_pos)[:, None, None]
    return (base_draw * factor * rising).astype(jnp.bfloat16)


def with_ends(values, key, smallest, high):
    longest = values.shape.index(max(values.shape))
    spots = []
    for shift in (0, 1):
        where = [jax.random.randint(jax.random.fold_in(key, axis), (), 0, length) for axis, length in enumerate(values.shape)]
        where[longest] = (where[longest] + shift) % values.shape[longest]
        spots.append(tuple(where))
    return values.at[spots[0]].set(smallest).at[spots[1]].set(high)


def levels(rng, extent, cuts, least, top_value):
    def one(position, parts):
        steps = jax.random.uniform(jax.random.fold_in(jax.random.fold_in(rng, 6), position), (parts,), jnp.float32, least / len(cuts), top_value / len(cuts))
        return jnp.repeat(jnp.exp(steps), extent[position] // parts).reshape((-1,) + (1,) * (len(extent) - position - 1))

    gain = one(*cuts[0])
    for cut in cuts[1:]:
        gain = gain * one(*cut)
    return gain


def centred(stream_key, dims, spread, most, cuts=(), kind=jnp.bfloat16):
    drawn = spread * jax.random.normal(stream_key, dims, jnp.float32)
    if cuts:
        drawn = drawn * levels(stream_key, dims, cuts, -0.22, 0.18)
    return jnp.clip(drawn, -most, most).astype(kind)


def setup_inputs(seed: int = 0) -> dict:
    streams_of = jax.random.split(jax.random.key(seed), 8)
    features = draw_features(jax.random.fold_in(streams_of[7], 71), 0)
    labels = with_ends(jax.random.randint(streams_of[1], (CROPS, DEPTH, HH, WW), 0, CLASSES), jax.random.fold_in(streams_of[1], 1), 0, CLASSES - 1).astype(jnp.int32)
    masks = with_ends((jax.random.randint(streams_of[2], (NETS, CROPS, DEPTH, HH, WW), 0, 2) < 1).astype(jnp.int32), jax.random.fold_in(streams_of[2], 1), 0, 1)
    conv_kernel = centred(streams_of[3], (NETS, 27, CH, CH), (27 * CH) ** -0.5, 0.3125, ((0, 2),))
    conv_bias = centred(streams_of[4], (NETS, CH), 0.5, 3.0, ((0, 2),), jnp.float32)
    head_weight = centred(streams_of[5], (NETS, CLASSES, CH), CH ** -0.5, 1.5, ((0, 2),))
    head_bias = centred(streams_of[6], (NETS, CLASSES), 0.5, 3.0, ((0, 2),), jnp.float32)
    return {"features": features, "labels": labels, "masks": masks, "conv_kernel": conv_kernel, "conv_bias": conv_bias, "head_weight": head_weight, "head_bias": head_bias}


def correlate(field, kernel):
    filters = kernel.reshape(3, 3, 3, kernel.shape[1], kernel.shape[2]).transpose(3, 4, 0, 1, 2)
    result = lax.conv_general_dilated(field[None], filters, (1, 1, 1), ((1, 1), (1, 1), (1, 1)), dimension_numbers=('NCDHW', 'OIDHW', 'NCDHW'), precision=lax.Precision.HIGHEST)
    return result[0]

def net_forward(field, kernel, bias_vec, head_mat, head_off, label_map):
    preact = correlate(field, kernel) + bias_vec[:, None, None, None]
    hidden = jnp.maximum(preact, 0.0).astype(jnp.bfloat16)
    logits = jnp.einsum('kc,cdhw->kdhw', head_mat.astype(jnp.float32), hidden.astype(jnp.float32), precision=lax.Precision.HIGHEST) + head_off[:, None, None, None]
    log_total = jnp.log(lax.optimization_barrier(jnp.sum(jnp.exp(logits), axis=0)))
    classes = jnp.arange(logits.shape[0], dtype=jnp.int32)
    onehot = (label_map[None] == classes[:, None, None, None]).astype(jnp.float32)
    cross_ent = log_total - lax.optimization_barrier(jnp.sum(onehot * logits, axis=0))
    soft_probs = jnp.exp(logits - log_total[None])
    return (preact, hidden, cross_ent, soft_probs, onehot)

def reference(features, labels, masks, conv_kernel, conv_bias, head_weight, head_bias):
    crop_count = features.shape[1]
    input_lists = [[], []]
    kernel_sums = [jnp.zeros(conv_kernel.shape[1:], jnp.float32) for n in range(2)]
    bias_sums = [jnp.zeros(conv_bias.shape[1:], jnp.float32) for n in range(2)]
    head_sums = [jnp.zeros(head_weight.shape[1:], jnp.float32) for n in range(2)]
    offset_sums = [jnp.zeros(head_bias.shape[1:], jnp.float32) for n in range(2)]
    for crop in range(crop_count):
        fields = [features[n, crop].astype(jnp.float32) for n in range(2)]
        kernels = [conv_kernel[n].astype(jnp.float32) for n in range(2)]
        states = [net_forward(fields[n], kernels[n], conv_bias[n], head_weight[n], head_bias[n], labels[crop]) for n in range(2)]
        offered = [masks[n, crop].astype(jnp.float32) * jnp.exp(-states[n][2]) for n in range(2)]
        for n in range(2):
            preact, hidden, cross_ent, soft_probs, onehot = states[n]
            peer_weight = offered[1 - n]
            logit_grad = peer_weight[None] * (soft_probs - onehot)
            logit_half = logit_grad.astype(jnp.bfloat16)
            hidden_grad = jnp.einsum('kc,kdhw->cdhw', head_weight[n].astype(jnp.float32), logit_half.astype(jnp.float32), precision=lax.Precision.HIGHEST)
            pre_grad = jnp.where(preact > 0.0, hidden_grad, 0.0)
            pre_half = pre_grad.astype(jnp.bfloat16)
            unused, pullback = jax.vjp(correlate, fields[n], kernels[n])
            input_grad, kernel_grad = pullback(pre_half.astype(jnp.float32))
            input_lists[n].append(input_grad.astype(jnp.bfloat16))
            kernel_sums[n] = kernel_sums[n] + kernel_grad
            bias_sums[n] = bias_sums[n] + lax.optimization_barrier(jnp.sum(pre_grad, axis=(1, 2, 3)))
            head_sums[n] = head_sums[n] + jnp.einsum('kdhw,cdhw->kc', logit_half.astype(jnp.float32), hidden.astype(jnp.float32), precision=lax.Precision.HIGHEST)
            offset_sums[n] = offset_sums[n] + lax.optimization_barrier(jnp.sum(logit_grad, axis=(1, 2, 3)))
    inverse_count = 1.0 / VOXELS
    grad_input = jnp.stack([jnp.stack(input_lists[n]) for n in range(2)])
    grad_kernel = jnp.stack(kernel_sums) * inverse_count
    grad_bias = jnp.stack(bias_sums) * inverse_count
    grad_head = jnp.stack(head_sums) * inverse_count
    grad_head_bias = jnp.stack(offset_sums) * inverse_count
    return (grad_input, grad_kernel, grad_bias, grad_head, grad_head_bias)
```

```python
import functools

import jax
import jax.numpy as jnp
from jax import lax
from jax.experimental import pallas as pl
from jax.experimental.pallas import tpu as pltpu
from jax.sharding import PartitionSpec as P

BF = jnp.bfloat16
F32 = jnp.float32
VM = pltpu.VMEM
SM = pltpu.SMEM


def iota(shape, dim):
    return lax.broadcasted_iota(jnp.int32, shape, dim)


def dot(a, b):
    return jnp.dot(a, b, preferred_element_type=F32)


def dot_nt(a, b):
    return lax.dot_general(a, b, (((1,), (1,)), ((), ())), preferred_element_type=F32)


def split3(x):
    high = x.astype(BF)
    rest = x - high.astype(F32)
    mid = rest.astype(BF)
    return high, mid, (rest - mid.astype(F32)).astype(BF)


def dot_exact(x, ones):
    return sum(dot(part, ones) for part in split3(x))


def moved(x):
    y = x.astype(F32)
    lane = iota(y.shape, 1)
    width = y.shape[1]
    before = jnp.where(lane == 0, 0.0, pltpu.roll(y, 1, 1))
    after = jnp.where(lane == width - 1, 0.0, pltpu.roll(y, width - 1, 1))
    return before.astype(BF), after.astype(BF)


def fill_band(kernel_ref, band_ref, ch, hh):
    rows = ch * hh
    flat = kernel_ref[...].reshape(27 * ch, ch)
    spread = (iota((ch, rows), 1) // hh == iota((ch, rows), 0)).astype(F32).astype(BF)
    wide = dot(flat, spread).astype(BF)
    masks = [(iota((ch, rows), 1) % hh == h).astype(F32).astype(BF) for h in range(hh)]
    for i in range(3):
        for k in range(3):
            taps = [wide[(9 * i + 3 * j + k) * ch : (9 * i + 3 * j + k + 1) * ch] for j in range(3)]
            col = (3 * i + k) * rows
            for h in range(hh):
                block = masks[h] * taps[1]
                if h > 0:
                    block = block + masks[h - 1] * taps[0]
                if h < hh - 1:
                    block = block + masks[h + 1] * taps[2]
                band_ref[h * ch : (h + 1) * ch, col : col + rows] = block


def head_matrix(head_ref, ch, hh, classes):
    rows = ch * hh
    spread = (iota((ch, rows), 1) % ch == iota((ch, rows), 0)).astype(F32).astype(BF)
    wide = dot(head_ref[...], spread)
    wide = jnp.broadcast_to(wide[:, None, :], (classes, hh, rows))
    keep = iota((classes, hh, rows), 2) // ch == iota((classes, hh, rows), 1)
    return jnp.where(keep, wide, 0.0).reshape(classes * hh, rows).astype(BF)


def head_matrix_t(head_ref, ch, hh, classes):
    mat = head_matrix(head_ref, ch, hh, classes)
    rows = ch * hh
    unit = (iota((rows, rows), 0) == iota((rows, rows), 1)).astype(F32).astype(BF)
    return dot_nt(unit, mat).astype(BF)


def bias_rows(bias_ref, ch, width):
    out = jnp.zeros((ch, width), F32)
    sub = iota((ch, width), 0)
    for c in range(ch):
        out = jnp.where(sub == c, bias_ref[0, c], out)
    return out


def fill_shifted(x, ref, slot, rows):
    before, after = moved(x)
    ref[slot, 0:rows] = before
    ref[slot, rows : 2 * rows] = x
    ref[slot, 2 * rows : 3 * rows] = after


def forward_pair(band, shifted_ref, slot, bias, mat, head_bias_ref, label, mask, dims):
    ch, hh, ww, classes = dims
    rows = ch * hh
    left = shifted_ref[slot : slot + 3].reshape(9 * rows, ww)
    right = shifted_ref[slot + 1 : slot + 4].reshape(9 * rows, ww)
    preact = dot(band, jnp.concatenate([left, right], axis=1))
    preact = (preact.reshape(hh, ch, 2 * ww) + bias[None]).reshape(rows, 2 * ww)
    hidden = jnp.maximum(preact, 0.0).astype(BF)
    logits = dot(mat, hidden).reshape(classes, hh, 2 * ww)
    parts = [logits[c] + head_bias_ref[0, c] for c in range(classes)]
    total = functools.reduce(jnp.add, [jnp.exp(p) for p in parts])
    log_total = jnp.log(total)
    soft = [jnp.exp(p - log_total) for p in parts]
    hot = [label == c for c in range(classes)]
    chosen = functools.reduce(jnp.add, [jnp.where(o, s, 0.0) for o, s in zip(hot, soft)])
    diffs = [s - jnp.where(o, 1.0, 0.0) for o, s in zip(hot, soft)]
    return hidden, jnp.stack(diffs).reshape(classes * hh, 2 * ww), mask * chosen


def put_pair(ref, first, second, value, ww):
    ref[first] = value[:, :ww]
    ref[second] = value[:, ww:]


def interior_kernel(
    x_ref, label_ref, mask_ref, kernel_ref, bias_ref, head_ref, head_bias_ref,
    band_ref, hidden_ref, diff_ref, offered_ref, shifted_ref,
):
    ch, planes, hh, ww = x_ref.shape
    classes = head_ref.shape[0]
    rows = ch * hh
    fill_band(kernel_ref, band_ref, ch, hh)
    mat = head_matrix(head_ref, ch, hh, classes)
    bias = bias_rows(bias_ref, ch, 2 * ww)
    for d in range(planes):
        fill_shifted(x_ref[:, d].reshape(rows, ww), shifted_ref, d, rows)
    for d in range(1, planes - 1, 2):
        label = jnp.concatenate([label_ref[d], label_ref[d + 1]], axis=1)
        mask = jnp.concatenate([mask_ref[d], mask_ref[d + 1]], axis=1).astype(F32)
        hidden, diff, offered = forward_pair(
            band_ref[...], shifted_ref, d - 1, bias, mat, head_bias_ref, label, mask,
            (ch, hh, ww, classes),
        )
        put_pair(hidden_ref, d - 1, d, hidden, ww)
        put_pair(diff_ref, d - 1, d, diff, ww)
        put_pair(offered_ref, d - 1, d, offered, ww)


def edge_kernel(
    x_ref, up_ref, down_ref, label_ref, mask_ref, bias_ref, head_ref, head_bias_ref, band_ref, inner_ref,
    hidden_ref, diff_ref, offered_ref, shifted_ref,
):
    ch, planes, hh, ww = x_ref.shape
    classes = head_ref.shape[0]
    rows = ch * hh
    mat = head_matrix(head_ref, ch, hh, classes)
    bias = bias_rows(bias_ref, ch, 2 * ww)
    offered_ref[2:planes] = inner_ref[...]
    for side in range(2):
        far_ref = (up_ref, down_ref)[side]
        far = [far_ref[p * ch : (p + 1) * ch].reshape(rows, ww) for p in range(2)]
        near = [x_ref[:, p + side * (planes - 2)].reshape(rows, ww) for p in range(2)]
        for slot, x in enumerate((near + far) if side else (far + near)):
            fill_shifted(x, shifted_ref, slot, rows)
        own = side * (planes - 1)
        far_label, far_mask = far_ref[2 * ch].astype(F32).astype(jnp.int32), far_ref[2 * ch + 1].astype(F32)
        labels = [far_label, label_ref[own]]
        masks = [far_mask, mask_ref[own].astype(F32)]
        if side:
            labels, masks = labels[::-1], masks[::-1]
        hidden, diff, offered = forward_pair(
            band_ref[...], shifted_ref, 0, bias, mat, head_bias_ref,
            jnp.concatenate(labels, axis=1), jnp.concatenate(masks, axis=1), (ch, hh, ww, classes),
        )
        put_pair(hidden_ref, 2 * side, 2 * side + 1, hidden, ww)
        put_pair(diff_ref, 2 * side, 2 * side + 1, diff, ww)
        put_pair(offered_ref, side * planes, side * planes + 1, offered, ww)


def backward_kernel(
    edge_ref, x_ref, up_ref, down_ref, weight_ref, hidden_in_ref, hidden_edge_ref, diff_in_ref, diff_edge_ref,
    head_ref, shifted_ref, packed_ref, rows_ref,
):
    ch, planes, hh, ww = x_ref.shape
    classes = head_ref.shape[0]
    rows = ch * hh
    mat_t = head_matrix_t(head_ref, ch, hh, classes)
    bias_sum = jnp.zeros((rows, ww), F32)
    offset_sum = jnp.zeros((classes * hh, ww), F32)
    hiddens, halves = [], []
    for s in range(0, planes + 2, 2):
        if s == 0 or s == planes:
            a = 0 if s == 0 else 2
            hidden = [hidden_edge_ref[a], hidden_edge_ref[a + 1]]
            diff = [diff_edge_ref[a], diff_edge_ref[a + 1]]
        else:
            hidden = [hidden_in_ref[s - 2], hidden_in_ref[s - 1]]
            diff = [diff_in_ref[s - 2], diff_in_ref[s - 1]]
        grads = []
        for p in range(2):
            g = diff[p].reshape(classes, hh, ww) * weight_ref[s + p][None]
            grads.append(g.reshape(classes * hh, ww))
        half = [g.astype(BF) for g in grads]
        pre = dot(mat_t, jnp.concatenate(half, axis=1))
        for p in range(2):
            value = jnp.where(hidden[p].astype(F32) > 0.0, pre[:, p * ww : (p + 1) * ww], 0.0)
            if 1 <= s + p <= planes:
                bias_sum = bias_sum + value
                offset_sum = offset_sum + grads[p]
                hiddens.append(hidden[p])
                halves.append(half[p])
            else:
                value = jnp.where(edge_ref[0 if s + p == 0 else 1] > 0, value, 0.0)
            value = value.astype(BF)
            before, after = moved(value)
            shifted_ref[s + p, 0:rows] = after
            shifted_ref[s + p, rows : 2 * rows] = value
            shifted_ref[s + p, 2 * rows : 3 * rows] = before
    grad_cat = jnp.concatenate([shifted_ref[s] for s in range(1, planes + 1)], axis=1)
    field = [up_ref[ch : 2 * ch]] + [x_ref[:, d] for d in range(planes)] + [down_ref[0:ch]]
    field = [f.reshape(rows, ww) for f in field]
    place = iota((ch, rows), 1) % hh
    for i in range(3):
        product = dot_nt(grad_cat, jnp.concatenate(field[i : i + planes], axis=1))
        for k in range(3):
            for j in range(3):
                total = jnp.zeros((ch, rows), F32)
                for h in range(hh):
                    if 0 <= h + j - 1 < hh:
                        r = k * rows + h * ch
                        total = jnp.where(place == h + j - 1, product[r : r + ch], total)
                t = 9 * i + 3 * j + k
                rows_ref[t * ch : (t + 1) * ch] = total
    lane16 = iota((rows, 128), 1) % 16
    by_channel = (iota((rows, 128), 0) // hh == lane16).astype(F32).astype(BF)
    sums = dot_exact(rows_ref[...], by_channel)
    blocks = [sums[t * ch : (t + 1) * ch] for t in range(27)]
    product = dot_nt(jnp.concatenate(halves, axis=1), jnp.concatenate(hiddens, axis=1))
    product = product.reshape(classes, hh, rows)
    keep = iota((classes, hh, rows), 2) // ch == iota((classes, hh, rows), 1)
    head = jnp.sum(jnp.where(keep, product, 0.0), axis=1)
    by_last = (iota((rows, 128), 0) % ch == lane16).astype(F32).astype(BF)
    head = dot_exact(head, by_last)
    blocks.append(jnp.concatenate([head, jnp.zeros((ch - classes, 128), F32)], axis=0))
    ones = jnp.ones((16, ww), F32).astype(BF)
    bias = jnp.sum(bias_sum.reshape(hh, ch, ww), axis=0)
    bias = jnp.concatenate([bias] * 8, axis=0)
    blocks.append(sum(dot_nt(ones, part) for part in split3(bias)))
    offset = sum(dot_nt(ones, part) for part in split3(offset_sum))
    by_class = (iota((classes * hh, 128), 0) // hh == iota((classes * hh, 128), 1) % 16).astype(F32).astype(BF)
    blocks.append(dot_exact(offset, by_class))
    group = iota((ch, 128), 1) // 16
    for r in range(4):
        total = jnp.zeros((ch, 128), F32)
        for g in range(8):
            if 8 * r + g < len(blocks):
                total = jnp.where(group == g, blocks[8 * r + g], total)
        packed_ref[r * ch : (r + 1) * ch] = total


def input_kernel(shifted_ref, band_ref, out_ref, turned_ref):
    ch, planes, hh, ww = out_ref.shape
    rows = ch * hh
    unit = (iota((rows, rows), 0) == iota((rows, rows), 1)).astype(F32).astype(BF)
    for i in range(3):
        for k in range(3):
            block = band_ref[:, (3 * i + k) * rows : (3 * i + k + 1) * rows]
            col = (3 * (2 - i) + k) * rows
            turned_ref[:, col : col + rows] = dot_nt(unit, block).astype(BF)
    for d in range(0, planes, 2):
        left = shifted_ref[d : d + 3].reshape(9 * rows, ww)
        right = shifted_ref[d + 1 : d + 4].reshape(9 * rows, ww)
        grad = dot(turned_ref[...], jnp.concatenate([left, right], axis=1)).astype(BF)
        out_ref[:, d] = grad[:, :ww].reshape(ch, hh, ww)
        out_ref[:, d + 1] = grad[:, ww:].reshape(ch, hh, ww)


def unpack_kernel(scale, a_ref, b_ref, kernel_ref, bias_ref, head_ref, offset_ref):
    def block(t):
        r, g = t // 8, t % 8
        value = (a_ref[r * 16 : (r + 1) * 16] + b_ref[r * 16 : (r + 1) * 16]) * scale
        return pltpu.roll(value, (128 - 16 * g) % 128, 1) if g else value

    for t in range(27):
        kernel_ref[t] = block(t)[:, 0:16]
    head_ref[...] = block(27)[0:8, 0:16]
    bias_ref[...] = block(28)[0:1, 0:16]
    offset_ref[...] = block(29)[0:1, 0:8]


def call(kernel, out_shape, in_spaces, scratch, flops, args):
    moved_bytes = sum(a.size * a.dtype.itemsize for a in args)
    return pl.pallas_call(
        kernel,
        out_shape=out_shape,
        in_specs=[pl.BlockSpec(memory_space=s) for s in in_spaces],
        out_specs=jax.tree.map(lambda _: pl.BlockSpec(memory_space=VM), out_shape),
        scratch_shapes=scratch,
        compiler_params=pltpu.CompilerParams(vmem_limit_bytes=32 << 20),
        cost_estimate=pl.CostEstimate(flops=flops, bytes_accessed=moved_bytes, transcendentals=0),
    )(*args)


def body(features, labels, masks, conv_kernel, conv_bias, head_weight, head_bias):
    x, label, mask = features[0, 0], labels[0], masks[0, 0]
    kernel, head = conv_kernel[0], head_weight[0]
    ch, planes, hh, ww = x.shape
    classes = head.shape[0]
    rows = ch * hh
    sds = jax.ShapeDtypeStruct
    size, place = lax.axis_size("depth"), lax.axis_index("depth")

    def edge(first, own):
        tail = jnp.stack([label[own], mask[own]]).astype(BF)
        return jnp.concatenate([x[:, first], x[:, first + 1], tail], axis=0)

    up = lax.ppermute(edge(planes - 2, planes - 1), "depth", [(i, i + 1) for i in range(size - 1)])
    down = lax.ppermute(edge(0, 0), "depth", [(i + 1, i) for i in range(size - 1)])

    pair_flops = 2 * rows * 9 * rows * 2 * ww
    band, hidden_in, diff_in, inner = call(
        interior_kernel,
        (
            sds((rows, 9 * rows), BF),
            sds((planes - 2, rows, ww), BF),
            sds((planes - 2, classes * hh, ww), F32),
            sds((planes - 2, hh, ww), F32),
        ),
        (VM, VM, VM, VM, SM, VM, SM),
        [VM((planes, 3 * rows, ww), BF)],
        pair_flops * (planes // 2 - 1),
        (x, label, mask, kernel, conv_bias, head, head_bias),
    )
    hidden_edge, diff_edge, offered = call(
        edge_kernel,
        (
            sds((4, rows, ww), BF),
            sds((4, classes * hh, ww), F32),
            sds((planes + 2, hh, ww), F32),
        ),
        (VM, VM, VM, VM, VM, SM, VM, SM, VM, VM),
        [VM((4, 3 * rows, ww), BF)],
        pair_flops * 2,
        (x, up, down, label, mask, conv_bias, head, head_bias, band, inner),
    )
    weight = lax.ppermute(offered, "net", [(0, 1), (1, 0)])
    edges = jnp.stack([place > 0, place < size - 1]).astype(jnp.int32)
    shifted, packed = call(
        backward_kernel,
        (sds((planes + 2, 3 * rows, ww), BF), sds((4 * ch, 128), F32)),
        (SM, VM, VM, VM, VM, VM, VM, VM, VM, VM),
        [VM((27 * ch, rows), F32)],
        2 * 9 * rows * rows * planes * ww,
        (edges, x, up, down, weight, hidden_in, hidden_edge, diff_in, diff_edge, head),
    )
    grad_input = call(
        input_kernel,
        sds((ch, planes, hh, ww), BF),
        (VM, VM),
        [VM((rows, 9 * rows), BF)],
        pair_flops * planes // 2,
        (shifted, band),
    )
    rounds = [("dp", 1 << b) for b in range((lax.axis_size("dp") - 1).bit_length())]
    rounds += [("depth", 1 << b) for b in range((size - 1).bit_length())]
    for axis, bit in rounds:
        other = lax.ppermute(packed, axis, [(i, i ^ bit) for i in range(lax.axis_size(axis))])
        if (axis, bit) != rounds[-1]:
            packed = packed + other
    scale = 1.0 / (lax.axis_size("dp") * size * planes * hh * ww)
    grad_kernel, grad_bias, grad_head, grad_offset = call(
        functools.partial(unpack_kernel, scale),
        (sds((27, ch, ch), F32), sds((1, ch), F32), sds((classes, ch), F32), sds((1, classes), F32)),
        (VM, VM),
        [],
        1000,
        (packed, other),
    )
    return grad_input[None, None], grad_kernel[None], grad_bias, grad_head[None], grad_offset


def solution(mesh):
    in_specs = (
        P("net", "dp", None, "depth", None, None),
        P("dp", "depth", None, None),
        P("net", "dp", "depth", None, None),
        P("net", None, None, None),
        P("net", None),
        P("net", None, None),
        P("net", None),
    )
    out_specs = (
        P("net", "dp", None, "depth", None, None),
        P("net", None, None, None),
        P("net", None),
        P("net", None, None),
        P("net", None),
    )
    return jax.shard_map(body, mesh=mesh, in_specs=in_specs, out_specs=out_specs, check_vma=False)
```

```python
import functools

import jax
import jax.numpy as jnp
from jax import lax
from jax.experimental import pallas as pl
from jax.experimental.pallas import tpu as pltpu
from jax.sharding import PartitionSpec as P

BF = jnp.bfloat16
F32 = jnp.float32
VM = pltpu.VMEM
SM = pltpu.SMEM


def iota(shape, dim):
    return lax.broadcasted_iota(jnp.int32, shape, dim)


def dot(a, b):
    return jnp.dot(a, b, preferred_element_type=F32)


def dot_nt(a, b):
    return lax.dot_general(a, b, (((1,), (1,)), ((), ())), preferred_element_type=F32)


def split3(x):
    high = x.astype(BF)
    rest = x - high.astype(F32)
    mid = rest.astype(BF)
    return high, mid, (rest - mid.astype(F32)).astype(BF)


def dot_exact(x, ones):
    return sum(dot(part, ones) for part in split3(x))


def moved(x):
    y = x.astype(F32)
    lane = iota(y.shape, 1)
    width = y.shape[1]
    before = jnp.where(lane == 0, 0.0, pltpu.roll(y, 1, 1))
    after = jnp.where(lane == width - 1, 0.0, pltpu.roll(y, width - 1, 1))
    return before.astype(BF), after.astype(BF)


def fill_band(kernel_ref, band_ref, ch, hh):
    rows = ch * hh
    flat = kernel_ref[...].reshape(27 * ch, ch)
    spread = (iota((ch, rows), 1) // hh == iota((ch, rows), 0)).astype(F32).astype(BF)
    wide = dot(flat, spread).astype(BF)
    masks = [(iota((ch, rows), 1) % hh == h).astype(F32).astype(BF) for h in range(hh)]
    for i in range(3):
        for k in range(3):
            taps = [wide[(9 * i + 3 * j + k) * ch : (9 * i + 3 * j + k + 1) * ch] for j in range(3)]
            col = (3 * i + k) * rows
            for h in range(hh):
                block = masks[h] * taps[1]
                if h > 0:
                    block = block + masks[h - 1] * taps[0]
                if h < hh - 1:
                    block = block + masks[h + 1] * taps[2]
                band_ref[h * ch : (h + 1) * ch, col : col + rows] = block


def head_matrix(head_ref, ch, hh, classes):
    rows = ch * hh
    spread = (iota((ch, rows), 1) % ch == iota((ch, rows), 0)).astype(F32).astype(BF)
    wide = dot(head_ref[...], spread)
    wide = jnp.broadcast_to(wide[:, None, :], (classes, hh, rows))
    keep = iota((classes, hh, rows), 2) // ch == iota((classes, hh, rows), 1)
    return jnp.where(keep, wide, 0.0).reshape(classes * hh, rows).astype(BF)


def head_matrix_t(head_ref, ch, hh, classes):
    mat = head_matrix(head_ref, ch, hh, classes)
    rows = ch * hh
    unit = (iota((rows, rows), 0) == iota((rows, rows), 1)).astype(F32).astype(BF)
    return dot_nt(unit, mat).astype(BF)


def bias_rows(bias_ref, ch, width):
    out = jnp.zeros((ch, width), F32)
    sub = iota((ch, width), 0)
    for c in range(ch):
        out = jnp.where(sub == c, bias_ref[0, c], out)
    return out


def shifts(x):
    before, after = moved(x)
    return jnp.concatenate([before, x, after], axis=0)


def head_pair(preact, bias, mat, head_bias_ref, label, mask, dims):
    ch, hh, ww, classes = dims
    rows = ch * hh
    preact = (preact.reshape(hh, ch, 2 * ww) + bias[None]).reshape(rows, 2 * ww)
    hidden = jnp.maximum(preact, 0.0).astype(BF)
    logits = dot(mat, hidden).reshape(classes, hh, 2 * ww)
    parts = [logits[c] + head_bias_ref[0, c] for c in range(classes)]
    total = functools.reduce(jnp.add, [jnp.exp(p) for p in parts])
    log_total = jnp.log(total)
    soft = [jnp.exp(p - log_total) for p in parts]
    hot = [label == c for c in range(classes)]
    chosen = functools.reduce(jnp.add, [jnp.where(o, s, 0.0) for o, s in zip(hot, soft)])
    diffs = [s - jnp.where(o, 1.0, 0.0) for o, s in zip(hot, soft)]
    return hidden, jnp.stack(diffs).reshape(classes * hh, 2 * ww), mask * chosen


def put_pair(ref, first, second, value, ww):
    ref[first] = value[:, :ww]
    ref[second] = value[:, ww:]


def beside(ref, first, second):
    return jnp.concatenate([ref[first], ref[second]], axis=1)


def pack_kernel(x_ref, a_ref, b_ref, sems):
    planes = x_ref.shape[1]
    odd = lax.rem(lax.axis_index("depth"), 2)
    first = pltpu.make_async_copy(x_ref.at[:, (1 - odd) * (planes - 1)], a_ref, sems.at[0])
    second = pltpu.make_async_copy(x_ref.at[:, odd * (planes - 1)], b_ref, sems.at[1])
    first.start()
    second.start()
    first.wait()
    second.wait()


def sorted_halo(a, b):
    place, size = lax.axis_index("depth"), lax.axis_size("depth")
    odd = lax.rem(place, 2) == 1
    before, after = jnp.where(odd, a, b), jnp.where(odd, b, a)
    before = jnp.where(place > 0, before, 0.0)
    after = jnp.where(place < size - 1, after, 0.0)
    return before.astype(BF), after.astype(BF)


def interior_kernel(
    x_ref, label_ref, mask_ref, kernel_ref, bias_ref, head_ref, head_bias_ref,
    band_ref, shifted_ref, hidden_ref, diff_ref, offered_ref,
):
    ch, planes, hh, ww = x_ref.shape
    classes = head_ref.shape[0]
    rows = ch * hh
    fill_band(kernel_ref, band_ref, ch, hh)
    mat = head_matrix(head_ref, ch, hh, classes)
    bias = bias_rows(bias_ref, ch, 2 * ww)
    for d in range(planes):
        shifted_ref[d] = shifts(x_ref[:, d].reshape(rows, ww))
    for d in range(1, planes - 1, 2):
        left = shifted_ref[d - 1 : d + 2].reshape(9 * rows, ww)
        right = shifted_ref[d : d + 3].reshape(9 * rows, ww)
        preact = dot(band_ref[...], jnp.concatenate([left, right], axis=1))
        hidden, diff, offered = head_pair(
            preact, bias, mat, head_bias_ref, beside(label_ref, d, d + 1),
            beside(mask_ref, d, d + 1).astype(F32), (ch, hh, ww, classes),
        )
        put_pair(hidden_ref, d - 1, d, hidden, ww)
        put_pair(diff_ref, d - 1, d, diff, ww)
        put_pair(offered_ref, d - 1, d, offered, ww)


def edge_kernel(
    a_ref, b_ref, label_ref, mask_ref, bias_ref, head_ref, head_bias_ref, band_ref, shifted_ref, inner_ref,
    halo_ref, hidden_ref, diff_ref, offered_ref,
):
    ch, hh, ww = a_ref.shape
    planes, classes = label_ref.shape[0], head_ref.shape[0]
    rows = ch * hh
    mat = head_matrix(head_ref, ch, hh, classes)
    bias = bias_rows(bias_ref, ch, 2 * ww)
    offered_ref[1 : planes - 1] = inner_ref[...]
    before, after = sorted_halo(a_ref[...].reshape(rows, ww).astype(F32), b_ref[...].reshape(rows, ww).astype(F32))
    halo_ref[0], halo_ref[1] = before, after
    left = jnp.concatenate([shifts(before), shifted_ref[0:2].reshape(6 * rows, ww)], axis=0)
    right = jnp.concatenate([shifted_ref[planes - 2 : planes].reshape(6 * rows, ww), shifts(after)], axis=0)
    preact = dot(band_ref[...], jnp.concatenate([left, right], axis=1))
    hidden, diff, offered = head_pair(
        preact, bias, mat, head_bias_ref, beside(label_ref, 0, planes - 1),
        beside(mask_ref, 0, planes - 1).astype(F32), (ch, hh, ww, classes),
    )
    put_pair(hidden_ref, 0, 1, hidden, ww)
    put_pair(diff_ref, 0, 1, diff, ww)
    put_pair(offered_ref, 0, planes - 1, offered, ww)


def backward_kernel(
    x_ref, halo_ref, weight_ref, hidden_in_ref, hidden_edge_ref, diff_in_ref, diff_edge_ref, head_ref,
    packed_ref, a_ref, b_ref, shifted_ref, rows_ref,
):
    ch, planes, hh, ww = x_ref.shape
    classes = head_ref.shape[0]
    rows = ch * hh
    mat_t = head_matrix_t(head_ref, ch, hh, classes)
    bias_sum = jnp.zeros((rows, ww), F32)
    offset_sum = jnp.zeros((classes * hh, ww), F32)
    hiddens, halves, values = [], [], []
    for d in range(planes):
        if d == 0 or d == planes - 1:
            hiddens.append(hidden_edge_ref[min(d, 1)])
            diff = diff_edge_ref[min(d, 1)]
        else:
            hiddens.append(hidden_in_ref[d - 1])
            diff = diff_in_ref[d - 1]
        grad = (diff.reshape(classes, hh, ww) * weight_ref[d][None]).reshape(classes * hh, ww)
        offset_sum = offset_sum + grad
        halves.append(grad.astype(BF))
    for d in range(0, planes, 2):
        pre = dot(mat_t, jnp.concatenate(halves[d : d + 2], axis=1))
        for p in range(2):
            value = jnp.where(hiddens[d + p].astype(F32) > 0.0, pre[:, p * ww : (p + 1) * ww], 0.0)
            bias_sum = bias_sum + value
            value = value.astype(BF)
            values.append(value)
            before, after = moved(value)
            shifted_ref[d + p] = jnp.concatenate([after, value, before], axis=0)
    odd = lax.rem(lax.axis_index("depth"), 2) == 1
    first, last = values[0].astype(F32), values[-1].astype(F32)
    a_ref[...] = jnp.where(odd, first, last).astype(BF)
    b_ref[...] = jnp.where(odd, last, first).astype(BF)
    grad_cat = jnp.concatenate([shifted_ref[d] for d in range(planes)], axis=1)
    field = [halo_ref[0]] + [x_ref[:, d].reshape(rows, ww) for d in range(planes)] + [halo_ref[1]]
    place = iota((ch, rows), 1) % hh
    for i in range(3):
        product = dot_nt(grad_cat, jnp.concatenate(field[i : i + planes], axis=1))
        for k in range(3):
            for j in range(3):
                total = jnp.zeros((ch, rows), F32)
                for h in range(hh):
                    if 0 <= h + j - 1 < hh:
                        r = k * rows + h * ch
                        total = jnp.where(place == h + j - 1, product[r : r + ch], total)
                t = 9 * i + 3 * j + k
                for half in range(rows // 128):
                    rows_ref[half, pl.ds(t, ch, stride=32)] = total[:, 128 * half : 128 * half + 128]
    for half in range(rows // 128):
        for t in range(27, 32):
            rows_ref[half, pl.ds(t, ch, stride=32)] = jnp.zeros((ch, 128), F32)
    sums = 0.0
    for half in range(rows // 128):
        pick = (iota((ch, 128), 1) + 128 * half) // hh == iota((ch, 128), 0)
        pick = pick.astype(F32).astype(BF)
        sums = sums + sum(dot_nt(pick, part) for part in split3(rows_ref[half]))
    for q in range(ch // 4):
        packed_ref[q * ch : (q + 1) * ch] = sums[:, 128 * q : 128 * q + 128]
    product = dot_nt(jnp.concatenate(halves, axis=1), jnp.concatenate(hiddens, axis=1))
    product = product.reshape(classes, hh, rows)
    keep = iota((classes, hh, rows), 2) // ch == iota((classes, hh, rows), 1)
    head = jnp.sum(jnp.where(keep, product, 0.0), axis=1)
    by_last = (iota((rows, 128), 0) % ch == iota((rows, 128), 1) % 16).astype(F32).astype(BF)
    head = dot_exact(head, by_last)
    ones = jnp.ones((16, ww), F32).astype(BF)
    bias = jnp.sum(bias_sum.reshape(hh, ch, ww), axis=0)
    bias = jnp.concatenate([bias] * 8, axis=0)
    bias = sum(dot_nt(ones, part) for part in split3(bias))[:classes]
    offset = sum(dot_nt(ones, part) for part in split3(offset_sum))
    by_class = (iota((classes * hh, 128), 0) // hh == iota((classes * hh, 128), 1) % 16).astype(F32).astype(BF)
    offset = dot_exact(offset, by_class)[:classes]
    group = iota((classes, 128), 1) // 16
    packed_ref[4 * ch : 4 * ch + classes] = jnp.where(group == 0, head, jnp.where(group == 1, bias, offset))


def inner_grad_kernel(shifted_ref, band_ref, turned_ref, out_ref):
    ch, inner, hh, ww = out_ref.shape
    rows = ch * hh
    unit = (iota((rows, rows), 0) == iota((rows, rows), 1)).astype(F32).astype(BF)
    for i in range(3):
        for k in range(3):
            block = band_ref[:, (3 * i + k) * rows : (3 * i + k + 1) * rows]
            col = (3 * (2 - i) + k) * rows
            turned_ref[:, col : col + rows] = dot_nt(unit, block).astype(BF)
    for d in range(0, inner, 2):
        left = shifted_ref[d : d + 3].reshape(9 * rows, ww)
        right = shifted_ref[d + 1 : d + 4].reshape(9 * rows, ww)
        grad = dot(turned_ref[...], jnp.concatenate([left, right], axis=1)).astype(BF)
        out_ref[:, d] = grad[:, :ww].reshape(ch, hh, ww)
        out_ref[:, d + 1] = grad[:, ww:].reshape(ch, hh, ww)


def edge_grad_kernel(a_ref, b_ref, shifted_ref, turned_ref, inner_ref, out_ref):
    ch, planes, hh, ww = out_ref.shape
    rows = ch * hh

    def turned_shifts(x):
        before, after = moved(x)
        return jnp.concatenate([after, x, before], axis=0)

    before, after = sorted_halo(a_ref[...].astype(F32), b_ref[...].astype(F32))
    left = jnp.concatenate([turned_shifts(before), shifted_ref[0:2].reshape(6 * rows, ww)], axis=0)
    right = jnp.concatenate([shifted_ref[planes - 2 : planes].reshape(6 * rows, ww), turned_shifts(after)], axis=0)
    grad = dot(turned_ref[...], jnp.concatenate([left, right], axis=1)).astype(BF)
    out_ref[:, 0] = grad[:, :ww].reshape(ch, hh, ww)
    out_ref[:, 1 : planes - 1] = inner_ref[...]
    out_ref[:, planes - 1] = grad[:, ww:].reshape(ch, hh, ww)


def unpack_kernel(scale, a_ref, b_ref, kernel_ref, bias_ref, head_ref, offset_ref):
    ch = kernel_ref.shape[0]
    for q in range(ch // 4):
        value = (a_ref[q * ch : (q + 1) * ch] + b_ref[q * ch : (q + 1) * ch]) * scale
        for r in range(4):
            turned = pltpu.roll(value, 128 - 32 * r, 1) if r else value
            kernel_ref[4 * q + r] = turned[:, 0:27]
    value = (a_ref[4 * ch :] + b_ref[4 * ch :]) * scale
    head_ref[...] = value[:, 0:16]
    bias_ref[...] = pltpu.roll(value, 112, 1)[0:1, 0:16]
    offset_ref[...] = pltpu.roll(value, 96, 1)[0:1, 0:8]


def call(kernel, out_shape, in_spaces, scratch, flops, args):
    moved_bytes = sum(a.size * a.dtype.itemsize for a in args)
    return pl.pallas_call(
        kernel,
        out_shape=out_shape,
        in_specs=[pl.BlockSpec(memory_space=s) for s in in_spaces],
        out_specs=jax.tree.map(lambda _: pl.BlockSpec(memory_space=VM), out_shape),
        scratch_shapes=scratch,
        compiler_params=pltpu.CompilerParams(vmem_limit_bytes=32 << 20),
        cost_estimate=pl.CostEstimate(flops=flops, bytes_accessed=moved_bytes, transcendentals=0),
    )(*args)


def exchange_pairs():
    crops, size = lax.axis_size("dp"), lax.axis_size("depth")
    one, two = [], []
    for c in range(crops):
        for d in range(size):
            one.append((c * size + d, c * size + (d ^ 1)))
            e = ((d + 1) ^ 1) - 1
            if 0 <= e < size:
                two.append((c * size + d, c * size + e))
            elif crops % 2 == 0:
                two.append((c * size + d, (c ^ 1) * size + d))
    return one, two


def exchanged(a, b):
    one, two = exchange_pairs()
    return lax.ppermute(a, ("dp", "depth"), one), lax.ppermute(b, ("dp", "depth"), two)


def body(features, labels, masks, conv_kernel, conv_bias, head_weight, head_bias):
    x, label, mask = features[0, 0], labels[0], masks[0, 0]
    kernel, head = conv_kernel[0], head_weight[0]
    ch, planes, hh, ww = x.shape
    classes = head.shape[0]
    rows = ch * hh
    sds = jax.ShapeDtypeStruct
    size = lax.axis_size("depth")
    pair_flops = 2 * rows * 9 * rows * 2 * ww

    plane = sds((ch, hh, ww), BF)
    ends = call(pack_kernel, (plane, plane), (pltpu.HBM,), [pltpu.SemaphoreType.DMA((2,))], 0, (x,))
    far = exchanged(*ends)
    band, shifted, hidden_in, diff_in, inner = call(
        interior_kernel,
        (
            sds((rows, 9 * rows), BF),
            sds((planes, 3 * rows, ww), BF),
            sds((planes - 2, rows, ww), BF),
            sds((planes - 2, classes * hh, ww), F32),
            sds((planes - 2, hh, ww), F32),
        ),
        (VM, VM, VM, VM, SM, VM, SM),
        [],
        pair_flops * (planes // 2 - 1),
        (x, label, mask, kernel, conv_bias, head, head_bias),
    )
    halo, hidden_edge, diff_edge, offered = call(
        edge_kernel,
        (
            sds((2, rows, ww), BF),
            sds((2, rows, ww), BF),
            sds((2, classes * hh, ww), F32),
            sds((planes, hh, ww), F32),
        ),
        (VM, VM, VM, VM, SM, VM, SM, VM, VM, VM),
        [],
        pair_flops,
        (*far, label, mask, conv_bias, head, head_bias, band, shifted, inner),
    )
    weight = lax.ppermute(offered, "net", [(0, 1), (1, 0)])
    edge = sds((rows, ww), BF)
    packed, grad_a, grad_b, grads = call(
        backward_kernel,
        (sds((4 * ch + 8, 128), F32), edge, edge, sds((planes, 3 * rows, ww), BF)),
        (VM,) * 8,
        [VM((rows // 128, 32 * ch, 128), F32)],
        2 * 9 * rows * rows * planes * ww,
        (x, halo, weight, hidden_in, hidden_edge, diff_in, diff_edge, head),
    )
    grad_far = exchanged(grad_a, grad_b)
    turned, grad_inner = call(
        inner_grad_kernel,
        (sds((rows, 9 * rows), BF), sds((ch, planes - 2, hh, ww), BF)),
        (VM, VM),
        [],
        pair_flops * (planes // 2 - 1),
        (grads, band),
    )
    grad_input = call(
        edge_grad_kernel,
        sds((ch, planes, hh, ww), BF),
        (VM,) * 5,
        [],
        pair_flops,
        (*grad_far, grads, turned, grad_inner),
    )
    rounds = [("dp", 1 << b) for b in range((lax.axis_size("dp") - 1).bit_length())]
    rounds += [("depth", 1 << b) for b in range((size - 1).bit_length())]
    for axis, bit in rounds:
        other = lax.ppermute(packed, axis, [(i, i ^ bit) for i in range(lax.axis_size(axis))])
        if (axis, bit) != rounds[-1]:
            packed = packed + other
    scale = 1.0 / (lax.axis_size("dp") * size * planes * hh * ww)
    grad_kernel, grad_bias, grad_head, grad_offset = call(
        functools.partial(unpack_kernel, scale),
        (sds((ch, ch, 27), F32), sds((1, ch), F32), sds((classes, ch), F32), sds((1, classes), F32)),
        (VM, VM),
        [],
        1000,
        (packed, other),
    )
    return (
        grad_input[None, None],
        grad_kernel.transpose(2, 0, 1)[None],
        grad_bias,
        grad_head[None],
        grad_offset,
    )


def solution(mesh):
    in_specs = (
        P("net", "dp", None, "depth", None, None),
        P("dp", "depth", None, None),
        P("net", "dp", "depth", None, None),
        P("net", None, None, None),
        P("net", None),
        P("net", None, None),
        P("net", None),
    )
    out_specs = (
        P("net", "dp", None, "depth", None, None),
        P("net", None, None, None),
        P("net", None),
        P("net", None, None),
        P("net", None),
    )
    return jax.shard_map(body, mesh=mesh, in_specs=in_specs, out_specs=out_specs, check_vma=False)
```

```python
import functools

import jax
import jax.numpy as jnp
from jax import lax
from jax.experimental import pallas as pl
from jax.experimental.pallas import tpu as pltpu
from jax.sharding import PartitionSpec as P

BF = jnp.bfloat16
F32 = jnp.float32
VM = pltpu.VMEM
SM = pltpu.SMEM


def iota(shape, dim):
    return lax.broadcasted_iota(jnp.int32, shape, dim)


def dot(a, b):
    return jnp.dot(a, b, preferred_element_type=F32)


def dot_nt(a, b):
    return lax.dot_general(a, b, (((1,), (1,)), ((), ())), preferred_element_type=F32)


def split3(x):
    high = x.astype(BF)
    rest = x - high.astype(F32)
    mid = rest.astype(BF)
    return high, mid, (rest - mid.astype(F32)).astype(BF)


def dot_exact(x, ones):
    return sum(dot(part, ones) for part in split3(x))


def moved(x):
    y = x.astype(F32)
    lane = iota(y.shape, 1)
    width = y.shape[1]
    before = jnp.where(lane == 0, 0.0, pltpu.roll(y, 1, 1))
    after = jnp.where(lane == width - 1, 0.0, pltpu.roll(y, width - 1, 1))
    return before.astype(BF), after.astype(BF)


def fill_band(kernel_ref, band_ref, ch, hh):
    rows = ch * hh
    unit = (iota((32, 27), 0) == iota((32, 27), 1)).astype(F32).astype(BF)
    by_tap = dot_nt(unit, kernel_ref[...].reshape(ch * ch, 27))
    wide = jnp.broadcast_to(by_tap[:27, None, :], (27, ch, ch * ch))
    wide = jnp.where(iota((27, ch, ch * ch), 2) // ch == iota((27, ch, ch * ch), 1), wide, 0.0)
    spread = (iota((ch * ch, rows), 1) // hh == iota((ch * ch, rows), 0) % ch).astype(F32).astype(BF)
    wide = dot(wide.reshape(27 * ch, ch * ch).astype(BF), spread).astype(BF)
    masks = [(iota((ch, rows), 1) % hh == h).astype(F32).astype(BF) for h in range(hh)]
    for i in range(3):
        for k in range(3):
            taps = [wide[(9 * i + 3 * j + k) * ch : (9 * i + 3 * j + k + 1) * ch] for j in range(3)]
            col = (3 * i + k) * rows
            for h in range(hh):
                block = masks[h] * taps[1]
                if h > 0:
                    block = block + masks[h - 1] * taps[0]
                if h < hh - 1:
                    block = block + masks[h + 1] * taps[2]
                band_ref[h * ch : (h + 1) * ch, col : col + rows] = block


def head_matrix(head_ref, ch, hh, classes):
    rows = ch * hh
    spread = (iota((ch, rows), 1) % ch == iota((ch, rows), 0)).astype(F32).astype(BF)
    wide = dot(head_ref[...], spread)
    wide = jnp.broadcast_to(wide[:, None, :], (classes, hh, rows))
    keep = iota((classes, hh, rows), 2) // ch == iota((classes, hh, rows), 1)
    return jnp.where(keep, wide, 0.0).reshape(classes * hh, rows).astype(BF)


def head_matrix_t(head_ref, ch, hh, classes):
    mat = head_matrix(head_ref, ch, hh, classes)
    rows = ch * hh
    unit = (iota((rows, rows), 0) == iota((rows, rows), 1)).astype(F32).astype(BF)
    return dot_nt(unit, mat).astype(BF)


def bias_rows(bias_ref, ch, width):
    square = jnp.broadcast_to(bias_ref[...], (ch, ch))
    column = jnp.sum(jnp.where(iota((ch, ch), 0) == iota((ch, ch), 1), square, 0.0), axis=1, keepdims=True)
    return jnp.broadcast_to(column, (ch, width))


def shifts(x):
    before, after = moved(x)
    return jnp.concatenate([before, x, after], axis=0)


def head_pair(preact, bias, mat, head_bias_ref, label, mask, dims):
    ch, hh, ww, classes = dims
    rows = ch * hh
    preact = (preact.reshape(hh, ch, 2 * ww) + bias[None]).reshape(rows, 2 * ww)
    hidden = jnp.maximum(preact, 0.0).astype(BF)
    logits = dot(mat, hidden).reshape(classes, hh, 2 * ww)
    parts = [logits[c] + head_bias_ref[0:1, c : c + 1] for c in range(classes)]
    total = functools.reduce(jnp.add, [jnp.exp(p) for p in parts])
    log_total = jnp.log(total)
    soft = [jnp.exp(p - log_total) for p in parts]
    hot = [label == c for c in range(classes)]
    chosen = functools.reduce(jnp.add, [jnp.where(o, s, 0.0) for o, s in zip(hot, soft)])
    diffs = [s - jnp.where(o, 1.0, 0.0) for o, s in zip(hot, soft)]
    return hidden, jnp.stack(diffs).reshape(classes * hh, 2 * ww), mask * chosen


def put_pair(ref, first, second, value, ww):
    ref[first] = value[:, :ww]
    ref[second] = value[:, ww:]


def beside(ref, first, second):
    return jnp.concatenate([ref[first], ref[second]], axis=1)


def load_kernel(*refs):
    count = (len(refs) - 3) // 2
    sources, targets, (a_ref, b_ref, sems) = refs[:count], refs[count : 2 * count], refs[2 * count :]
    planes = sources[0].shape[1]
    copies = [pltpu.make_async_copy(s, t, sems.at[n]) for n, (s, t) in enumerate(zip(sources, targets))]
    for copy in copies:
        copy.start()
    copies[0].wait()
    odd = lax.rem(lax.axis_index("depth"), 2)
    a_ref[...] = targets[0][:, (1 - odd) * (planes - 1)]
    b_ref[...] = targets[0][:, odd * (planes - 1)]
    for copy in copies[1:]:
        copy.wait()


def sorted_halo(a, b):
    place, size = lax.axis_index("depth"), lax.axis_size("depth")
    odd = lax.rem(place, 2) == 1
    before, after = jnp.where(odd, a, b), jnp.where(odd, b, a)
    before = jnp.where(place > 0, before, 0.0)
    after = jnp.where(place < size - 1, after, 0.0)
    return before.astype(BF), after.astype(BF)


def interior_kernel(
    x_ref, label_ref, mask_ref, kernel_ref, bias_ref, head_ref, head_bias_ref,
    band_ref, shifted_ref, hidden_ref, diff_ref, offered_ref,
):
    ch, planes, hh, ww = x_ref.shape
    classes = head_ref.shape[0]
    rows = ch * hh
    fill_band(kernel_ref, band_ref, ch, hh)
    mat = head_matrix(head_ref, ch, hh, classes)
    bias = bias_rows(bias_ref, ch, 2 * ww)
    for d in range(planes):
        shifted_ref[d] = shifts(x_ref[:, d].reshape(rows, ww))
    for d in range(1, planes - 1, 2):
        left = shifted_ref[d - 1 : d + 2].reshape(9 * rows, ww)
        right = shifted_ref[d : d + 3].reshape(9 * rows, ww)
        preact = dot(band_ref[...], jnp.concatenate([left, right], axis=1))
        hidden, diff, offered = head_pair(
            preact, bias, mat, head_bias_ref, beside(label_ref, d, d + 1),
            beside(mask_ref, d, d + 1).astype(F32), (ch, hh, ww, classes),
        )
        put_pair(hidden_ref, d - 1, d, hidden, ww)
        put_pair(diff_ref, d - 1, d, diff, ww)
        put_pair(offered_ref, d - 1, d, offered, ww)


def edge_kernel(
    a_ref, b_ref, label_ref, mask_ref, bias_ref, head_ref, head_bias_ref, band_ref, shifted_ref, inner_ref,
    halo_ref, hidden_ref, diff_ref, offered_ref,
):
    ch, hh, ww = a_ref.shape
    planes, classes = label_ref.shape[0], head_ref.shape[0]
    rows = ch * hh
    mat = head_matrix(head_ref, ch, hh, classes)
    bias = bias_rows(bias_ref, ch, 2 * ww)
    offered_ref[1 : planes - 1] = inner_ref[...]
    before, after = sorted_halo(a_ref[...].reshape(rows, ww).astype(F32), b_ref[...].reshape(rows, ww).astype(F32))
    halo_ref[0], halo_ref[1] = before, after
    left = jnp.concatenate([shifts(before), shifted_ref[0:2].reshape(6 * rows, ww)], axis=0)
    right = jnp.concatenate([shifted_ref[planes - 2 : planes].reshape(6 * rows, ww), shifts(after)], axis=0)
    preact = dot(band_ref[...], jnp.concatenate([left, right], axis=1))
    hidden, diff, offered = head_pair(
        preact, bias, mat, head_bias_ref, beside(label_ref, 0, planes - 1),
        beside(mask_ref, 0, planes - 1).astype(F32), (ch, hh, ww, classes),
    )
    put_pair(hidden_ref, 0, 1, hidden, ww)
    put_pair(diff_ref, 0, 1, diff, ww)
    put_pair(offered_ref, 0, planes - 1, offered, ww)


def backward_kernel(
    x_ref, halo_ref, weight_ref, hidden_in_ref, hidden_edge_ref, diff_in_ref, diff_edge_ref, head_ref,
    packed_ref, a_ref, b_ref, shifted_ref, rows_ref,
):
    ch, planes, hh, ww = x_ref.shape
    classes = head_ref.shape[0]
    rows = ch * hh
    mat_t = head_matrix_t(head_ref, ch, hh, classes)
    bias_sum = jnp.zeros((rows, ww), F32)
    offset_sum = jnp.zeros((classes * hh, ww), F32)
    hiddens, halves, values = [], [], []
    for d in range(planes):
        if d == 0 or d == planes - 1:
            hiddens.append(hidden_edge_ref[min(d, 1)])
            diff = diff_edge_ref[min(d, 1)]
        else:
            hiddens.append(hidden_in_ref[d - 1])
            diff = diff_in_ref[d - 1]
        grad = (diff.reshape(classes, hh, ww) * weight_ref[d][None]).reshape(classes * hh, ww)
        offset_sum = offset_sum + grad
        halves.append(grad.astype(BF))
    for d in range(0, planes, 2):
        pre = dot(mat_t, jnp.concatenate(halves[d : d + 2], axis=1))
        for p in range(2):
            value = jnp.where(hiddens[d + p].astype(F32) > 0.0, pre[:, p * ww : (p + 1) * ww], 0.0)
            bias_sum = bias_sum + value
            value = value.astype(BF)
            values.append(value)
            before, after = moved(value)
            shifted_ref[d + p] = jnp.concatenate([after, value, before], axis=0)
    odd = lax.rem(lax.axis_index("depth"), 2) == 1
    first, last = values[0].astype(F32), values[-1].astype(F32)
    a_ref[...] = jnp.where(odd, first, last).astype(BF)
    b_ref[...] = jnp.where(odd, last, first).astype(BF)
    grad_cat = jnp.concatenate([shifted_ref[d] for d in range(planes)], axis=1)
    field = [halo_ref[0]] + [x_ref[:, d].reshape(rows, ww) for d in range(planes)] + [halo_ref[1]]
    place = iota((ch, rows), 1) % hh
    for i in range(3):
        product = dot_nt(grad_cat, jnp.concatenate(field[i : i + planes], axis=1))
        for k in range(3):
            for j in range(3):
                total = jnp.zeros((ch, rows), F32)
                for h in range(hh):
                    if 0 <= h + j - 1 < hh:
                        r = k * rows + h * ch
                        total = jnp.where(place == h + j - 1, product[r : r + ch], total)
                t = 9 * i + 3 * j + k
                for half in range(rows // 128):
                    rows_ref[half, pl.ds(t, ch, stride=32)] = total[:, 128 * half : 128 * half + 128]
    for half in range(rows // 128):
        for t in range(27, 32):
            rows_ref[half, pl.ds(t, ch, stride=32)] = jnp.zeros((ch, 128), F32)
    sums = 0.0
    for half in range(rows // 128):
        pick = (iota((ch, 128), 1) + 128 * half) // hh == iota((ch, 128), 0)
        pick = pick.astype(F32).astype(BF)
        sums = sums + sum(dot_nt(pick, part) for part in split3(rows_ref[half]))
    for q in range(ch // 4):
        packed_ref[q * ch : (q + 1) * ch] = sums[:, 128 * q : 128 * q + 128]
    product = dot_nt(jnp.concatenate(halves, axis=1), jnp.concatenate(hiddens, axis=1))
    product = product.reshape(classes, hh, rows)
    keep = iota((classes, hh, rows), 2) // ch == iota((classes, hh, rows), 1)
    head = jnp.sum(jnp.where(keep, product, 0.0), axis=1)
    by_last = (iota((rows, 128), 0) % ch == iota((rows, 128), 1) % 16).astype(F32).astype(BF)
    head = dot_exact(head, by_last)
    ones = jnp.ones((16, ww), F32).astype(BF)
    bias = jnp.sum(bias_sum.reshape(hh, ch, ww), axis=0)
    bias = jnp.concatenate([bias] * 8, axis=0)
    bias = sum(dot_nt(ones, part) for part in split3(bias))[:classes]
    offset = sum(dot_nt(ones, part) for part in split3(offset_sum))
    by_class = (iota((classes * hh, 128), 0) // hh == iota((classes * hh, 128), 1) % 16).astype(F32).astype(BF)
    offset = dot_exact(offset, by_class)[:classes]
    group = iota((classes, 128), 1) // 16
    packed_ref[4 * ch : 4 * ch + classes] = jnp.where(group == 0, head, jnp.where(group == 1, bias, offset))


def inner_grad_kernel(shifted_ref, band_ref, turned_ref, out_ref):
    ch, inner, hh, ww = out_ref.shape
    rows = ch * hh
    unit = (iota((rows, rows), 0) == iota((rows, rows), 1)).astype(F32).astype(BF)
    for i in range(3):
        for k in range(3):
            block = band_ref[:, (3 * i + k) * rows : (3 * i + k + 1) * rows]
            col = (3 * (2 - i) + k) * rows
            turned_ref[:, col : col + rows] = dot_nt(unit, block).astype(BF)
    for d in range(0, inner, 2):
        left = shifted_ref[d : d + 3].reshape(9 * rows, ww)
        right = shifted_ref[d + 1 : d + 4].reshape(9 * rows, ww)
        grad = dot(turned_ref[...], jnp.concatenate([left, right], axis=1)).astype(BF)
        out_ref[:, d] = grad[:, :ww].reshape(ch, hh, ww)
        out_ref[:, d + 1] = grad[:, ww:].reshape(ch, hh, ww)


def edge_grad_kernel(a_ref, b_ref, shifted_ref, turned_ref, inner_ref, out_ref):
    ch, planes, hh, ww = out_ref.shape
    rows = ch * hh

    def turned_shifts(x):
        before, after = moved(x)
        return jnp.concatenate([after, x, before], axis=0)

    before, after = sorted_halo(a_ref[...].astype(F32), b_ref[...].astype(F32))
    left = jnp.concatenate([turned_shifts(before), shifted_ref[0:2].reshape(6 * rows, ww)], axis=0)
    right = jnp.concatenate([shifted_ref[planes - 2 : planes].reshape(6 * rows, ww), turned_shifts(after)], axis=0)
    grad = dot(turned_ref[...], jnp.concatenate([left, right], axis=1)).astype(BF)
    out_ref[:, 0] = grad[:, :ww].reshape(ch, hh, ww)
    out_ref[:, 1 : planes - 1] = inner_ref[...]
    out_ref[:, planes - 1] = grad[:, ww:].reshape(ch, hh, ww)


def unpack_kernel(scale, a_ref, b_ref, kernel_ref, bias_ref, head_ref, offset_ref):
    ch = kernel_ref.shape[0]
    for q in range(ch // 4):
        value = (a_ref[q * ch : (q + 1) * ch] + b_ref[q * ch : (q + 1) * ch]) * scale
        for r in range(4):
            turned = pltpu.roll(value, 128 - 32 * r, 1) if r else value
            kernel_ref[4 * q + r] = turned[:, 0:27]
    value = (a_ref[4 * ch :] + b_ref[4 * ch :]) * scale
    head_ref[...] = value[:, 0:16]
    bias_ref[...] = pltpu.roll(value, 112, 1)[0:1, 0:16]
    offset_ref[...] = pltpu.roll(value, 96, 1)[0:1, 0:8]


def call(kernel, out_shape, in_spaces, scratch, flops, args):
    moved_bytes = sum(a.size * a.dtype.itemsize for a in args)
    return pl.pallas_call(
        kernel,
        out_shape=out_shape,
        in_specs=[pl.BlockSpec(memory_space=s) for s in in_spaces],
        out_specs=jax.tree.map(lambda _: pl.BlockSpec(memory_space=VM), out_shape),
        scratch_shapes=scratch,
        compiler_params=pltpu.CompilerParams(vmem_limit_bytes=32 << 20),
        cost_estimate=pl.CostEstimate(flops=flops, bytes_accessed=moved_bytes, transcendentals=0),
    )(*args)


def exchange_pairs():
    crops, size = lax.axis_size("dp"), lax.axis_size("depth")
    one, two = [], []
    for c in range(crops):
        for d in range(size):
            one.append((c * size + d, c * size + (d ^ 1)))
            e = ((d + 1) ^ 1) - 1
            if 0 <= e < size:
                two.append((c * size + d, c * size + e))
            elif crops % 2 == 0:
                two.append((c * size + d, (c ^ 1) * size + d))
    return one, two


def exchanged(a, b):
    one, two = exchange_pairs()
    return lax.ppermute(a, ("dp", "depth"), one), lax.ppermute(b, ("dp", "depth"), two)


def body(features, labels, masks, conv_kernel, conv_bias, head_weight, head_bias):
    x, label, mask = features[0, 0], labels[0], masks[0, 0]
    kernel, head = conv_kernel[0], head_weight[0]
    ch, planes, hh, ww = x.shape
    classes = head.shape[0]
    rows = ch * hh
    sds = jax.ShapeDtypeStruct
    size = lax.axis_size("depth")
    pair_flops = 2 * rows * 9 * rows * 2 * ww

    plane = sds((ch, hh, ww), BF)
    inputs = (x, label, mask, kernel.transpose(1, 2, 0), conv_bias, head, head_bias)
    inputs = tuple(pltpu.with_memory_space_constraint(v, pltpu.HBM) for v in inputs)
    shapes = tuple(sds(v.shape, v.dtype) for v in inputs)
    *inputs, end_a, end_b = call(
        load_kernel,
        (*shapes, plane, plane),
        (pltpu.HBM,) * len(inputs),
        [pltpu.SemaphoreType.DMA((len(inputs),))],
        0,
        inputs,
    )
    x, label, mask, kernel, conv_bias, head, head_bias = inputs
    far = exchanged(end_a, end_b)
    band, shifted, hidden_in, diff_in, inner = call(
        interior_kernel,
        (
            sds((rows, 9 * rows), BF),
            sds((planes, 3 * rows, ww), BF),
            sds((planes - 2, rows, ww), BF),
            sds((planes - 2, classes * hh, ww), F32),
            sds((planes - 2, hh, ww), F32),
        ),
        (VM,) * 7,
        [],
        pair_flops * (planes // 2 - 1),
        (x, label, mask, kernel, conv_bias, head, head_bias),
    )
    halo, hidden_edge, diff_edge, offered = call(
        edge_kernel,
        (
            sds((2, rows, ww), BF),
            sds((2, rows, ww), BF),
            sds((2, classes * hh, ww), F32),
            sds((planes, hh, ww), F32),
        ),
        (VM,) * 10,
        [],
        pair_flops,
        (*far, label, mask, conv_bias, head, head_bias, band, shifted, inner),
    )
    weight = lax.ppermute(offered, "net", [(0, 1), (1, 0)])
    edge = sds((rows, ww), BF)
    packed, grad_a, grad_b, grads = call(
        backward_kernel,
        (sds((4 * ch + 8, 128), F32), edge, edge, sds((planes, 3 * rows, ww), BF)),
        (VM,) * 8,
        [VM((rows // 128, 32 * ch, 128), F32)],
        2 * 9 * rows * rows * planes * ww,
        (x, halo, weight, hidden_in, hidden_edge, diff_in, diff_edge, head),
    )
    turned, grad_inner = call(
        inner_grad_kernel,
        (sds((rows, 9 * rows), BF), sds((ch, planes - 2, hh, ww), BF)),
        (VM, VM),
        [],
        pair_flops * (planes // 2 - 1),
        (grads, band),
    )
    rounds = [("dp", 1 << b) for b in range((lax.axis_size("dp") - 1).bit_length())]
    rounds += [("depth", 1 << b) for b in range((size - 1).bit_length())]
    ends, pairs, grad_far = [grad_a, grad_b], exchange_pairs(), []
    for n, (axis, bit) in enumerate(rounds):
        other = lax.ppermute(packed, axis, [(i, i ^ bit) for i in range(lax.axis_size(axis))])
        if 1 <= n <= 2:
            grad_far.append(lax.ppermute(ends[n - 1], ("dp", "depth"), pairs[n - 1]))
        if n < len(rounds) - 1:
            packed = packed + other
        if n == 0:
            packed, grad_inner, ends[0] = lax.optimization_barrier((packed, grad_inner, ends[0]))
        if n == 1:
            packed, ends[1] = lax.optimization_barrier((packed, ends[1]))
    grad_input = call(
        edge_grad_kernel,
        sds((ch, planes, hh, ww), BF),
        (VM,) * 5,
        [],
        pair_flops,
        (*grad_far, grads, turned, grad_inner),
    )
    scale = 1.0 / (lax.axis_size("dp") * size * planes * hh * ww)
    grad_kernel, grad_bias, grad_head, grad_offset = call(
        functools.partial(unpack_kernel, scale),
        (sds((ch, ch, 27), F32), sds((1, ch), F32), sds((classes, ch), F32), sds((1, classes), F32)),
        (VM, VM),
        [],
        1000,
        (packed, other),
    )
    return (
        grad_input[None, None],
        grad_kernel.transpose(2, 0, 1)[None],
        grad_bias,
        grad_head[None],
        grad_offset,
    )


def solution(mesh):
    in_specs = (
        P("net", "dp", None, "depth", None, None),
        P("dp", "depth", None, None),
        P("net", "dp", "depth", None, None),
        P("net", None, None, None),
        P("net", None),
        P("net", None, None),
        P("net", None),
    )
    out_specs = (
        P("net", "dp", None, "depth", None, None),
        P("net", None, None, None),
        P("net", None),
        P("net", None, None),
        P("net", None),
    )
    return jax.shard_map(body, mesh=mesh, in_specs=in_specs, out_specs=out_specs, check_vma=False)
```

```python
import functools

import jax
import jax.numpy as jnp
from jax import lax
from jax.experimental import pallas as pl
from jax.experimental.pallas import tpu as pltpu
from jax.sharding import PartitionSpec as P

BF = jnp.bfloat16
F32 = jnp.float32
VM = pltpu.VMEM
SM = pltpu.SMEM


def iota(shape, dim):
    return lax.broadcasted_iota(jnp.int32, shape, dim)


def dot(a, b):
    return jnp.dot(a, b, preferred_element_type=F32)


def dot_nt(a, b):
    return lax.dot_general(a, b, (((1,), (1,)), ((), ())), preferred_element_type=F32)


def split3(x):
    high = x.astype(BF)
    rest = x - high.astype(F32)
    mid = rest.astype(BF)
    return high, mid, (rest - mid.astype(F32)).astype(BF)


def dot_exact(x, ones):
    return sum(dot(part, ones) for part in split3(x))


def moved(x):
    y = x.astype(F32)
    lane = iota(y.shape, 1)
    width = y.shape[1]
    before = jnp.where(lane == 0, 0.0, pltpu.roll(y, 1, 1))
    after = jnp.where(lane == width - 1, 0.0, pltpu.roll(y, width - 1, 1))
    return before.astype(BF), after.astype(BF)


def fill_band(kernel_ref, band_ref, ch, hh):
    rows = ch * hh
    unit = (iota((32, 27), 0) == iota((32, 27), 1)).astype(F32).astype(BF)
    by_tap = dot_nt(unit, kernel_ref[...].reshape(ch * ch, 27))
    wide = jnp.broadcast_to(by_tap[:27, None, :], (27, ch, ch * ch))
    wide = jnp.where(iota((27, ch, ch * ch), 2) // ch == iota((27, ch, ch * ch), 1), wide, 0.0)
    spread = (iota((ch * ch, rows), 1) // hh == iota((ch * ch, rows), 0) % ch).astype(F32).astype(BF)
    wide = dot(wide.reshape(27 * ch, ch * ch).astype(BF), spread).astype(BF)
    masks = [(iota((ch, rows), 1) % hh == h).astype(F32).astype(BF) for h in range(hh)]
    for i in range(3):
        for k in range(3):
            taps = [wide[(9 * i + 3 * j + k) * ch : (9 * i + 3 * j + k + 1) * ch] for j in range(3)]
            col = (3 * i + k) * rows
            for h in range(hh):
                block = masks[h] * taps[1]
                if h > 0:
                    block = block + masks[h - 1] * taps[0]
                if h < hh - 1:
                    block = block + masks[h + 1] * taps[2]
                band_ref[h * ch : (h + 1) * ch, col : col + rows] = block


def head_matrix(head_ref, ch, hh, classes):
    rows = ch * hh
    spread = (iota((ch, rows), 1) % ch == iota((ch, rows), 0)).astype(F32).astype(BF)
    wide = dot(head_ref[...], spread)
    wide = jnp.broadcast_to(wide[:, None, :], (classes, hh, rows))
    keep = iota((classes, hh, rows), 2) // ch == iota((classes, hh, rows), 1)
    return jnp.where(keep, wide, 0.0).reshape(classes * hh, rows).astype(BF)


def head_matrix_t(head_ref, ch, hh, classes):
    mat = head_matrix(head_ref, ch, hh, classes)
    rows = ch * hh
    unit = (iota((rows, rows), 0) == iota((rows, rows), 1)).astype(F32).astype(BF)
    return dot_nt(unit, mat).astype(BF)


def bias_rows(bias_ref, ch, width):
    square = jnp.broadcast_to(bias_ref[...], (ch, ch))
    column = jnp.sum(jnp.where(iota((ch, ch), 0) == iota((ch, ch), 1), square, 0.0), axis=1, keepdims=True)
    return jnp.broadcast_to(column, (ch, width))


def shifts(x):
    before, after = moved(x)
    return jnp.concatenate([before, x, after], axis=0)


def head_pair(preact, bias, mat, head_bias_ref, label, mask, dims):
    ch, hh, ww, classes = dims
    rows = ch * hh
    preact = (preact.reshape(hh, ch, 2 * ww) + bias[None]).reshape(rows, 2 * ww)
    hidden = jnp.maximum(preact, 0.0).astype(BF)
    logits = dot(mat, hidden).reshape(classes, hh, 2 * ww)
    parts = [logits[c] + head_bias_ref[0:1, c : c + 1] for c in range(classes)]
    total = functools.reduce(jnp.add, [jnp.exp(p) for p in parts])
    log_total = jnp.log(total)
    soft = [jnp.exp(p - log_total) for p in parts]
    hot = [label == c for c in range(classes)]
    chosen = functools.reduce(jnp.add, [jnp.where(o, s, 0.0) for o, s in zip(hot, soft)])
    diffs = [s - jnp.where(o, 1.0, 0.0) for o, s in zip(hot, soft)]
    return hidden, jnp.stack(diffs).reshape(classes * hh, 2 * ww), mask * chosen


def put_pair(ref, first, second, value, ww):
    ref[first] = value[:, :ww]
    ref[second] = value[:, ww:]


def beside(ref, first, second):
    return jnp.concatenate([ref[first], ref[second]], axis=1)


def load_kernel(*refs):
    count = (len(refs) - 3) // 2
    sources, targets, (a_ref, b_ref, sems) = refs[:count], refs[count : 2 * count], refs[2 * count :]
    planes = sources[0].shape[1]
    copies = [pltpu.make_async_copy(s, t, sems.at[n]) for n, (s, t) in enumerate(zip(sources, targets))]
    for copy in copies:
        copy.start()
    copies[0].wait()
    odd = lax.rem(lax.axis_index("depth"), 2)
    a_ref[...] = targets[0][:, (1 - odd) * (planes - 1)]
    b_ref[...] = targets[0][:, odd * (planes - 1)]
    for copy in copies[1:]:
        copy.wait()


def sorted_halo(a, b):
    place, size = lax.axis_index("depth"), lax.axis_size("depth")
    odd = lax.rem(place, 2) == 1
    before, after = jnp.where(odd, a, b), jnp.where(odd, b, a)
    before = jnp.where(place > 0, before, 0.0)
    after = jnp.where(place < size - 1, after, 0.0)
    return before.astype(BF), after.astype(BF)


def interior_kernel(
    x_ref, label_ref, mask_ref, kernel_ref, bias_ref, head_ref, head_bias_ref,
    band_ref, shifted_ref, hidden_ref, diff_ref, offered_ref,
):
    ch, planes, hh, ww = x_ref.shape
    classes = head_ref.shape[0]
    rows = ch * hh
    fill_band(kernel_ref, band_ref, ch, hh)
    mat = head_matrix(head_ref, ch, hh, classes)
    bias = bias_rows(bias_ref, ch, 2 * ww)
    for d in range(planes):
        shifted_ref[d] = shifts(x_ref[:, d].reshape(rows, ww))
    for d in range(1, planes - 1, 2):
        left = shifted_ref[d - 1 : d + 2].reshape(9 * rows, ww)
        right = shifted_ref[d : d + 3].reshape(9 * rows, ww)
        preact = dot(band_ref[...], jnp.concatenate([left, right], axis=1))
        hidden, diff, offered = head_pair(
            preact, bias, mat, head_bias_ref, beside(label_ref, d, d + 1),
            beside(mask_ref, d, d + 1).astype(F32), (ch, hh, ww, classes),
        )
        put_pair(hidden_ref, d - 1, d, hidden, ww)
        put_pair(diff_ref, d - 1, d, diff, ww)
        put_pair(offered_ref, d - 1, d, offered, ww)


def edge_kernel(
    a_ref, b_ref, label_ref, mask_ref, bias_ref, head_ref, head_bias_ref, band_ref, shifted_ref, inner_ref,
    halo_ref, hidden_ref, diff_ref, offered_ref,
):
    ch, hh, ww = a_ref.shape
    planes, classes = label_ref.shape[0], head_ref.shape[0]
    rows = ch * hh
    mat = head_matrix(head_ref, ch, hh, classes)
    bias = bias_rows(bias_ref, ch, 2 * ww)
    offered_ref[1 : planes - 1] = inner_ref[...]
    before, after = sorted_halo(a_ref[...].reshape(rows, ww).astype(F32), b_ref[...].reshape(rows, ww).astype(F32))
    halo_ref[0], halo_ref[1] = before, after
    left = jnp.concatenate([shifts(before), shifted_ref[0:2].reshape(6 * rows, ww)], axis=0)
    right = jnp.concatenate([shifted_ref[planes - 2 : planes].reshape(6 * rows, ww), shifts(after)], axis=0)
    preact = dot(band_ref[...], jnp.concatenate([left, right], axis=1))
    hidden, diff, offered = head_pair(
        preact, bias, mat, head_bias_ref, beside(label_ref, 0, planes - 1),
        beside(mask_ref, 0, planes - 1).astype(F32), (ch, hh, ww, classes),
    )
    put_pair(hidden_ref, 0, 1, hidden, ww)
    put_pair(diff_ref, 0, 1, diff, ww)
    put_pair(offered_ref, 0, planes - 1, offered, ww)


def backward_kernel(
    x_ref, halo_ref, weight_ref, hidden_in_ref, hidden_edge_ref, diff_in_ref, diff_edge_ref, head_ref,
    packed_ref, a_ref, b_ref, shifted_ref, rows_ref,
):
    ch, planes, hh, ww = x_ref.shape
    classes = head_ref.shape[0]
    rows = ch * hh
    mat_t = head_matrix_t(head_ref, ch, hh, classes)
    bias_sum = jnp.zeros((rows, ww), F32)
    offset_sum = jnp.zeros((classes * hh, ww), F32)
    hiddens, halves, values = [], [], []
    for d in range(planes):
        if d == 0 or d == planes - 1:
            hiddens.append(hidden_edge_ref[min(d, 1)])
            diff = diff_edge_ref[min(d, 1)]
        else:
            hiddens.append(hidden_in_ref[d - 1])
            diff = diff_in_ref[d - 1]
        grad = (diff.reshape(classes, hh, ww) * weight_ref[d][None]).reshape(classes * hh, ww)
        offset_sum = offset_sum + grad
        halves.append(grad.astype(BF))
    for d in range(0, planes, 2):
        pre = dot(mat_t, jnp.concatenate(halves[d : d + 2], axis=1))
        for p in range(2):
            value = jnp.where(hiddens[d + p].astype(F32) > 0.0, pre[:, p * ww : (p + 1) * ww], 0.0)
            bias_sum = bias_sum + value
            value = value.astype(BF)
            values.append(value)
            before, after = moved(value)
            shifted_ref[d + p] = jnp.concatenate([after, value, before], axis=0)
    odd = lax.rem(lax.axis_index("depth"), 2) == 1
    first, last = values[0].astype(F32), values[-1].astype(F32)
    a_ref[...] = jnp.where(odd, first, last).astype(BF)
    b_ref[...] = jnp.where(odd, last, first).astype(BF)
    grad_cat = jnp.concatenate([shifted_ref[d] for d in range(planes)], axis=1)
    field = [halo_ref[0]] + [x_ref[:, d].reshape(rows, ww) for d in range(planes)] + [halo_ref[1]]
    place = iota((ch, rows), 1) % hh
    for i in range(3):
        product = dot_nt(grad_cat, jnp.concatenate(field[i : i + planes], axis=1))
        for k in range(3):
            for j in range(3):
                total = jnp.zeros((ch, rows), F32)
                for h in range(hh):
                    if 0 <= h + j - 1 < hh:
                        r = k * rows + h * ch
                        total = jnp.where(place == h + j - 1, product[r : r + ch], total)
                t = 9 * i + 3 * j + k
                for half in range(rows // 128):
                    rows_ref[half, pl.ds(t, ch, stride=32)] = total[:, 128 * half : 128 * half + 128]
    for half in range(rows // 128):
        for t in range(27, 32):
            rows_ref[half, pl.ds(t, ch, stride=32)] = jnp.zeros((ch, 128), F32)
    sums = 0.0
    for half in range(rows // 128):
        pick = (iota((ch, 128), 1) + 128 * half) // hh == iota((ch, 128), 0)
        pick = pick.astype(F32).astype(BF)
        sums = sums + sum(dot_nt(pick, part) for part in split3(rows_ref[half]))
    for q in range(ch // 4):
        packed_ref[q * ch : (q + 1) * ch] = sums[:, 128 * q : 128 * q + 128]
    product = dot_nt(jnp.concatenate(halves, axis=1), jnp.concatenate(hiddens, axis=1))
    product = product.reshape(classes, hh, rows)
    keep = iota((classes, hh, rows), 2) // ch == iota((classes, hh, rows), 1)
    head = jnp.sum(jnp.where(keep, product, 0.0), axis=1)
    by_last = (iota((rows, 128), 0) % ch == iota((rows, 128), 1) % 16).astype(F32).astype(BF)
    head = dot_exact(head, by_last)
    ones = jnp.ones((16, ww), F32).astype(BF)
    bias = jnp.sum(bias_sum.reshape(hh, ch, ww), axis=0)
    bias = jnp.concatenate([bias] * 8, axis=0)
    bias = sum(dot_nt(ones, part) for part in split3(bias))[:classes]
    offset = sum(dot_nt(ones, part) for part in split3(offset_sum))
    by_class = (iota((classes * hh, 128), 0) // hh == iota((classes * hh, 128), 1) % 16).astype(F32).astype(BF)
    offset = dot_exact(offset, by_class)[:classes]
    group = iota((classes, 128), 1) // 16
    packed_ref[4 * ch : 4 * ch + classes] = jnp.where(group == 0, head, jnp.where(group == 1, bias, offset))


def inner_grad_kernel(shifted_ref, band_ref, end_ref, turned_ref, out_ref, end_out_ref):
    end_out_ref[...] = end_ref[...]
    ch, inner, hh, ww = out_ref.shape
    rows = ch * hh
    unit = (iota((rows, rows), 0) == iota((rows, rows), 1)).astype(F32).astype(BF)
    for i in range(3):
        for k in range(3):
            block = band_ref[:, (3 * i + k) * rows : (3 * i + k + 1) * rows]
            col = (3 * (2 - i) + k) * rows
            turned_ref[:, col : col + rows] = dot_nt(unit, block).astype(BF)
    for d in range(0, inner, 2):
        left = shifted_ref[d : d + 3].reshape(9 * rows, ww)
        right = shifted_ref[d + 1 : d + 4].reshape(9 * rows, ww)
        grad = dot(turned_ref[...], jnp.concatenate([left, right], axis=1)).astype(BF)
        out_ref[:, d] = grad[:, :ww].reshape(ch, hh, ww)
        out_ref[:, d + 1] = grad[:, ww:].reshape(ch, hh, ww)


def edge_grad_kernel(a_ref, b_ref, shifted_ref, turned_ref, inner_ref, out_ref):
    ch, planes, hh, ww = out_ref.shape
    rows = ch * hh

    def turned_shifts(x):
        before, after = moved(x)
        return jnp.concatenate([after, x, before], axis=0)

    before, after = sorted_halo(a_ref[...].astype(F32), b_ref[...].astype(F32))
    left = jnp.concatenate([turned_shifts(before), shifted_ref[0:2].reshape(6 * rows, ww)], axis=0)
    right = jnp.concatenate([shifted_ref[planes - 2 : planes].reshape(6 * rows, ww), turned_shifts(after)], axis=0)
    grad = dot(turned_ref[...], jnp.concatenate([left, right], axis=1)).astype(BF)
    out_ref[:, 0] = grad[:, :ww].reshape(ch, hh, ww)
    out_ref[:, 1 : planes - 1] = inner_ref[...]
    out_ref[:, planes - 1] = grad[:, ww:].reshape(ch, hh, ww)


def unpack_kernel(scale, a_ref, b_ref, kernel_ref, bias_ref, head_ref, offset_ref):
    ch = kernel_ref.shape[0]
    for q in range(ch // 4):
        value = (a_ref[q * ch : (q + 1) * ch] + b_ref[q * ch : (q + 1) * ch]) * scale
        for r in range(4):
            turned = pltpu.roll(value, 128 - 32 * r, 1) if r else value
            kernel_ref[4 * q + r] = turned[:, 0:27]
    value = (a_ref[4 * ch :] + b_ref[4 * ch :]) * scale
    head_ref[...] = value[:, 0:16]
    bias_ref[...] = pltpu.roll(value, 112, 1)[0:1, 0:16]
    offset_ref[...] = pltpu.roll(value, 96, 1)[0:1, 0:8]


def call(kernel, out_shape, in_spaces, scratch, flops, args):
    moved_bytes = sum(a.size * a.dtype.itemsize for a in args)
    return pl.pallas_call(
        kernel,
        out_shape=out_shape,
        in_specs=[pl.BlockSpec(memory_space=s) for s in in_spaces],
        out_specs=jax.tree.map(lambda _: pl.BlockSpec(memory_space=VM), out_shape),
        scratch_shapes=scratch,
        compiler_params=pltpu.CompilerParams(vmem_limit_bytes=32 << 20),
        cost_estimate=pl.CostEstimate(flops=flops, bytes_accessed=moved_bytes, transcendentals=0),
    )(*args)


def exchange_pairs():
    crops, size = lax.axis_size("dp"), lax.axis_size("depth")
    one, two = [], []
    for c in range(crops):
        for d in range(size):
            one.append((c * size + d, c * size + (d ^ 1)))
            e = ((d + 1) ^ 1) - 1
            if 0 <= e < size:
                two.append((c * size + d, c * size + e))
            elif crops % 2 == 0:
                two.append((c * size + d, (c ^ 1) * size + d))
    return one, two


def exchanged(a, b):
    one, two = exchange_pairs()
    return lax.ppermute(a, ("dp", "depth"), one), lax.ppermute(b, ("dp", "depth"), two)


def body(features, labels, masks, conv_kernel, conv_bias, head_weight, head_bias):
    x, label, mask = features[0, 0], labels[0], masks[0, 0]
    kernel, head = conv_kernel[0], head_weight[0]
    ch, planes, hh, ww = x.shape
    classes = head.shape[0]
    rows = ch * hh
    sds = jax.ShapeDtypeStruct
    size = lax.axis_size("depth")
    pair_flops = 2 * rows * 9 * rows * 2 * ww

    plane = sds((ch, hh, ww), BF)
    inputs = (x, label, mask, kernel.transpose(1, 2, 0), conv_bias, head, head_bias)
    inputs = tuple(pltpu.with_memory_space_constraint(v, pltpu.HBM) for v in inputs)
    shapes = tuple(sds(v.shape, v.dtype) for v in inputs)
    *inputs, end_a, end_b = call(
        load_kernel,
        (*shapes, plane, plane),
        (pltpu.HBM,) * len(inputs),
        [pltpu.SemaphoreType.DMA((len(inputs),))],
        0,
        inputs,
    )
    x, label, mask, kernel, conv_bias, head, head_bias = inputs
    far = exchanged(end_a, end_b)
    band, shifted, hidden_in, diff_in, inner = call(
        interior_kernel,
        (
            sds((rows, 9 * rows), BF),
            sds((planes, 3 * rows, ww), BF),
            sds((planes - 2, rows, ww), BF),
            sds((planes - 2, classes * hh, ww), F32),
            sds((planes - 2, hh, ww), F32),
        ),
        (VM,) * 7,
        [],
        pair_flops * (planes // 2 - 1),
        (x, label, mask, kernel, conv_bias, head, head_bias),
    )
    halo, hidden_edge, diff_edge, offered = call(
        edge_kernel,
        (
            sds((2, rows, ww), BF),
            sds((2, rows, ww), BF),
            sds((2, classes * hh, ww), F32),
            sds((planes, hh, ww), F32),
        ),
        (VM,) * 10,
        [],
        pair_flops,
        (*far, label, mask, conv_bias, head, head_bias, band, shifted, inner),
    )
    weight = lax.ppermute(offered, "net", [(0, 1), (1, 0)])
    edge = sds((rows, ww), BF)
    packed, grad_a, grad_b, grads = call(
        backward_kernel,
        (sds((4 * ch + 8, 128), F32), edge, edge, sds((planes, 3 * rows, ww), BF)),
        (VM,) * 8,
        [VM((rows // 128, 32 * ch, 128), F32)],
        2 * 9 * rows * rows * planes * ww,
        (x, halo, weight, hidden_in, hidden_edge, diff_in, diff_edge, head),
    )
    turned, grad_inner, grad_a = call(
        inner_grad_kernel,
        (sds((rows, 9 * rows), BF), sds((ch, planes - 2, hh, ww), BF), edge),
        (VM, VM, VM),
        [],
        pair_flops * (planes // 2 - 1),
        (grads, band, grad_a),
    )
    rounds = [("dp", 1 << b) for b in range((lax.axis_size("dp") - 1).bit_length())]
    rounds += [("depth", 1 << b) for b in range((size - 1).bit_length())]
    ends, pairs, grad_far = [grad_a, grad_b], exchange_pairs(), []
    for n, (axis, bit) in enumerate(rounds):
        other = lax.ppermute(packed, axis, [(i, i ^ bit) for i in range(lax.axis_size(axis))])
        if n <= 1:
            grad_far.append(lax.ppermute(ends[n], ("dp", "depth"), pairs[n]))
        if n < len(rounds) - 1:
            packed = packed + other
        if n == 0:
            packed, grad_inner, ends[1] = lax.optimization_barrier((packed, grad_inner, ends[1]))
    grad_input = call(
        edge_grad_kernel,
        sds((ch, planes, hh, ww), BF),
        (VM,) * 5,
        [],
        pair_flops,
        (*grad_far, grads, turned, grad_inner),
    )
    scale = 1.0 / (lax.axis_size("dp") * size * planes * hh * ww)
    grad_kernel, grad_bias, grad_head, grad_offset = call(
        functools.partial(unpack_kernel, scale),
        (sds((ch, ch, 27), F32), sds((1, ch), F32), sds((classes, ch), F32), sds((1, classes), F32)),
        (VM, VM),
        [],
        1000,
        (packed, other),
    )
    return (
        grad_input[None, None],
        grad_kernel.transpose(2, 0, 1)[None],
        grad_bias,
        grad_head[None],
        grad_offset,
    )


def solution(mesh):
    in_specs = (
        P("net", "dp", None, "depth", None, None),
        P("dp", "depth", None, None),
        P("net", "dp", "depth", None, None),
        P("net", None, None, None),
        P("net", None),
        P("net", None, None),
        P("net", None),
    )
    out_specs = (
        P("net", "dp", None, "depth", None, None),
        P("net", None, None, None),
        P("net", None),
        P("net", None, None),
        P("net", None),
    )
    return jax.shard_map(body, mesh=mesh, in_specs=in_specs, out_specs=out_specs, check_vma=False)
```

```python
import functools

import jax
import jax.numpy as jnp
from jax import lax
from jax.experimental import pallas as pl
from jax.experimental.pallas import tpu as pltpu
from jax.sharding import PartitionSpec as P

BF = jnp.bfloat16
F32 = jnp.float32
VM = pltpu.VMEM
SM = pltpu.SMEM


def iota(shape, dim):
    return lax.broadcasted_iota(jnp.int32, shape, dim)


def dot(a, b):
    return jnp.dot(a, b, preferred_element_type=F32)


def dot_nt(a, b):
    return lax.dot_general(a, b, (((1,), (1,)), ((), ())), preferred_element_type=F32)


def split3(x):
    high = x.astype(BF)
    rest = x - high.astype(F32)
    mid = rest.astype(BF)
    return high, mid, (rest - mid.astype(F32)).astype(BF)


def dot_exact(x, ones):
    return sum(dot(part, ones) for part in split3(x))


def moved(x):
    y = x.astype(F32)
    lane = iota(y.shape, 1)
    width = y.shape[1]
    before = jnp.where(lane == 0, 0.0, pltpu.roll(y, 1, 1))
    after = jnp.where(lane == width - 1, 0.0, pltpu.roll(y, width - 1, 1))
    return before.astype(BF), after.astype(BF)


def fill_band(kernel_ref, band_ref, ch, hh):
    rows = ch * hh
    unit = (iota((32, 27), 0) == iota((32, 27), 1)).astype(F32).astype(BF)
    by_tap = dot_nt(unit, kernel_ref[...].reshape(ch * ch, 27))
    wide = jnp.broadcast_to(by_tap[:27, None, :], (27, ch, ch * ch))
    wide = jnp.where(iota((27, ch, ch * ch), 2) // ch == iota((27, ch, ch * ch), 1), wide, 0.0)
    spread = (iota((ch * ch, rows), 1) // hh == iota((ch * ch, rows), 0) % ch).astype(F32).astype(BF)
    wide = dot(wide.reshape(27 * ch, ch * ch).astype(BF), spread).astype(BF)
    masks = [(iota((ch, rows), 1) % hh == h).astype(F32).astype(BF) for h in range(hh)]
    for i in range(3):
        for k in range(3):
            taps = [wide[(9 * i + 3 * j + k) * ch : (9 * i + 3 * j + k + 1) * ch] for j in range(3)]
            col = (3 * i + k) * rows
            for h in range(hh):
                block = masks[h] * taps[1]
                if h > 0:
                    block = block + masks[h - 1] * taps[0]
                if h < hh - 1:
                    block = block + masks[h + 1] * taps[2]
                band_ref[h * ch : (h + 1) * ch, col : col + rows] = block


def head_matrix(head_ref, ch, hh, classes):
    rows = ch * hh
    spread = (iota((ch, rows), 1) % ch == iota((ch, rows), 0)).astype(F32).astype(BF)
    wide = dot(head_ref[...], spread)
    wide = jnp.broadcast_to(wide[:, None, :], (classes, hh, rows))
    keep = iota((classes, hh, rows), 2) // ch == iota((classes, hh, rows), 1)
    return jnp.where(keep, wide, 0.0).reshape(classes * hh, rows).astype(BF)


def head_matrix_t(head_ref, ch, hh, classes):
    mat = head_matrix(head_ref, ch, hh, classes)
    rows = ch * hh
    unit = (iota((rows, rows), 0) == iota((rows, rows), 1)).astype(F32).astype(BF)
    return dot_nt(unit, mat).astype(BF)


def bias_rows(bias_ref, ch, width):
    square = jnp.broadcast_to(bias_ref[...], (ch, ch))
    column = jnp.sum(jnp.where(iota((ch, ch), 0) == iota((ch, ch), 1), square, 0.0), axis=1, keepdims=True)
    return jnp.broadcast_to(column, (ch, width))


def shifts(x):
    before, after = moved(x)
    return jnp.concatenate([before, x, after], axis=0)


def head_pair(preact, bias, mat, head_bias_ref, label, mask, dims):
    ch, hh, ww, classes = dims
    rows = ch * hh
    preact = (preact.reshape(hh, ch, 2 * ww) + bias[None]).reshape(rows, 2 * ww)
    hidden = jnp.maximum(preact, 0.0).astype(BF)
    logits = dot(mat, hidden).reshape(classes, hh, 2 * ww)
    parts = [logits[c] + head_bias_ref[0:1, c : c + 1] for c in range(classes)]
    total = functools.reduce(jnp.add, [jnp.exp(p) for p in parts])
    log_total = jnp.log(total)
    soft = [jnp.exp(p - log_total) for p in parts]
    hot = [label == c for c in range(classes)]
    chosen = functools.reduce(jnp.add, [jnp.where(o, s, 0.0) for o, s in zip(hot, soft)])
    diffs = [s - jnp.where(o, 1.0, 0.0) for o, s in zip(hot, soft)]
    return hidden, jnp.stack(diffs).reshape(classes * hh, 2 * ww), mask * chosen


def put_pair(ref, first, second, value, ww):
    ref[first] = value[:, :ww]
    ref[second] = value[:, ww:]


def beside(ref, first, second):
    return jnp.concatenate([ref[first], ref[second]], axis=1)


def load_kernel(*refs):
    count = (len(refs) - 3) // 2
    sources, targets, (a_ref, b_ref, sems) = refs[:count], refs[count : 2 * count], refs[2 * count :]
    planes = sources[0].shape[1]
    copies = [pltpu.make_async_copy(s, t, sems.at[n]) for n, (s, t) in enumerate(zip(sources, targets))]
    for copy in copies:
        copy.start()
    copies[0].wait()
    odd = lax.rem(lax.axis_index("depth"), 2)
    a_ref[...] = targets[0][:, (1 - odd) * (planes - 1)]
    b_ref[...] = targets[0][:, odd * (planes - 1)]
    for copy in copies[1:]:
        copy.wait()


def sorted_halo(a, b):
    place, size = lax.axis_index("depth"), lax.axis_size("depth")
    odd = lax.rem(place, 2) == 1
    before, after = jnp.where(odd, a, b), jnp.where(odd, b, a)
    before = jnp.where(place > 0, before, 0.0)
    after = jnp.where(place < size - 1, after, 0.0)
    return before.astype(BF), after.astype(BF)


def turner(ch, hh):
    rows = ch * hh
    row, col = iota((rows, rows), 0), iota((rows, rows), 1)
    return ((row // ch == col % hh) & (row % ch == col // hh)).astype(F32).astype(BF)


def interior_kernel(
    x_ref, label_ref, mask_ref, kernel_ref, bias_ref, head_ref, head_bias_ref,
    band_ref, shifted_ref, turned_ref, hidden_ref, diff_ref, offered_ref,
):
    ch, planes, hh, ww = x_ref.shape
    classes = head_ref.shape[0]
    rows = ch * hh
    inner = planes - 2
    fill_band(kernel_ref, band_ref, ch, hh)
    mat = head_matrix(head_ref, ch, hh, classes)
    bias = bias_rows(bias_ref, ch, 2 * ww)
    field = [x_ref[:, d].reshape(rows, ww) for d in range(planes)]
    for d in range(planes):
        shifted_ref[d] = shifts(field[d])
    wide = [shifted_ref[d : d + 3].reshape(9 * rows, ww) for d in range(inner)]
    preact = dot(band_ref[...], jnp.concatenate(wide, axis=1))
    for d in range(0, inner, 2):
        hidden, diff, offered = head_pair(
            preact[:, d * ww : (d + 2) * ww], bias, mat, head_bias_ref, beside(label_ref, d + 1, d + 2),
            beside(mask_ref, d + 1, d + 2).astype(F32), (ch, hh, ww, classes),
        )
        put_pair(hidden_ref, d, d + 1, hidden, ww)
        put_pair(diff_ref, d, d + 1, diff, ww)
        put_pair(offered_ref, d, d + 1, offered, ww)
    turned = dot(turner(ch, hh), jnp.concatenate(field, axis=1)).astype(BF)
    for d in range(planes):
        turned_ref[d] = turned[:, d * ww : (d + 1) * ww]


def edge_kernel(
    a_ref, b_ref, label_ref, mask_ref, bias_ref, head_ref, head_bias_ref, band_ref, shifted_ref,
    halo_ref, hidden_ref, diff_ref, offered_ref,
):
    ch, hh, ww = a_ref.shape
    planes, classes = label_ref.shape[0], head_ref.shape[0]
    rows = ch * hh
    mat = head_matrix(head_ref, ch, hh, classes)
    bias = bias_rows(bias_ref, ch, 2 * ww)
    before, after = sorted_halo(a_ref[...].reshape(rows, ww).astype(F32), b_ref[...].reshape(rows, ww).astype(F32))
    left = jnp.concatenate([shifts(before), shifted_ref[0:2].reshape(6 * rows, ww)], axis=0)
    right = jnp.concatenate([shifted_ref[planes - 2 : planes].reshape(6 * rows, ww), shifts(after)], axis=0)
    preact = dot(band_ref[...], jnp.concatenate([left, right], axis=1))
    hidden, diff, offered = head_pair(
        preact, bias, mat, head_bias_ref, beside(label_ref, 0, planes - 1),
        beside(mask_ref, 0, planes - 1).astype(F32), (ch, hh, ww, classes),
    )
    put_pair(hidden_ref, 0, 1, hidden, ww)
    put_pair(diff_ref, 0, 1, diff, ww)
    put_pair(offered_ref, 0, 1, offered, ww)
    turned = dot(turner(ch, hh), jnp.concatenate([before, after], axis=1)).astype(BF)
    put_pair(halo_ref, 0, 1, turned, ww)


def backward_planes(diff_ref, weight_ref, hidden_ref, head_ref, shifted_ref):
    count, rows, ww = hidden_ref.shape
    classes, ch = head_ref.shape
    hh = rows // ch
    mat_t = head_matrix_t(head_ref, ch, hh, classes)
    offset_sum, halves = 0.0, []
    for d in range(count):
        grad = (diff_ref[d].reshape(classes, hh, ww) * weight_ref[d][None]).reshape(classes * hh, ww)
        offset_sum = offset_sum + grad
        halves.append(grad.astype(BF))
    halves = jnp.concatenate(halves, axis=1)
    hiddens = jnp.concatenate([hidden_ref[d] for d in range(count)], axis=1)
    pre = jnp.where(hiddens.astype(F32) > 0.0, dot(mat_t, halves), 0.0)
    bias_sum = sum(pre[:, d * ww : (d + 1) * ww] for d in range(count))
    values = [pre[:, d * ww : (d + 1) * ww].astype(BF) for d in range(count)]
    for d in range(count):
        before, after = moved(values[d])
        shifted_ref[d] = jnp.concatenate([after, values[d], before], axis=0)
    return values, bias_sum, offset_sum, dot_nt(halves, hiddens)


STEP = 3


def weight_products(shifted_ref, fields, ch, hh, totals):
    count, rows3, ww = shifted_ref.shape
    rows = rows3 // 3
    span = STEP + 2
    spot = iota((ch, 256), 1) // ch % span
    grads = [shifted_ref[d] for d in range(count)]
    for h0 in range(0, hh, STEP):
        step = min(STEP, hh - h0)
        left = [g[k * rows + h0 * ch : k * rows + (h0 + step) * ch] for k in range(3) for g in grads]
        left = [jnp.concatenate(left[k * count : (k + 1) * count], axis=1) for k in range(3)]
        low, high = max(h0 - 1, 0), min(h0 + span - 1, hh)
        right = []
        for i in range(3):
            if h0 == 0:
                right.append(jnp.zeros((ch, count * ww), BF))
            right.append(jnp.concatenate([f[low * ch : high * ch] for f in fields[i]], axis=1))
            if h0 + span - 1 > hh:
                right.append(jnp.zeros(((h0 + span - 1 - hh) * ch, count * ww), BF))
        right.append(jnp.zeros((256 - 3 * span * ch, count * ww), BF))
        product = dot_nt(jnp.concatenate(left, axis=0), jnp.concatenate(right, axis=0))
        for k in range(3):
            for j in range(3):
                total = jnp.zeros((ch, 256), F32)
                for h in range(step):
                    r = (k * step + h) * ch
                    total = jnp.where(spot == h + j, product[r : r + ch], total)
                totals[3 * k + j] = totals[3 * k + j] + total
    return totals


def inner_backward_kernel(
    turned_ref, weight_ref, hidden_ref, diff_ref, head_ref, after_ref,
    shifted_ref, total_ref, bias_ref, offset_ref, product_ref,
):
    del after_ref
    classes, ch = head_ref.shape
    inner, rows, ww = hidden_ref.shape
    _, bias_ref[...], offset_ref[...], product_ref[...] = backward_planes(
        diff_ref, weight_ref, hidden_ref, head_ref, shifted_ref
    )
    fields = [[turned_ref[d + i] for d in range(inner)] for i in range(3)]
    totals = weight_products(shifted_ref, fields, ch, rows // ch, [0.0] * 9)
    for n in range(9):
        total_ref[n] = totals[n]


def edge_backward_kernel(
    turned_ref, halo_ref, weight_ref, hidden_ref, diff_ref, head_ref, total_ref, bias_in_ref, offset_in_ref, product_in_ref,
    packed_ref, a_ref, b_ref, shifted_ref, rows_ref,
):
    classes, ch = head_ref.shape
    planes, rows, ww = turned_ref.shape
    hh = rows // ch
    values, bias_sum, offset_sum, product = backward_planes(diff_ref, weight_ref, hidden_ref, head_ref, shifted_ref)
    bias_sum, offset_sum = bias_sum + bias_in_ref[...], offset_sum + offset_in_ref[...]
    product = product + product_in_ref[...]
    odd = lax.rem(lax.axis_index("depth"), 2) == 1
    first, last = values[0].astype(F32), values[1].astype(F32)
    a_ref[...] = jnp.where(odd, first, last).astype(BF)
    b_ref[...] = jnp.where(odd, last, first).astype(BF)
    fields = [
        [halo_ref[0], turned_ref[planes - 2]],
        [turned_ref[0], turned_ref[planes - 1]],
        [turned_ref[1], halo_ref[1]],
    ]
    totals = weight_products(shifted_ref, fields, ch, hh, [total_ref[n] for n in range(9)])
    part = iota((ch, 256), 1) // (ch * (STEP + 2))
    for half in range(2):
        for t in range(32):
            i, j, k = t // 9, t // 3 % 3, t % 3
            value = jnp.where(part == i, totals[3 * k + j], 0.0) if t < 27 else jnp.zeros((ch, 256), F32)
            rows_ref[half, pl.ds(t, ch, stride=32)] = value[:, 128 * half : 128 * half + 128]
    pick = (iota((ch, 128), 1) % ch == iota((ch, 128), 0)).astype(F32).astype(BF)
    sums = sum(dot_nt(pick, part) for half in range(2) for part in split3(rows_ref[half]))
    for q in range(ch // 4):
        packed_ref[q * ch : (q + 1) * ch] = sums[:, 128 * q : 128 * q + 128]
    product = product.reshape(classes, hh, rows)
    keep = iota((classes, hh, rows), 2) // ch == iota((classes, hh, rows), 1)
    head = jnp.sum(jnp.where(keep, product, 0.0), axis=1)
    by_last = (iota((rows, 128), 0) % ch == iota((rows, 128), 1) % 16).astype(F32).astype(BF)
    head = dot_exact(head, by_last)
    ones = jnp.ones((16, ww), F32).astype(BF)
    bias = jnp.sum(bias_sum.reshape(hh, ch, ww), axis=0)
    bias = jnp.concatenate([bias] * 8, axis=0)
    bias = sum(dot_nt(ones, part) for part in split3(bias))[:classes]
    offset = sum(dot_nt(ones, part) for part in split3(offset_sum))
    by_class = (iota((classes * hh, 128), 0) // hh == iota((classes * hh, 128), 1) % 16).astype(F32).astype(BF)
    offset = dot_exact(offset, by_class)[:classes]
    group = iota((classes, 128), 1) // 16
    packed_ref[4 * ch : 4 * ch + classes] = jnp.where(group == 0, head, jnp.where(group == 1, bias, offset))


def inner_grad_kernel(shifted_ref, edge_ref, band_ref, end_ref, turned_ref, out_ref, end_out_ref):
    end_out_ref[...] = end_ref[...]
    ch, inner, hh, ww = out_ref.shape
    rows = ch * hh
    unit = (iota((rows, rows), 0) == iota((rows, rows), 1)).astype(F32).astype(BF)
    for i in range(3):
        for k in range(3):
            block = band_ref[:, (3 * i + k) * rows : (3 * i + k + 1) * rows]
            col = (3 * (2 - i) + k) * rows
            turned_ref[:, col : col + rows] = dot_nt(unit, block).astype(BF)
    planes = [edge_ref[0]] + [shifted_ref[d] for d in range(inner)] + [edge_ref[1]]
    wide = [jnp.concatenate(planes[d : d + 3], axis=0) for d in range(inner)]
    grad = dot(turned_ref[...], jnp.concatenate(wide, axis=1)).astype(BF)
    for d in range(inner):
        out_ref[:, d] = grad[:, d * ww : (d + 1) * ww].reshape(ch, hh, ww)


def edge_grad_kernel(a_ref, b_ref, shifted_ref, edge_ref, turned_ref, inner_ref, out_ref):
    ch, planes, hh, ww = out_ref.shape
    rows = ch * hh

    def turned_shifts(x):
        before, after = moved(x)
        return jnp.concatenate([after, x, before], axis=0)

    before, after = sorted_halo(a_ref[...].astype(F32), b_ref[...].astype(F32))
    left = jnp.concatenate([turned_shifts(before), edge_ref[0], shifted_ref[0]], axis=0)
    right = jnp.concatenate([shifted_ref[planes - 3], edge_ref[1], turned_shifts(after)], axis=0)
    grad = dot(turned_ref[...], jnp.concatenate([left, right], axis=1)).astype(BF)
    out_ref[:, 0] = grad[:, :ww].reshape(ch, hh, ww)
    out_ref[:, 1 : planes - 1] = inner_ref[...]
    out_ref[:, planes - 1] = grad[:, ww:].reshape(ch, hh, ww)


def unpack_kernel(scale, a_ref, b_ref, kernel_ref, bias_ref, head_ref, offset_ref):
    ch = kernel_ref.shape[0]
    for q in range(ch // 4):
        value = (a_ref[q * ch : (q + 1) * ch] + b_ref[q * ch : (q + 1) * ch]) * scale
        for r in range(4):
            turned = pltpu.roll(value, 128 - 32 * r, 1) if r else value
            kernel_ref[4 * q + r] = turned[:, 0:27]
    value = (a_ref[4 * ch :] + b_ref[4 * ch :]) * scale
    head_ref[...] = value[:, 0:16]
    bias_ref[...] = pltpu.roll(value, 112, 1)[0:1, 0:16]
    offset_ref[...] = pltpu.roll(value, 96, 1)[0:1, 0:8]


def call(kernel, out_shape, in_spaces, scratch, flops, args):
    moved_bytes = sum(a.size * a.dtype.itemsize for a in args)
    return pl.pallas_call(
        kernel,
        out_shape=out_shape,
        in_specs=[pl.BlockSpec(memory_space=s) for s in in_spaces],
        out_specs=jax.tree.map(lambda _: pl.BlockSpec(memory_space=VM), out_shape),
        scratch_shapes=scratch,
        compiler_params=pltpu.CompilerParams(vmem_limit_bytes=32 << 20),
        cost_estimate=pl.CostEstimate(flops=flops, bytes_accessed=moved_bytes, transcendentals=0),
    )(*args)


def exchange_pairs():
    crops, size = lax.axis_size("dp"), lax.axis_size("depth")
    one, two = [], []
    for c in range(crops):
        for d in range(size):
            one.append((c * size + d, c * size + (d ^ 1)))
            e = ((d + 1) ^ 1) - 1
            if 0 <= e < size:
                two.append((c * size + d, c * size + e))
            elif crops % 2 == 0:
                two.append((c * size + d, (c ^ 1) * size + d))
    return one, two


def exchanged(a, b):
    one, two = exchange_pairs()
    return lax.ppermute(a, ("dp", "depth"), one), lax.ppermute(b, ("dp", "depth"), two)


def body(features, labels, masks, conv_kernel, conv_bias, head_weight, head_bias):
    x, label, mask = features[0, 0], labels[0], masks[0, 0]
    kernel, head = conv_kernel[0], head_weight[0]
    ch, planes, hh, ww = x.shape
    classes = head.shape[0]
    rows = ch * hh
    sds = jax.ShapeDtypeStruct
    size = lax.axis_size("depth")
    pair_flops = 2 * rows * 9 * rows * 2 * ww

    plane = sds((ch, hh, ww), BF)
    inputs = (x, label, mask, kernel.transpose(1, 2, 0), conv_bias, head, head_bias)
    inputs = tuple(pltpu.with_memory_space_constraint(v, pltpu.HBM) for v in inputs)
    shapes = tuple(sds(v.shape, v.dtype) for v in inputs)
    *inputs, end_a, end_b = call(
        load_kernel,
        (*shapes, plane, plane),
        (pltpu.HBM,) * len(inputs),
        [pltpu.SemaphoreType.DMA((len(inputs),))],
        0,
        inputs,
    )
    x, label, mask, kernel, conv_bias, head, head_bias = inputs
    far = exchanged(end_a, end_b)
    inner = planes - 2
    band, shifted, turned_x, hidden_in, diff_in, offered_in = call(
        interior_kernel,
        (
            sds((rows, 9 * rows), BF),
            sds((planes, 3 * rows, ww), BF),
            sds((planes, rows, ww), BF),
            sds((inner, rows, ww), BF),
            sds((inner, classes * hh, ww), F32),
            sds((inner, hh, ww), F32),
        ),
        (VM,) * 7,
        [],
        pair_flops * inner // 2,
        (x, label, mask, kernel, conv_bias, head, head_bias),
    )
    peers = [(0, 1), (1, 0)]
    weight_in = lax.ppermute(offered_in, "net", peers)
    halo, hidden_edge, diff_edge, offered_edge = call(
        edge_kernel,
        (
            sds((2, rows, ww), BF),
            sds((2, rows, ww), BF),
            sds((2, classes * hh, ww), F32),
            sds((2, hh, ww), F32),
        ),
        (VM,) * 9,
        [],
        pair_flops,
        (*far, label, mask, conv_bias, head, head_bias, band, shifted),
    )
    weight_edge = lax.ppermute(offered_edge, "net", peers)
    sums = (
        sds((9, ch, 256), F32),
        sds((rows, ww), F32),
        sds((classes * hh, ww), F32),
        sds((classes * hh, rows), F32),
    )
    grads, *sums = call(
        inner_backward_kernel,
        (sds((inner, 3 * rows, ww), BF), *sums),
        (VM,) * 6,
        [],
        pair_flops * inner // 2,
        (turned_x, weight_in, hidden_in, diff_in, head, halo),
    )
    edge = sds((rows, ww), BF)
    packed, grad_a, grad_b, grad_edge = call(
        edge_backward_kernel,
        (sds((4 * ch + 8, 128), F32), edge, edge, sds((2, 3 * rows, ww), BF)),
        (VM,) * 10,
        [VM((2, 32 * ch, 128), F32)],
        pair_flops,
        (turned_x, halo, weight_edge, hidden_edge, diff_edge, head, *sums),
    )
    turned, grad_inner, grad_a = call(
        inner_grad_kernel,
        (sds((rows, 9 * rows), BF), sds((ch, inner, hh, ww), BF), edge),
        (VM,) * 4,
        [],
        pair_flops * inner // 2,
        (grads, grad_edge, band, grad_a),
    )
    rounds = [("dp", 1 << b) for b in range((lax.axis_size("dp") - 1).bit_length())]
    rounds += [("depth", 1 << b) for b in range((size - 1).bit_length())]
    ends, pairs, grad_far = [grad_a, grad_b], exchange_pairs(), []
    for n, (axis, bit) in enumerate(rounds):
        other = lax.ppermute(packed, axis, [(i, i ^ bit) for i in range(lax.axis_size(axis))])
        if n <= 1:
            grad_far.append(lax.ppermute(ends[n], ("dp", "depth"), pairs[n]))
        if n < len(rounds) - 1:
            packed = packed + other
        if n == 0:
            packed, grad_inner, ends[1] = lax.optimization_barrier((packed, grad_inner, ends[1]))
    grad_input = call(
        edge_grad_kernel,
        sds((ch, planes, hh, ww), BF),
        (VM,) * 6,
        [],
        pair_flops,
        (*grad_far, grads, grad_edge, turned, grad_inner),
    )
    scale = 1.0 / (lax.axis_size("dp") * size * planes * hh * ww)
    grad_kernel, grad_bias, grad_head, grad_offset = call(
        functools.partial(unpack_kernel, scale),
        (sds((ch, ch, 27), F32), sds((1, ch), F32), sds((classes, ch), F32), sds((1, classes), F32)),
        (VM, VM),
        [],
        1000,
        (packed, other),
    )
    return (
        grad_input[None, None],
        grad_kernel.transpose(2, 0, 1)[None],
        grad_bias,
        grad_head[None],
        grad_offset,
    )


def solution(mesh):
    in_specs = (
        P("net", "dp", None, "depth", None, None),
        P("dp", "depth", None, None),
        P("net", "dp", "depth", None, None),
        P("net", None, None, None),
        P("net", None),
        P("net", None, None),
        P("net", None),
    )
    out_specs = (
        P("net", "dp", None, "depth", None, None),
        P("net", None, None, None),
        P("net", None),
        P("net", None, None),
        P("net", None),
    )
    return jax.shard_map(body, mesh=mesh, in_specs=in_specs, out_specs=out_specs, check_vma=False)
```

```python
import functools

import jax
import jax.numpy as jnp
from jax import lax
from jax.experimental import pallas as pl
from jax.experimental.pallas import tpu as pltpu
from jax.sharding import PartitionSpec as P

BF = jnp.bfloat16
F32 = jnp.float32
VM = pltpu.VMEM
SM = pltpu.SMEM


def iota(shape, dim):
    return lax.broadcasted_iota(jnp.int32, shape, dim)


def over(x, n):
    return lax.shift_right_logical(x, n.bit_length() - 1) if n & (n - 1) == 0 else x // n


def rest(x, n):
    return lax.bitwise_and(x, n - 1) if n & (n - 1) == 0 else lax.rem(x, n)


def dot(a, b):
    return jnp.dot(a, b, preferred_element_type=F32)


def dot_nt(a, b):
    return lax.dot_general(a, b, (((1,), (1,)), ((), ())), preferred_element_type=F32)


def split3(x):
    high = x.astype(BF)
    rest = x - high.astype(F32)
    mid = rest.astype(BF)
    return high, mid, (rest - mid.astype(F32)).astype(BF)


def dot_exact(x, ones):
    return sum(dot(part, ones) for part in split3(x))


def moved(x):
    y = x.astype(F32)
    lane = iota(y.shape, 1)
    width = y.shape[1]
    before = jnp.where(lane == 0, 0.0, pltpu.roll(y, 1, 1))
    after = jnp.where(lane == width - 1, 0.0, pltpu.roll(y, width - 1, 1))
    return before.astype(BF), after.astype(BF)


def fill_band(kernel_ref, band_ref, ch, hh):
    rows = ch * hh
    unit = (iota((32, 27), 0) == iota((32, 27), 1)).astype(F32).astype(BF)
    by_tap = dot_nt(unit, kernel_ref[...].reshape(ch * ch, 27))
    wide = jnp.broadcast_to(by_tap[:27, None, :], (27, ch, ch * ch))
    wide = jnp.where(over(iota((27, ch, ch * ch), 2), ch) == iota((27, ch, ch * ch), 1), wide, 0.0)
    spread = (over(iota((ch * ch, rows), 1), hh) == rest(iota((ch * ch, rows), 0), ch)).astype(F32).astype(BF)
    wide = dot(wide.reshape(27 * ch, ch * ch).astype(BF), spread).astype(BF)
    masks = [(rest(iota((ch, rows), 1), hh) == h).astype(F32).astype(BF) for h in range(hh)]
    for i in range(3):
        for k in range(3):
            taps = [wide[(9 * i + 3 * j + k) * ch : (9 * i + 3 * j + k + 1) * ch] for j in range(3)]
            col = (3 * i + k) * rows
            for h in range(hh):
                block = masks[h] * taps[1]
                if h > 0:
                    block = block + masks[h - 1] * taps[0]
                if h < hh - 1:
                    block = block + masks[h + 1] * taps[2]
                band_ref[h * ch : (h + 1) * ch, col : col + rows] = block


def head_matrix(head_ref, ch, hh, classes):
    rows = ch * hh
    spread = (rest(iota((ch, rows), 1), ch) == iota((ch, rows), 0)).astype(F32).astype(BF)
    wide = dot(head_ref[...], spread)
    wide = jnp.broadcast_to(wide[:, None, :], (classes, hh, rows))
    keep = over(iota((classes, hh, rows), 2), ch) == iota((classes, hh, rows), 1)
    return jnp.where(keep, wide, 0.0).reshape(classes * hh, rows).astype(BF)


def bias_rows(bias_ref, ch, width):
    square = jnp.broadcast_to(bias_ref[...], (ch, ch))
    column = jnp.sum(jnp.where(iota((ch, ch), 0) == iota((ch, ch), 1), square, 0.0), axis=1, keepdims=True)
    return jnp.broadcast_to(column, (ch, width))


def shifts(x):
    before, after = moved(x)
    return jnp.concatenate([before, x, after], axis=0)


def head_pair(preact, bias, mat, head_bias_ref, label, mask, dims):
    ch, hh, ww, classes = dims
    rows = ch * hh
    preact = (preact.reshape(hh, ch, 2 * ww) + bias[None]).reshape(rows, 2 * ww)
    hidden = jnp.maximum(preact, 0.0).astype(BF)
    logits = dot(mat, hidden).reshape(classes, hh, 2 * ww)
    parts = [logits[c] + head_bias_ref[0:1, c : c + 1] for c in range(classes)]
    total = functools.reduce(jnp.add, [jnp.exp(p) for p in parts])
    log_total = jnp.log(total)
    soft = [jnp.exp(p - log_total) for p in parts]
    hot = [label == c for c in range(classes)]
    chosen = functools.reduce(jnp.add, [jnp.where(o, s, 0.0) for o, s in zip(hot, soft)])
    diffs = [s - jnp.where(o, 1.0, 0.0) for o, s in zip(hot, soft)]
    return hidden, jnp.stack(diffs).reshape(classes * hh, 2 * ww), mask * chosen


def put_pair(ref, first, second, value, ww):
    ref[first] = value[:, :ww]
    ref[second] = value[:, ww:]


def beside(ref, first, second):
    return jnp.concatenate([ref[first], ref[second]], axis=1)


def load_kernel(*refs):
    count = (len(refs) - 3) // 2
    sources, targets, (a_ref, b_ref, sems) = refs[:count], refs[count : 2 * count], refs[2 * count :]
    planes = sources[0].shape[1]
    copies = [pltpu.make_async_copy(s, t, sems.at[n]) for n, (s, t) in enumerate(zip(sources, targets))]
    for copy in copies:
        copy.start()
    copies[0].wait()
    odd = lax.rem(lax.axis_index("depth"), 2)
    a_ref[...] = targets[0][:, (1 - odd) * (planes - 1)]
    b_ref[...] = targets[0][:, odd * (planes - 1)]
    for copy in copies[1:]:
        copy.wait()


def sorted_halo(a, b):
    place, size = lax.axis_index("depth"), lax.axis_size("depth")
    odd = lax.rem(place, 2) == 1
    before, after = jnp.where(odd, a, b), jnp.where(odd, b, a)
    before = jnp.where(place > 0, before, 0.0)
    after = jnp.where(place < size - 1, after, 0.0)
    return before.astype(BF), after.astype(BF)


def turner(ch, hh):
    rows = ch * hh
    row, col = iota((rows, rows), 0), iota((rows, rows), 1)
    return ((over(row, ch) == rest(col, hh)) & (rest(row, ch) == over(col, hh))).astype(F32).astype(BF)


def interior_kernel(
    x_ref, label_ref, mask_ref, kernel_ref, bias_ref, head_ref, head_bias_ref,
    band_ref, mat_ref, mat_t_ref, turner_ref, bias_out_ref,
    shifted_ref, turned_ref, hidden_ref, diff_ref, offered_ref,
):
    ch, planes, hh, ww = x_ref.shape
    classes = head_ref.shape[0]
    rows = ch * hh
    inner = planes - 2
    fill_band(kernel_ref, band_ref, ch, hh)
    mat = head_matrix(head_ref, ch, hh, classes)
    bias = bias_rows(bias_ref, ch, 2 * ww)
    field = [x_ref[:, d].reshape(rows, ww) for d in range(planes)]
    for d in range(planes):
        shifted_ref[d] = shifts(field[d])
    wide = [shifted_ref[d : d + 3].reshape(9 * rows, ww) for d in range(inner)]
    preact = dot(band_ref[...], jnp.concatenate(wide, axis=1))
    for d in range(0, inner, 2):
        hidden, diff, offered = head_pair(
            preact[:, d * ww : (d + 2) * ww], bias, mat, head_bias_ref, beside(label_ref, d + 1, d + 2),
            beside(mask_ref, d + 1, d + 2).astype(F32), (ch, hh, ww, classes),
        )
        put_pair(hidden_ref, d, d + 1, hidden, ww)
        put_pair(diff_ref, d, d + 1, diff, ww)
        put_pair(offered_ref, d, d + 1, offered, ww)
    turn = turner(ch, hh)
    turned = dot(turn, jnp.concatenate(field, axis=1)).astype(BF)
    for d in range(planes):
        turned_ref[d] = turned[:, d * ww : (d + 1) * ww]
    unit = (iota((rows, rows), 0) == iota((rows, rows), 1)).astype(F32).astype(BF)
    mat_ref[...], mat_t_ref[...], turner_ref[...], bias_out_ref[...] = mat, dot_nt(unit, mat).astype(BF), turn, bias


def edge_kernel(
    a_ref, b_ref, label_ref, mask_ref, head_bias_ref, band_ref, mat_ref, turner_ref, bias_ref, shifted_ref,
    halo_ref, hidden_ref, diff_ref, offered_ref,
):
    ch, hh, ww = a_ref.shape
    planes, classes = label_ref.shape[0], mat_ref.shape[0] // hh
    rows = ch * hh
    before, after = sorted_halo(a_ref[...].reshape(rows, ww).astype(F32), b_ref[...].reshape(rows, ww).astype(F32))
    left = jnp.concatenate([shifts(before), shifted_ref[0:2].reshape(6 * rows, ww)], axis=0)
    right = jnp.concatenate([shifted_ref[planes - 2 : planes].reshape(6 * rows, ww), shifts(after)], axis=0)
    preact = dot(band_ref[...], jnp.concatenate([left, right], axis=1))
    hidden, diff, offered = head_pair(
        preact, bias_ref[...], mat_ref[...], head_bias_ref, beside(label_ref, 0, planes - 1),
        beside(mask_ref, 0, planes - 1).astype(F32), (ch, hh, ww, classes),
    )
    put_pair(hidden_ref, 0, 1, hidden, ww)
    put_pair(diff_ref, 0, 1, diff, ww)
    put_pair(offered_ref, 0, 1, offered, ww)
    turned = dot(turner_ref[...], jnp.concatenate([before, after], axis=1)).astype(BF)
    put_pair(halo_ref, 0, 1, turned, ww)


def backward_planes(diff_ref, weight_ref, hidden_ref, mat_t_ref, shifted_ref):
    count, rows, ww = hidden_ref.shape
    hh = weight_ref.shape[1]
    classes = diff_ref.shape[1] // hh
    offset_sum, halves = 0.0, []
    for d in range(count):
        grad = (diff_ref[d].reshape(classes, hh, ww) * weight_ref[d][None]).reshape(classes * hh, ww)
        offset_sum = offset_sum + grad
        halves.append(grad.astype(BF))
    halves = jnp.concatenate(halves, axis=1)
    hiddens = jnp.concatenate([hidden_ref[d] for d in range(count)], axis=1)
    pre = jnp.where(hiddens.astype(F32) > 0.0, dot(mat_t_ref[...], halves), 0.0)
    bias_sum = sum(pre[:, d * ww : (d + 1) * ww] for d in range(count))
    values = [pre[:, d * ww : (d + 1) * ww].astype(BF) for d in range(count)]
    for d in range(count):
        before, after = moved(values[d])
        shifted_ref[d] = jnp.concatenate([after, values[d], before], axis=0)
    return values, bias_sum, offset_sum, dot_nt(halves, hiddens)


STEP = 3


def weight_products(shifted_ref, fields, ch, hh, totals):
    count, rows3, ww = shifted_ref.shape
    rows = rows3 // 3
    span = STEP + 2
    spot = rest(over(iota((ch, 256), 1), ch), span)
    grads = [shifted_ref[d] for d in range(count)]
    for h0 in range(0, hh, STEP):
        step = min(STEP, hh - h0)
        left = [g[k * rows + h0 * ch : k * rows + (h0 + step) * ch] for k in range(3) for g in grads]
        left = [jnp.concatenate(left[k * count : (k + 1) * count], axis=1) for k in range(3)]
        low, high = max(h0 - 1, 0), min(h0 + span - 1, hh)
        right = []
        for i in range(3):
            if h0 == 0:
                right.append(jnp.zeros((ch, count * ww), BF))
            right.append(jnp.concatenate([f[low * ch : high * ch] for f in fields[i]], axis=1))
            if h0 + span - 1 > hh:
                right.append(jnp.zeros(((h0 + span - 1 - hh) * ch, count * ww), BF))
        right.append(jnp.zeros((256 - 3 * span * ch, count * ww), BF))
        product = dot_nt(jnp.concatenate(left, axis=0), jnp.concatenate(right, axis=0))
        for k in range(3):
            for j in range(3):
                total = jnp.zeros((ch, 256), F32)
                for h in range(step):
                    r = (k * step + h) * ch
                    total = jnp.where(spot == h + j, product[r : r + ch], total)
                totals[3 * k + j] = totals[3 * k + j] + total
    return totals


def inner_backward_kernel(
    turned_ref, weight_ref, hidden_ref, diff_ref, mat_t_ref, after_ref,
    shifted_ref, total_ref, bias_ref, offset_ref, product_ref,
):
    del after_ref
    inner, rows, ww = hidden_ref.shape
    hh = weight_ref.shape[1]
    _, bias_ref[...], offset_ref[...], product_ref[...] = backward_planes(
        diff_ref, weight_ref, hidden_ref, mat_t_ref, shifted_ref
    )
    fields = [[turned_ref[d + i] for d in range(inner)] for i in range(3)]
    totals = weight_products(shifted_ref, fields, rows // hh, hh, [0.0] * 9)
    for n in range(9):
        total_ref[n] = totals[n]


def edge_backward_kernel(
    turned_ref, halo_ref, weight_ref, hidden_ref, diff_ref, mat_t_ref, total_ref, bias_in_ref, offset_in_ref, product_in_ref,
    packed_ref, a_ref, b_ref, shifted_ref, rows_ref,
):
    planes, rows, ww = turned_ref.shape
    hh = weight_ref.shape[1]
    ch, classes = rows // hh, diff_ref.shape[1] // hh
    values, bias_sum, offset_sum, product = backward_planes(diff_ref, weight_ref, hidden_ref, mat_t_ref, shifted_ref)
    bias_sum, offset_sum = bias_sum + bias_in_ref[...], offset_sum + offset_in_ref[...]
    product = product + product_in_ref[...]
    odd = lax.rem(lax.axis_index("depth"), 2) == 1
    first, last = values[0].astype(F32), values[1].astype(F32)
    a_ref[...] = jnp.where(odd, first, last).astype(BF)
    b_ref[...] = jnp.where(odd, last, first).astype(BF)
    fields = [
        [halo_ref[0], turned_ref[planes - 2]],
        [turned_ref[0], turned_ref[planes - 1]],
        [turned_ref[1], halo_ref[1]],
    ]
    totals = weight_products(shifted_ref, fields, ch, hh, [total_ref[n] for n in range(9)])
    part = over(iota((ch, 256), 1), ch * (STEP + 2))
    for half in range(2):
        for t in range(32):
            i, j, k = t // 9, t // 3 % 3, t % 3
            value = jnp.where(part == i, totals[3 * k + j], 0.0) if t < 27 else jnp.zeros((ch, 256), F32)
            rows_ref[half, pl.ds(t, ch, stride=32)] = value[:, 128 * half : 128 * half + 128]
    pick = (rest(iota((ch, 128), 1), ch) == iota((ch, 128), 0)).astype(F32).astype(BF)
    sums = sum(dot_nt(pick, part) for half in range(2) for part in split3(rows_ref[half]))
    for q in range(ch // 4):
        packed_ref[q * ch : (q + 1) * ch] = sums[:, 128 * q : 128 * q + 128]
    product = product.reshape(classes, hh, rows)
    keep = over(iota((classes, hh, rows), 2), ch) == iota((classes, hh, rows), 1)
    head = jnp.sum(jnp.where(keep, product, 0.0), axis=1)
    by_last = (rest(iota((rows, 128), 0), ch) == rest(iota((rows, 128), 1), 16)).astype(F32).astype(BF)
    head = dot_exact(head, by_last)
    ones = jnp.ones((16, ww), F32).astype(BF)
    bias = jnp.sum(bias_sum.reshape(hh, ch, ww), axis=0)
    bias = jnp.concatenate([bias] * 8, axis=0)
    bias = sum(dot_nt(ones, part) for part in split3(bias))[:classes]
    offset = sum(dot_nt(ones, part) for part in split3(offset_sum))
    by_class = (over(iota((classes * hh, 128), 0), hh) == rest(iota((classes * hh, 128), 1), 16)).astype(F32).astype(BF)
    offset = dot_exact(offset, by_class)[:classes]
    group = over(iota((classes, 128), 1), 16)
    packed_ref[4 * ch : 4 * ch + classes] = jnp.where(group == 0, head, jnp.where(group == 1, bias, offset))


def inner_grad_kernel(shifted_ref, edge_ref, band_ref, turned_ref, out_ref):
    ch, inner, hh, ww = out_ref.shape
    rows = ch * hh
    unit = (iota((rows, rows), 0) == iota((rows, rows), 1)).astype(F32).astype(BF)
    for i in range(3):
        for k in range(3):
            block = band_ref[:, (3 * i + k) * rows : (3 * i + k + 1) * rows]
            col = (3 * (2 - i) + k) * rows
            turned_ref[:, col : col + rows] = dot_nt(unit, block).astype(BF)
    planes = [edge_ref[0]] + [shifted_ref[d] for d in range(inner)] + [edge_ref[1]]
    wide = [jnp.concatenate(planes[d : d + 3], axis=0) for d in range(inner)]
    grad = dot(turned_ref[...], jnp.concatenate(wide, axis=1)).astype(BF)
    for d in range(inner):
        out_ref[:, d] = grad[:, d * ww : (d + 1) * ww].reshape(ch, hh, ww)


def edge_grad_kernel(a_ref, b_ref, shifted_ref, edge_ref, turned_ref, inner_ref, out_ref):
    ch, planes, hh, ww = out_ref.shape
    rows = ch * hh

    def turned_shifts(x):
        before, after = moved(x)
        return jnp.concatenate([after, x, before], axis=0)

    before, after = sorted_halo(a_ref[...].astype(F32), b_ref[...].astype(F32))
    left = jnp.concatenate([turned_shifts(before), edge_ref[0], shifted_ref[0]], axis=0)
    right = jnp.concatenate([shifted_ref[planes - 3], edge_ref[1], turned_shifts(after)], axis=0)
    grad = dot(turned_ref[...], jnp.concatenate([left, right], axis=1)).astype(BF)
    out_ref[:, 0] = grad[:, :ww].reshape(ch, hh, ww)
    out_ref[:, 1 : planes - 1] = inner_ref[...]
    out_ref[:, planes - 1] = grad[:, ww:].reshape(ch, hh, ww)


def unpack_kernel(scale, own_ref, *refs):
    others, (kernel_ref, bias_ref, head_ref, offset_ref) = refs[:-4], refs[-4:]
    ch = kernel_ref.shape[0]
    total = functools.reduce(jnp.add, [r[...] for r in others], own_ref[...]) * scale
    for q in range(ch // 4):
        value = total[q * ch : (q + 1) * ch]
        for r in range(4):
            turned = pltpu.roll(value, 128 - 32 * r, 1) if r else value
            kernel_ref[4 * q + r] = turned[:, 0:27]
    value = total[4 * ch :]
    head_ref[...] = value[:, 0:16]
    bias_ref[...] = pltpu.roll(value, 112, 1)[0:1, 0:16]
    offset_ref[...] = pltpu.roll(value, 96, 1)[0:1, 0:8]


def call(kernel, out_shape, in_spaces, scratch, flops, args):
    moved_bytes = sum(a.size * a.dtype.itemsize for a in args)
    return pl.pallas_call(
        kernel,
        out_shape=out_shape,
        in_specs=[pl.BlockSpec(memory_space=s) for s in in_spaces],
        out_specs=jax.tree.map(lambda _: pl.BlockSpec(memory_space=VM), out_shape),
        scratch_shapes=scratch,
        compiler_params=pltpu.CompilerParams(vmem_limit_bytes=32 << 20),
        cost_estimate=pl.CostEstimate(flops=flops, bytes_accessed=moved_bytes, transcendentals=0),
    )(*args)


def exchange_pairs():
    crops, size = lax.axis_size("dp"), lax.axis_size("depth")
    one, two = [], []
    for c in range(crops):
        for d in range(size):
            one.append((c * size + d, c * size + (d ^ 1)))
            e = ((d + 1) ^ 1) - 1
            if 0 <= e < size:
                two.append((c * size + d, c * size + e))
            elif crops % 2 == 0:
                two.append((c * size + d, (c ^ 1) * size + d))
    return one, two


def exchanged(a, b):
    one, two = exchange_pairs()
    return lax.ppermute(a, ("dp", "depth"), one), lax.ppermute(b, ("dp", "depth"), two)


def reduction_rounds():
    count = lax.axis_size("dp") * lax.axis_size("depth")
    bits = [1 << b for b in range((count - 1).bit_length())]
    bits = bits[-1:] + bits[1:2] + bits[:1] + bits[2:-1] if len(bits) >= 4 else bits
    rounds = []
    for n in range(0, len(bits), 2):
        masks = bits[n : n + 2]
        masks = masks + [sum(masks)] if len(masks) == 2 else masks
        rounds.append([[(i, i ^ m) for i in range(count)] for m in masks])
    return rounds


def body(features, labels, masks, conv_kernel, conv_bias, head_weight, head_bias):
    x, label, mask = features[0, 0], labels[0], masks[0, 0]
    kernel, head = conv_kernel[0], head_weight[0]
    ch, planes, hh, ww = x.shape
    classes = head.shape[0]
    rows = ch * hh
    sds = jax.ShapeDtypeStruct
    size = lax.axis_size("depth")
    pair_flops = 2 * rows * 9 * rows * 2 * ww

    plane = sds((ch, hh, ww), BF)
    inputs = (x, label, mask, kernel.transpose(1, 2, 0), conv_bias, head, head_bias)
    inputs = tuple(pltpu.with_memory_space_constraint(v, pltpu.HBM) for v in inputs)
    shapes = tuple(sds(v.shape, v.dtype) for v in inputs)
    *inputs, end_a, end_b = call(
        load_kernel,
        (*shapes, plane, plane),
        (pltpu.HBM,) * len(inputs),
        [pltpu.SemaphoreType.DMA((len(inputs),))],
        0,
        inputs,
    )
    x, label, mask, kernel, conv_bias, head, head_bias = inputs
    far = exchanged(end_a, end_b)
    inner = planes - 2
    band, mat, mat_t, turn, bias, shifted, turned_x, hidden_in, diff_in, offered_in = call(
        interior_kernel,
        (
            sds((rows, 9 * rows), BF),
            sds((classes * hh, rows), BF),
            sds((rows, classes * hh), BF),
            sds((rows, rows), BF),
            sds((ch, 2 * ww), F32),
            sds((planes, 3 * rows, ww), BF),
            sds((planes, rows, ww), BF),
            sds((inner, rows, ww), BF),
            sds((inner, classes * hh, ww), F32),
            sds((inner, hh, ww), F32),
        ),
        (VM,) * 7,
        [],
        pair_flops * inner // 2,
        (x, label, mask, kernel, conv_bias, head, head_bias),
    )
    peers = [(0, 1), (1, 0)]
    weight_in = lax.ppermute(offered_in, "net", peers)
    halo, hidden_edge, diff_edge, offered_edge = call(
        edge_kernel,
        (
            sds((2, rows, ww), BF),
            sds((2, rows, ww), BF),
            sds((2, classes * hh, ww), F32),
            sds((2, hh, ww), F32),
        ),
        (VM,) * 10,
        [],
        pair_flops,
        (*far, label, mask, head_bias, band, mat, turn, bias, shifted),
    )
    weight_edge = lax.ppermute(offered_edge, "net", peers)
    sums = (
        sds((9, ch, 256), F32),
        sds((rows, ww), F32),
        sds((classes * hh, ww), F32),
        sds((classes * hh, rows), F32),
    )
    grads, *sums = call(
        inner_backward_kernel,
        (sds((inner, 3 * rows, ww), BF), *sums),
        (VM,) * 6,
        [],
        pair_flops * inner // 2,
        (turned_x, weight_in, hidden_in, diff_in, mat_t, halo),
    )
    edge = sds((rows, ww), BF)
    packed, grad_a, grad_b, grad_edge = call(
        edge_backward_kernel,
        (sds((4 * ch + 8, 128), F32), edge, edge, sds((2, 3 * rows, ww), BF)),
        (VM,) * 10,
        [VM((2, 32 * ch, 128), F32)],
        pair_flops,
        (turned_x, halo, weight_edge, hidden_edge, diff_edge, mat_t, *sums),
    )
    rounds, pairs = reduction_rounds(), exchange_pairs()
    for n, masks in enumerate(rounds):
        others = [lax.ppermute(packed, ("dp", "depth"), p) for p in masks]
        if n == 0:
            grad_far = [lax.ppermute(e, ("dp", "depth"), p) for e, p in zip((grad_a, grad_b), pairs)]
        if n < len(rounds) - 1:
            packed = functools.reduce(jnp.add, others, packed)
        if n == len(rounds) - 2:
            packed, band = lax.optimization_barrier((packed, band))
    turned, grad_inner = call(
        inner_grad_kernel,
        (sds((rows, 9 * rows), BF), sds((ch, inner, hh, ww), BF)),
        (VM,) * 3,
        [],
        pair_flops * inner // 2,
        (grads, grad_edge, band),
    )
    grad_input = call(
        edge_grad_kernel,
        sds((ch, planes, hh, ww), BF),
        (VM,) * 6,
        [],
        pair_flops,
        (*grad_far, grads, grad_edge, turned, grad_inner),
    )
    scale = 1.0 / (lax.axis_size("dp") * size * planes * hh * ww)
    grad_kernel, grad_bias, grad_head, grad_offset = call(
        functools.partial(unpack_kernel, scale),
        (sds((ch, ch, 27), F32), sds((1, ch), F32), sds((classes, ch), F32), sds((1, classes), F32)),
        (VM,) * (1 + len(others)),
        [],
        1000,
        (packed, *others),
    )
    return (
        grad_input[None, None],
        grad_kernel.transpose(2, 0, 1)[None],
        grad_bias,
        grad_head[None],
        grad_offset,
    )


def solution(mesh):
    in_specs = (
        P("net", "dp", None, "depth", None, None),
        P("dp", "depth", None, None),
        P("net", "dp", "depth", None, None),
        P("net", None, None, None),
        P("net", None),
        P("net", None, None),
        P("net", None),
    )
    out_specs = (
        P("net", "dp", None, "depth", None, None),
        P("net", None, None, None),
        P("net", None),
        P("net", None, None),
        P("net", None),
    )
    return jax.shard_map(body, mesh=mesh, in_specs=in_specs, out_specs=out_specs, check_vma=False)
```

```python
import functools

import jax
import jax.numpy as jnp
from jax import lax
from jax.experimental import pallas as pl
from jax.experimental.pallas import tpu as pltpu
from jax.sharding import PartitionSpec as P

BF = jnp.bfloat16
F32 = jnp.float32
VM = pltpu.VMEM
SM = pltpu.SMEM


def iota(shape, dim):
    return lax.broadcasted_iota(jnp.int32, shape, dim)


def over(x, n):
    return lax.shift_right_logical(x, n.bit_length() - 1) if n & (n - 1) == 0 else x // n


def rest(x, n):
    return lax.bitwise_and(x, n - 1) if n & (n - 1) == 0 else lax.rem(x, n)


def dot(a, b):
    return jnp.dot(a, b, preferred_element_type=F32)


def dot_nt(a, b):
    return lax.dot_general(a, b, (((1,), (1,)), ((), ())), preferred_element_type=F32)


def split3(x):
    high = x.astype(BF)
    rest = x - high.astype(F32)
    mid = rest.astype(BF)
    return high, mid, (rest - mid.astype(F32)).astype(BF)


def dot_exact(x, ones):
    return sum(dot(part, ones) for part in split3(x))


def moved(x):
    y = x.astype(F32)
    lane = iota(y.shape, 1)
    width = y.shape[1]
    before = jnp.where(lane == 0, 0.0, pltpu.roll(y, 1, 1))
    after = jnp.where(lane == width - 1, 0.0, pltpu.roll(y, width - 1, 1))
    return before.astype(BF), after.astype(BF)


def fill_band(kernel_ref, band_ref, ch, hh):
    rows = ch * hh
    unit = (iota((32, 27), 0) == iota((32, 27), 1)).astype(F32).astype(BF)
    by_tap = dot_nt(unit, kernel_ref[...].reshape(ch * ch, 27))
    wide = jnp.broadcast_to(by_tap[:27, None, :], (27, ch, ch * ch))
    wide = jnp.where(over(iota((27, ch, ch * ch), 2), ch) == iota((27, ch, ch * ch), 1), wide, 0.0)
    spread = (over(iota((ch * ch, rows), 1), hh) == rest(iota((ch * ch, rows), 0), ch)).astype(F32).astype(BF)
    wide = dot(wide.reshape(27 * ch, ch * ch).astype(BF), spread).astype(BF)
    masks = [(rest(iota((ch, rows), 1), hh) == h).astype(F32).astype(BF) for h in range(hh)]
    for i in range(3):
        for k in range(3):
            taps = [wide[(9 * i + 3 * j + k) * ch : (9 * i + 3 * j + k + 1) * ch] for j in range(3)]
            col = (3 * i + k) * rows
            for h in range(hh):
                block = masks[h] * taps[1]
                if h > 0:
                    block = block + masks[h - 1] * taps[0]
                if h < hh - 1:
                    block = block + masks[h + 1] * taps[2]
                band_ref[h * ch : (h + 1) * ch, col : col + rows] = block


def head_matrix(head_ref, ch, hh, classes):
    rows = ch * hh
    spread = (rest(iota((ch, rows), 1), ch) == iota((ch, rows), 0)).astype(F32).astype(BF)
    wide = dot(head_ref[...], spread)
    wide = jnp.broadcast_to(wide[:, None, :], (classes, hh, rows))
    keep = over(iota((classes, hh, rows), 2), ch) == iota((classes, hh, rows), 1)
    return jnp.where(keep, wide, 0.0).reshape(classes * hh, rows).astype(BF)


def bias_rows(bias_ref, ch, width):
    square = jnp.broadcast_to(bias_ref[...], (ch, ch))
    column = jnp.sum(jnp.where(iota((ch, ch), 0) == iota((ch, ch), 1), square, 0.0), axis=1, keepdims=True)
    return jnp.broadcast_to(column, (ch, width))


def shifts(x):
    before, after = moved(x)
    return jnp.concatenate([before, x, after], axis=0)


def head_pair(preact, bias, mat, head_bias_ref, label, mask, dims):
    ch, hh, ww, classes = dims
    rows = ch * hh
    preact = (preact.reshape(hh, ch, 2 * ww) + bias[None]).reshape(rows, 2 * ww)
    hidden = jnp.maximum(preact, 0.0).astype(BF)
    logits = dot(mat, hidden).reshape(classes, hh, 2 * ww)
    parts = [logits[c] + head_bias_ref[0:1, c : c + 1] for c in range(classes)]
    total = functools.reduce(jnp.add, [jnp.exp(p) for p in parts])
    log_total = jnp.log(total)
    soft = [jnp.exp(p - log_total) for p in parts]
    hot = [label == c for c in range(classes)]
    chosen = functools.reduce(jnp.add, [jnp.where(o, s, 0.0) for o, s in zip(hot, soft)])
    diffs = [s - jnp.where(o, 1.0, 0.0) for o, s in zip(hot, soft)]
    return hidden, jnp.stack(diffs).reshape(classes * hh, 2 * ww), mask * chosen


def put_pair(ref, first, second, value, ww):
    ref[first] = value[:, :ww]
    ref[second] = value[:, ww:]


def beside(ref, first, second):
    return jnp.concatenate([ref[first], ref[second]], axis=1)


def load_kernel(*refs):
    count = (len(refs) - 3) // 2
    sources, targets, (a_ref, b_ref, sems) = refs[:count], refs[count : 2 * count], refs[2 * count :]
    planes = sources[0].shape[1]
    copies = [pltpu.make_async_copy(s, t, sems.at[n]) for n, (s, t) in enumerate(zip(sources, targets))]
    for copy in copies:
        copy.start()
    copies[0].wait()
    odd = lax.rem(lax.axis_index("depth"), 2)
    a_ref[...] = targets[0][:, (1 - odd) * (planes - 1)]
    b_ref[...] = targets[0][:, odd * (planes - 1)]
    for copy in copies[1:]:
        copy.wait()


def sorted_halo(a, b):
    place, size = lax.axis_index("depth"), lax.axis_size("depth")
    odd = lax.rem(place, 2) == 1
    before, after = jnp.where(odd, a, b), jnp.where(odd, b, a)
    before = jnp.where(place > 0, before, 0.0)
    after = jnp.where(place < size - 1, after, 0.0)
    return before.astype(BF), after.astype(BF)


def turner(ch, hh):
    rows = ch * hh
    row, col = iota((rows, rows), 0), iota((rows, rows), 1)
    return ((over(row, ch) == rest(col, hh)) & (rest(row, ch) == over(col, hh))).astype(F32).astype(BF)


def interior_kernel(
    x_ref, label_ref, mask_ref, kernel_ref, bias_ref, head_ref, head_bias_ref,
    band_ref, mat_ref, mat_t_ref, turner_ref, bias_out_ref,
    shifted_ref, turned_ref, hidden_ref, diff_ref, offered_ref,
):
    ch, planes, hh, ww = x_ref.shape
    classes = head_ref.shape[0]
    rows = ch * hh
    inner = planes - 2
    fill_band(kernel_ref, band_ref, ch, hh)
    mat = head_matrix(head_ref, ch, hh, classes)
    bias = bias_rows(bias_ref, ch, 2 * ww)
    field = [x_ref[:, d].reshape(rows, ww) for d in range(planes)]
    for d in range(planes):
        shifted_ref[d] = shifts(field[d])
    wide = [shifted_ref[d : d + 3].reshape(9 * rows, ww) for d in range(inner)]
    preact = dot(band_ref[...], jnp.concatenate(wide, axis=1))
    for d in range(0, inner, 2):
        hidden, diff, offered = head_pair(
            preact[:, d * ww : (d + 2) * ww], bias, mat, head_bias_ref, beside(label_ref, d + 1, d + 2),
            beside(mask_ref, d + 1, d + 2).astype(F32), (ch, hh, ww, classes),
        )
        put_pair(hidden_ref, d, d + 1, hidden, ww)
        put_pair(diff_ref, d, d + 1, diff, ww)
        put_pair(offered_ref, d, d + 1, offered, ww)
    turn = turner(ch, hh)
    turned = dot(turn, jnp.concatenate(field, axis=1)).astype(BF)
    for d in range(planes):
        turned_ref[d] = turned[:, d * ww : (d + 1) * ww]
    unit = (iota((rows, rows), 0) == iota((rows, rows), 1)).astype(F32).astype(BF)
    mat_ref[...], mat_t_ref[...], turner_ref[...], bias_out_ref[...] = mat, dot_nt(unit, mat).astype(BF), turn, bias


def edge_kernel(
    a_ref, b_ref, label_ref, mask_ref, head_bias_ref, band_ref, mat_ref, turner_ref, bias_ref, shifted_ref,
    halo_ref, hidden_ref, diff_ref, offered_ref,
):
    ch, hh, ww = a_ref.shape
    planes, classes = label_ref.shape[0], mat_ref.shape[0] // hh
    rows = ch * hh
    before, after = sorted_halo(a_ref[...].reshape(rows, ww).astype(F32), b_ref[...].reshape(rows, ww).astype(F32))
    left = jnp.concatenate([shifts(before), shifted_ref[0:2].reshape(6 * rows, ww)], axis=0)
    right = jnp.concatenate([shifted_ref[planes - 2 : planes].reshape(6 * rows, ww), shifts(after)], axis=0)
    preact = dot(band_ref[...], jnp.concatenate([left, right], axis=1))
    hidden, diff, offered = head_pair(
        preact, bias_ref[...], mat_ref[...], head_bias_ref, beside(label_ref, 0, planes - 1),
        beside(mask_ref, 0, planes - 1).astype(F32), (ch, hh, ww, classes),
    )
    put_pair(hidden_ref, 0, 1, hidden, ww)
    put_pair(diff_ref, 0, 1, diff, ww)
    put_pair(offered_ref, 0, 1, offered, ww)
    turned = dot(turner_ref[...], jnp.concatenate([before, after], axis=1)).astype(BF)
    put_pair(halo_ref, 0, 1, turned, ww)


def backward_planes(diff_ref, weight_ref, hidden_ref, mat_t_ref, shifted_ref):
    count, rows, ww = hidden_ref.shape
    hh = weight_ref.shape[1]
    classes = diff_ref.shape[1] // hh
    offset_sum, halves = 0.0, []
    for d in range(count):
        grad = (diff_ref[d].reshape(classes, hh, ww) * weight_ref[d][None]).reshape(classes * hh, ww)
        offset_sum = offset_sum + grad
        halves.append(grad.astype(BF))
    halves = jnp.concatenate(halves, axis=1)
    hiddens = jnp.concatenate([hidden_ref[d] for d in range(count)], axis=1)
    pre = jnp.where(hiddens.astype(F32) > 0.0, dot(mat_t_ref[...], halves), 0.0)
    bias_sum = sum(pre[:, d * ww : (d + 1) * ww] for d in range(count))
    values = [pre[:, d * ww : (d + 1) * ww].astype(BF) for d in range(count)]
    for d in range(count):
        before, after = moved(values[d])
        shifted_ref[d] = jnp.concatenate([after, values[d], before], axis=0)
    return values, bias_sum, offset_sum, dot_nt(halves, hiddens)


STEP = 3


def weight_products(shifted_ref, fields, ch, hh, totals):
    count, rows3, ww = shifted_ref.shape
    rows = rows3 // 3
    span = STEP + 2
    spot = rest(over(iota((ch, 256), 1), ch), span)
    grads = [shifted_ref[d] for d in range(count)]
    for h0 in range(0, hh, STEP):
        step = min(STEP, hh - h0)
        left = [g[k * rows + h0 * ch : k * rows + (h0 + step) * ch] for k in range(3) for g in grads]
        left = [jnp.concatenate(left[k * count : (k + 1) * count], axis=1) for k in range(3)]
        low, high = max(h0 - 1, 0), min(h0 + span - 1, hh)
        right = []
        for i in range(3):
            if h0 == 0:
                right.append(jnp.zeros((ch, count * ww), BF))
            right.append(jnp.concatenate([f[low * ch : high * ch] for f in fields[i]], axis=1))
            if h0 + span - 1 > hh:
                right.append(jnp.zeros(((h0 + span - 1 - hh) * ch, count * ww), BF))
        right.append(jnp.zeros((256 - 3 * span * ch, count * ww), BF))
        product = dot_nt(jnp.concatenate(left, axis=0), jnp.concatenate(right, axis=0))
        for k in range(3):
            for j in range(3):
                total = jnp.zeros((ch, 256), F32)
                for h in range(step):
                    r = (k * step + h) * ch
                    total = jnp.where(spot == h + j, product[r : r + ch], total)
                totals[3 * k + j] = totals[3 * k + j] + total
    return totals


def inner_backward_kernel(
    turned_ref, weight_ref, hidden_ref, diff_ref, mat_t_ref, after_ref,
    shifted_ref, total_ref, bias_ref, offset_ref, product_ref,
):
    del after_ref
    inner, rows, ww = hidden_ref.shape
    hh = weight_ref.shape[1]
    _, bias_ref[...], offset_ref[...], product_ref[...] = backward_planes(
        diff_ref, weight_ref, hidden_ref, mat_t_ref, shifted_ref
    )
    fields = [[turned_ref[d + i] for d in range(inner)] for i in range(3)]
    totals = weight_products(shifted_ref, fields, rows // hh, hh, [0.0] * 9)
    for n in range(9):
        total_ref[n] = totals[n]


def edge_backward_kernel(
    turned_ref, halo_ref, weight_ref, hidden_ref, diff_ref, mat_t_ref, total_ref, bias_in_ref, offset_in_ref, product_in_ref,
    packed_ref, a_ref, b_ref, shifted_ref, rows_ref,
):
    planes, rows, ww = turned_ref.shape
    hh = weight_ref.shape[1]
    ch, classes = rows // hh, diff_ref.shape[1] // hh
    values, bias_sum, offset_sum, product = backward_planes(diff_ref, weight_ref, hidden_ref, mat_t_ref, shifted_ref)
    bias_sum, offset_sum = bias_sum + bias_in_ref[...], offset_sum + offset_in_ref[...]
    product = product + product_in_ref[...]
    odd = lax.rem(lax.axis_index("depth"), 2) == 1
    first, last = values[0].astype(F32), values[1].astype(F32)
    a_ref[...] = jnp.where(odd, first, last).astype(BF)
    b_ref[...] = jnp.where(odd, last, first).astype(BF)
    fields = [
        [halo_ref[0], turned_ref[planes - 2]],
        [turned_ref[0], turned_ref[planes - 1]],
        [turned_ref[1], halo_ref[1]],
    ]
    totals = weight_products(shifted_ref, fields, ch, hh, [total_ref[n] for n in range(9)])
    part = over(iota((ch, 256), 1), ch * (STEP + 2))
    for half in range(2):
        rows_ref[half, 27 * ch :] = jnp.zeros((512 - 27 * ch, 128), F32)
        for t in range(27):
            i, j, k = t // 9, t // 3 % 3, t % 3
            value = jnp.where(part == i, totals[3 * k + j], 0.0)
            rows_ref[half, pl.ds(t, ch, stride=27)] = value[:, 128 * half : 128 * half + 128]
    pick = (rest(iota((ch, 128), 1), ch) == iota((ch, 128), 0)).astype(F32).astype(BF)
    sums = sum(dot_nt(pick, part) for half in range(2) for part in split3(rows_ref[half]))
    for q in range(3):
        packed_ref[q * ch : (q + 1) * ch] = sums[:, 128 * q : 128 * q + 128]
    product = product.reshape(classes, hh, rows)
    keep = over(iota((classes, hh, rows), 2), ch) == iota((classes, hh, rows), 1)
    head = jnp.sum(jnp.where(keep, product, 0.0), axis=1)
    by_last = (rest(iota((rows, 128), 0), ch) == rest(iota((rows, 128), 1), 16)).astype(F32).astype(BF)
    head = dot_exact(head, by_last)
    ones = jnp.ones((16, ww), F32).astype(BF)
    bias = jnp.sum(bias_sum.reshape(hh, ch, ww), axis=0)
    bias = jnp.concatenate([bias] * 8, axis=0)
    bias = sum(dot_nt(ones, part) for part in split3(bias))[:classes]
    offset = sum(dot_nt(ones, part) for part in split3(offset_sum))
    by_class = (over(iota((classes * hh, 128), 0), hh) == rest(iota((classes * hh, 128), 1), 16)).astype(F32).astype(BF)
    offset = dot_exact(offset, by_class)[:classes]
    lane, row = iota((8, 128), 1), iota((8, 128), 0)
    small = jnp.where(lane < 112, head, jnp.where(row == 0, bias, offset))
    low, high = sums[:8, 384:], pltpu.roll(sums[8:, 384:], 48, 1)
    packed_ref[3 * ch :] = jnp.where(lane < 48, low, jnp.where(lane < 96, high, small))


def input_kernel(a_ref, b_ref, shifted_ref, edge_ref, band_ref, out_ref, token_ref, turned_ref, grad_ref, sems):
    token_ref[...] = jnp.zeros_like(token_ref)
    ch, planes, hh, ww = grad_ref.shape
    rows = ch * hh
    unit = (iota((rows, rows), 0) == iota((rows, rows), 1)).astype(F32).astype(BF)
    for i in range(3):
        for k in range(3):
            block = band_ref[:, (3 * i + k) * rows : (3 * i + k + 1) * rows]
            col = (3 * (2 - i) + k) * rows
            turned_ref[:, col : col + rows] = dot_nt(unit, block).astype(BF)
    ends = []
    for x in sorted_halo(a_ref[...].astype(F32), b_ref[...].astype(F32)):
        before, after = moved(x)
        ends.append(jnp.concatenate([after, x, before], axis=0))
    field = [ends[0], edge_ref[0]] + [shifted_ref[d] for d in range(planes - 2)] + [edge_ref[1], ends[1]]
    part, copies = planes // 2, []
    for n in range(2):
        own = range(n * part, (n + 1) * part)
        wide = [jnp.concatenate(field[d : d + 3], axis=0) for d in own]
        grad = dot(turned_ref[...], jnp.concatenate(wide, axis=1)).astype(BF)
        for d in own:
            grad_ref[:, d] = grad[:, (d - n * part) * ww : (d - n * part + 1) * ww].reshape(ch, hh, ww)
        span = pl.ds(n * part, part)
        copies.append(pltpu.make_async_copy(grad_ref.at[:, span], out_ref.at[:, span], sems.at[n]))
        copies[-1].start()
    for copy in copies:
        copy.wait()


def unpack_kernel(scale, token_ref, own_ref, *refs):
    del token_ref
    others, (kernel_ref, bias_ref, head_ref, offset_ref) = refs[:-4], refs[-4:]
    ch = kernel_ref.shape[0]
    total = functools.reduce(jnp.add, [r[...] for r in others], own_ref[...]) * scale
    tail = total[3 * ch :]
    tiles = [total[q * ch : (q + 1) * ch] for q in range(3)]
    tiles.append(jnp.concatenate([tail, pltpu.roll(tail, 80, 1)], axis=0))
    lane = iota((ch, 128), 1)
    for co in range(ch):
        q, off = 27 * co // 128, 27 * co % 128
        value = pltpu.roll(tiles[q], 128 - off, 1) if off else tiles[q]
        if off + 27 > 128:
            value = jnp.where(lane < 128 - off, value, pltpu.roll(tiles[q + 1], 128 - off, 1))
        kernel_ref[co] = value[:, 0:27]
    head_ref[...] = pltpu.roll(tail, 32, 1)[:, 0:16]
    biases = pltpu.roll(tail, 16, 1)
    bias_ref[...] = biases[0:1, 0:16]
    offset_ref[...] = biases[1:2, 0:8]


def call(kernel, out_shape, in_spaces, scratch, flops, args, out_spaces=None):
    moved_bytes = sum(a.size * a.dtype.itemsize for a in args)
    return pl.pallas_call(
        kernel,
        out_shape=out_shape,
        in_specs=[pl.BlockSpec(memory_space=s) for s in in_spaces],
        out_specs=jax.tree.map(
            lambda _, s: pl.BlockSpec(memory_space=s), out_shape, out_spaces or jax.tree.map(lambda _: VM, out_shape)
        ),
        scratch_shapes=scratch,
        compiler_params=pltpu.CompilerParams(vmem_limit_bytes=32 << 20),
        cost_estimate=pl.CostEstimate(flops=flops, bytes_accessed=moved_bytes, transcendentals=0),
    )(*args)


def exchange_pairs():
    crops, size = lax.axis_size("dp"), lax.axis_size("depth")
    one, two = [], []
    for c in range(crops):
        for d in range(size):
            one.append((c * size + d, c * size + (d ^ 1)))
            e = ((d + 1) ^ 1) - 1
            if 0 <= e < size:
                two.append((c * size + d, c * size + e))
            elif crops % 2 == 0:
                two.append((c * size + d, (c ^ 1) * size + d))
    return one, two


def exchanged(a, b):
    one, two = exchange_pairs()
    return lax.ppermute(a, ("dp", "depth"), one), lax.ppermute(b, ("dp", "depth"), two)


def reduction_rounds():
    count = lax.axis_size("dp") * lax.axis_size("depth")
    bits = [1 << b for b in range((count - 1).bit_length())]
    bits = bits[-1:] + bits[1:2] + bits[:1] + bits[2:-1] if len(bits) >= 4 else bits
    rounds = []
    for n in range(0, len(bits), 2):
        masks = bits[n : n + 2]
        masks = masks + [sum(masks)] if len(masks) == 2 else masks
        rounds.append([[(i, i ^ m) for i in range(count)] for m in masks])
    return rounds


def body(features, labels, masks, conv_kernel, conv_bias, head_weight, head_bias):
    x, label, mask = features[0, 0], labels[0], masks[0, 0]
    kernel, head = conv_kernel[0], head_weight[0]
    ch, planes, hh, ww = x.shape
    classes = head.shape[0]
    rows = ch * hh
    sds = jax.ShapeDtypeStruct
    size = lax.axis_size("depth")
    pair_flops = 2 * rows * 9 * rows * 2 * ww

    plane = sds((ch, hh, ww), BF)
    inputs = (x, label, mask, kernel.transpose(1, 2, 0), conv_bias, head, head_bias)
    inputs = tuple(pltpu.with_memory_space_constraint(v, pltpu.HBM) for v in inputs)
    shapes = tuple(sds(v.shape, v.dtype) for v in inputs)
    *inputs, end_a, end_b = call(
        load_kernel,
        (*shapes, plane, plane),
        (pltpu.HBM,) * len(inputs),
        [pltpu.SemaphoreType.DMA((len(inputs),))],
        0,
        inputs,
    )
    x, label, mask, kernel, conv_bias, head, head_bias = inputs
    far = exchanged(end_a, end_b)
    inner = planes - 2
    band, mat, mat_t, turn, bias, shifted, turned_x, hidden_in, diff_in, offered_in = call(
        interior_kernel,
        (
            sds((rows, 9 * rows), BF),
            sds((classes * hh, rows), BF),
            sds((rows, classes * hh), BF),
            sds((rows, rows), BF),
            sds((ch, 2 * ww), F32),
            sds((planes, 3 * rows, ww), BF),
            sds((planes, rows, ww), BF),
            sds((inner, rows, ww), BF),
            sds((inner, classes * hh, ww), F32),
            sds((inner, hh, ww), F32),
        ),
        (VM,) * 7,
        [],
        pair_flops * inner // 2,
        (x, label, mask, kernel, conv_bias, head, head_bias),
    )
    peers = [(0, 1), (1, 0)]
    weight_in = lax.ppermute(offered_in, "net", peers)
    halo, hidden_edge, diff_edge, offered_edge = call(
        edge_kernel,
        (
            sds((2, rows, ww), BF),
            sds((2, rows, ww), BF),
            sds((2, classes * hh, ww), F32),
            sds((2, hh, ww), F32),
        ),
        (VM,) * 10,
        [],
        pair_flops,
        (*far, label, mask, head_bias, band, mat, turn, bias, shifted),
    )
    weight_edge = lax.ppermute(offered_edge, "net", peers)
    sums = (
        sds((9, ch, 256), F32),
        sds((rows, ww), F32),
        sds((classes * hh, ww), F32),
        sds((classes * hh, rows), F32),
    )
    grads, *sums = call(
        inner_backward_kernel,
        (sds((inner, 3 * rows, ww), BF), *sums),
        (VM,) * 6,
        [],
        pair_flops * inner // 2,
        (turned_x, weight_in, hidden_in, diff_in, mat_t, halo),
    )
    edge = sds((rows, ww), BF)
    packed, grad_a, grad_b, grad_edge = call(
        edge_backward_kernel,
        (sds((3 * ch + 8, 128), F32), edge, edge, sds((2, 3 * rows, ww), BF)),
        (VM,) * 10,
        [VM((2, 32 * ch, 128), F32)],
        pair_flops,
        (turned_x, halo, weight_edge, hidden_edge, diff_edge, mat_t, *sums),
    )
    rounds, pairs = reduction_rounds(), exchange_pairs()
    for n, masks in enumerate(rounds):
        others = [lax.ppermute(packed, ("dp", "depth"), p) for p in masks]
        if n == 0:
            grad_far = [lax.ppermute(e, ("dp", "depth"), p) for e, p in zip((grad_a, grad_b), pairs)]
        if n < len(rounds) - 1:
            packed = functools.reduce(jnp.add, others, packed)
        if n == len(rounds) - 2:
            packed, band = lax.optimization_barrier((packed, band))
    grad_input, token = call(
        input_kernel,
        (sds((ch, planes, hh, ww), BF), sds((8, 128), F32)),
        (VM,) * 5,
        [VM((rows, 9 * rows), BF), VM((ch, planes, hh, ww), BF), pltpu.SemaphoreType.DMA((2,))],
        pair_flops * planes // 2,
        (*grad_far, grads, grad_edge, band),
        (pltpu.HBM, VM),
    )
    scale = 1.0 / (lax.axis_size("dp") * size * planes * hh * ww)
    grad_kernel, grad_bias, grad_head, grad_offset = call(
        functools.partial(unpack_kernel, scale),
        (sds((ch, ch, 27), F32), sds((1, ch), F32), sds((classes, ch), F32), sds((1, classes), F32)),
        (VM,) * (2 + len(others)),
        [],
        1000,
        (token, packed, *others),
    )
    return (
        grad_input[None, None],
        grad_kernel.transpose(2, 0, 1)[None],
        grad_bias,
        grad_head[None],
        grad_offset,
    )


def solution(mesh):
    in_specs = (
        P("net", "dp", None, "depth", None, None),
        P("dp", "depth", None, None),
        P("net", "dp", "depth", None, None),
        P("net", None, None, None),
        P("net", None),
        P("net", None, None),
        P("net", None),
    )
    out_specs = (
        P("net", "dp", None, "depth", None, None),
        P("net", None, None, None),
        P("net", None),
        P("net", None, None),
        P("net", None),
    )
    return jax.shard_map(body, mesh=mesh, in_specs=in_specs, out_specs=out_specs, check_vma=False)
```

```python
import functools

import jax
import jax.numpy as jnp
from jax import lax
from jax.experimental import pallas as pl
from jax.experimental.pallas import tpu as pltpu
from jax.sharding import PartitionSpec as P

BF = jnp.bfloat16
F32 = jnp.float32
VM = pltpu.VMEM
SM = pltpu.SMEM


def iota(shape, dim):
    return lax.broadcasted_iota(jnp.int32, shape, dim)


def over(x, n):
    return lax.shift_right_logical(x, n.bit_length() - 1) if n & (n - 1) == 0 else x // n


def rest(x, n):
    return lax.bitwise_and(x, n - 1) if n & (n - 1) == 0 else lax.rem(x, n)


def dot(a, b):
    return jnp.dot(a, b, preferred_element_type=F32)


def dot_nt(a, b):
    return lax.dot_general(a, b, (((1,), (1,)), ((), ())), preferred_element_type=F32)


def split(x):
    high = x.astype(BF)
    return high, (x - high.astype(F32)).astype(BF)


def dot_exact(x, ones):
    return sum(dot(part, ones) for part in split(x))


def moved(x):
    y = x.astype(F32)
    lane = iota(y.shape, 1)
    width = y.shape[1]
    before = jnp.where(lane == 0, 0.0, pltpu.roll(y, 1, 1))
    after = jnp.where(lane == width - 1, 0.0, pltpu.roll(y, width - 1, 1))
    return before.astype(BF), after.astype(BF)


def fill_band(kernel_ref, band_ref, ch, hh):
    rows = ch * hh
    unit = (iota((32, 27), 0) == iota((32, 27), 1)).astype(F32).astype(BF)
    by_tap = dot_nt(unit, kernel_ref[...].reshape(ch * ch, 27))
    wide = jnp.broadcast_to(by_tap[:27, None, :], (27, ch, ch * ch))
    wide = jnp.where(over(iota((27, ch, ch * ch), 2), ch) == iota((27, ch, ch * ch), 1), wide, 0.0)
    spread = (over(iota((ch * ch, rows), 1), hh) == rest(iota((ch * ch, rows), 0), ch)).astype(F32).astype(BF)
    wide = dot(wide.reshape(27 * ch, ch * ch).astype(BF), spread).astype(BF)
    masks = [(rest(iota((ch, rows), 1), hh) == h).astype(F32).astype(BF) for h in range(hh)]
    for i in range(3):
        for k in range(3):
            taps = [wide[(9 * i + 3 * j + k) * ch : (9 * i + 3 * j + k + 1) * ch] for j in range(3)]
            col = (3 * i + k) * rows
            for h in range(hh):
                block = masks[h] * taps[1]
                if h > 0:
                    block = block + masks[h - 1] * taps[0]
                if h < hh - 1:
                    block = block + masks[h + 1] * taps[2]
                band_ref[h * ch : (h + 1) * ch, col : col + rows] = block


def head_matrix(head_ref, ch, hh, classes):
    rows = ch * hh
    spread = (rest(iota((ch, rows), 1), ch) == iota((ch, rows), 0)).astype(F32).astype(BF)
    wide = dot(head_ref[...], spread)
    wide = jnp.broadcast_to(wide[:, None, :], (classes, hh, rows))
    keep = over(iota((classes, hh, rows), 2), ch) == iota((classes, hh, rows), 1)
    return jnp.where(keep, wide, 0.0).reshape(classes * hh, rows).astype(BF)


def bias_rows(bias_ref, ch, width):
    square = jnp.broadcast_to(bias_ref[...], (ch, ch))
    column = jnp.sum(jnp.where(iota((ch, ch), 0) == iota((ch, ch), 1), square, 0.0), axis=1, keepdims=True)
    return jnp.broadcast_to(column, (ch, width))


def shifts(x):
    before, after = moved(x)
    return jnp.concatenate([before, x, after], axis=0)


def head_pair(preact, bias, mat, head_bias_ref, label, mask, dims):
    ch, hh, ww, classes = dims
    rows = ch * hh
    preact = (preact.reshape(hh, ch, 2 * ww) + bias[None]).reshape(rows, 2 * ww)
    hidden = jnp.maximum(preact, 0.0).astype(BF)
    logits = dot(mat, hidden).reshape(classes, hh, 2 * ww)
    parts = [logits[c] + head_bias_ref[0:1, c : c + 1] for c in range(classes)]
    total = functools.reduce(jnp.add, [jnp.exp(p) for p in parts])
    log_total = jnp.log(total)
    soft = [jnp.exp(p - log_total) for p in parts]
    hot = [label == c for c in range(classes)]
    chosen = functools.reduce(jnp.add, [jnp.where(o, s, 0.0) for o, s in zip(hot, soft)])
    diffs = [s - jnp.where(o, 1.0, 0.0) for o, s in zip(hot, soft)]
    return hidden, jnp.stack(diffs).reshape(classes * hh, 2 * ww), mask * chosen


def put_pair(ref, first, second, value, ww):
    ref[first] = value[:, :ww]
    ref[second] = value[:, ww:]


def beside(ref, first, second):
    return jnp.concatenate([ref[first], ref[second]], axis=1)


def load_kernel(*refs):
    count = (len(refs) - 3) // 2
    sources, targets, (a_ref, b_ref, sems) = refs[:count], refs[count : 2 * count], refs[2 * count :]
    planes = sources[0].shape[1]
    copies = [pltpu.make_async_copy(s, t, sems.at[n]) for n, (s, t) in enumerate(zip(sources, targets))]
    for copy in copies:
        copy.start()
    copies[0].wait()
    odd = lax.rem(lax.axis_index("depth"), 2)
    a_ref[...] = targets[0][:, (1 - odd) * (planes - 1)]
    b_ref[...] = targets[0][:, odd * (planes - 1)]
    for copy in copies[1:]:
        copy.wait()


def sorted_halo(a, b):
    place, size = lax.axis_index("depth"), lax.axis_size("depth")
    odd = lax.rem(place, 2) == 1
    before, after = jnp.where(odd, a, b), jnp.where(odd, b, a)
    before = jnp.where(place > 0, before, 0.0)
    after = jnp.where(place < size - 1, after, 0.0)
    return before.astype(BF), after.astype(BF)


def turner(ch, hh):
    rows = ch * hh
    row, col = iota((rows, rows), 0), iota((rows, rows), 1)
    return ((over(row, ch) == rest(col, hh)) & (rest(row, ch) == over(col, hh))).astype(F32).astype(BF)


def interior_kernel(
    x_ref, label_ref, mask_ref, kernel_ref, bias_ref, head_ref, head_bias_ref,
    band_ref, mat_ref, mat_t_ref, turner_ref, bias_out_ref,
    shifted_ref, turned_ref, hidden_ref, diff_ref, offered_ref,
):
    ch, planes, hh, ww = x_ref.shape
    classes = head_ref.shape[0]
    rows = ch * hh
    inner = planes - 2
    fill_band(kernel_ref, band_ref, ch, hh)
    mat = head_matrix(head_ref, ch, hh, classes)
    bias = bias_rows(bias_ref, ch, 2 * ww)
    field = [x_ref[:, d].reshape(rows, ww) for d in range(planes)]
    for d in range(planes):
        shifted_ref[d] = shifts(field[d])
    wide = [shifted_ref[d : d + 3].reshape(9 * rows, ww) for d in range(inner)]
    preact = dot(band_ref[...], jnp.concatenate(wide, axis=1))
    for d in range(0, inner, 2):
        hidden, diff, offered = head_pair(
            preact[:, d * ww : (d + 2) * ww], bias, mat, head_bias_ref, beside(label_ref, d + 1, d + 2),
            beside(mask_ref, d + 1, d + 2).astype(F32), (ch, hh, ww, classes),
        )
        put_pair(hidden_ref, d, d + 1, hidden, ww)
        put_pair(diff_ref, d, d + 1, diff, ww)
        put_pair(offered_ref, d, d + 1, offered, ww)
    turn = turner(ch, hh)
    turned = dot(turn, jnp.concatenate(field, axis=1)).astype(BF)
    for d in range(planes):
        turned_ref[d] = turned[:, d * ww : (d + 1) * ww]
    unit = (iota((rows, rows), 0) == iota((rows, rows), 1)).astype(F32).astype(BF)
    mat_ref[...], mat_t_ref[...], turner_ref[...], bias_out_ref[...] = mat, dot_nt(unit, mat).astype(BF), turn, bias


def edge_kernel(
    a_ref, b_ref, label_ref, mask_ref, head_bias_ref, band_ref, mat_ref, bias_ref, shifted_ref,
    halo_ref, hidden_ref, diff_ref, offered_ref,
):
    ch, hh, ww = a_ref.shape
    planes, classes = label_ref.shape[0], mat_ref.shape[0] // hh
    rows = ch * hh
    before, after = sorted_halo(a_ref[...].reshape(rows, ww).astype(F32), b_ref[...].reshape(rows, ww).astype(F32))
    left = jnp.concatenate([shifts(before), shifted_ref[0:2].reshape(6 * rows, ww)], axis=0)
    right = jnp.concatenate([shifted_ref[planes - 2 : planes].reshape(6 * rows, ww), shifts(after)], axis=0)
    preact = dot(band_ref[...], jnp.concatenate([left, right], axis=1))
    hidden, diff, offered = head_pair(
        preact, bias_ref[...], mat_ref[...], head_bias_ref, beside(label_ref, 0, planes - 1),
        beside(mask_ref, 0, planes - 1).astype(F32), (ch, hh, ww, classes),
    )
    put_pair(hidden_ref, 0, 1, hidden, ww)
    put_pair(diff_ref, 0, 1, diff, ww)
    put_pair(offered_ref, 0, 1, offered, ww)
    halo_ref[0], halo_ref[1] = before, after


def backward_planes(diff_ref, weight_ref, hidden_ref, mat_t_ref, shifted_ref):
    count, rows, ww = hidden_ref.shape
    hh = weight_ref.shape[1]
    classes = diff_ref.shape[1] // hh
    offset_sum, halves = 0.0, []
    for d in range(count):
        grad = (diff_ref[d].reshape(classes, hh, ww) * weight_ref[d][None]).reshape(classes * hh, ww)
        offset_sum = offset_sum + grad
        halves.append(grad.astype(BF))
    halves = jnp.concatenate(halves, axis=1)
    hiddens = jnp.concatenate([hidden_ref[d] for d in range(count)], axis=1)
    pre = jnp.where(hiddens.astype(F32) > 0.0, dot(mat_t_ref[...], halves), 0.0)
    bias_sum = sum(pre[:, d * ww : (d + 1) * ww] for d in range(count))
    values = [pre[:, d * ww : (d + 1) * ww].astype(BF) for d in range(count)]
    for d in range(count):
        before, after = moved(values[d])
        shifted_ref[d] = jnp.concatenate([after, values[d], before], axis=0)
    return values, bias_sum, offset_sum, dot_nt(halves, hiddens)


STEP = 3


def weight_products(shifted_ref, fields, ch, hh, totals):
    count, rows3, ww = shifted_ref.shape
    rows = rows3 // 3
    span = STEP + 2
    spot = rest(over(iota((ch, 256), 1), ch), span)
    grads = [shifted_ref[d] for d in range(count)]
    for h0 in range(0, hh, STEP):
        step = min(STEP, hh - h0)
        left = [g[k * rows + h0 * ch : k * rows + (h0 + step) * ch] for k in range(3) for g in grads]
        left = [jnp.concatenate(left[k * count : (k + 1) * count], axis=1) for k in range(3)]
        low, high = max(h0 - 1, 0), min(h0 + span - 1, hh)
        right = []
        for i in range(3):
            if h0 == 0:
                right.append(jnp.zeros((ch, count * ww), BF))
            right.append(jnp.concatenate([f[low * ch : high * ch] for f in fields[i]], axis=1))
            if h0 + span - 1 > hh:
                right.append(jnp.zeros(((h0 + span - 1 - hh) * ch, count * ww), BF))
        right.append(jnp.zeros((256 - 3 * span * ch, count * ww), BF))
        product = dot_nt(jnp.concatenate(left, axis=0), jnp.concatenate(right, axis=0))
        for k in range(3):
            for j in range(3):
                total = jnp.zeros((ch, 256), F32)
                for h in range(step):
                    r = (k * step + h) * ch
                    total = jnp.where(spot == h + j, product[r : r + ch], total)
                totals[3 * k + j] = totals[3 * k + j] + total
    return totals


def inner_backward_kernel(
    turned_ref, weight_ref, hidden_ref, diff_ref, mat_t_ref, halo_ref, turner_ref,
    shifted_ref, total_ref, bias_ref, offset_ref, product_ref, halo_turned_ref,
):
    inner, rows, ww = hidden_ref.shape
    put_pair(halo_turned_ref, 0, 1, dot(turner_ref[...], beside(halo_ref, 0, 1)).astype(BF), ww)
    hh = weight_ref.shape[1]
    _, bias_ref[...], offset_ref[...], product_ref[...] = backward_planes(
        diff_ref, weight_ref, hidden_ref, mat_t_ref, shifted_ref
    )
    fields = [[turned_ref[d + i] for d in range(inner)] for i in range(3)]
    totals = weight_products(shifted_ref, fields, rows // hh, hh, [0.0] * 9)
    for n in range(9):
        total_ref[n] = totals[n]


def edge_backward_kernel(
    turned_ref, halo_ref, weight_ref, hidden_ref, diff_ref, mat_t_ref, total_ref, bias_in_ref, offset_in_ref, product_in_ref,
    packed_ref, a_ref, b_ref, shifted_ref, rows_ref,
):
    planes, rows, ww = turned_ref.shape
    hh = weight_ref.shape[1]
    ch, classes = rows // hh, diff_ref.shape[1] // hh
    values, bias_sum, offset_sum, product = backward_planes(diff_ref, weight_ref, hidden_ref, mat_t_ref, shifted_ref)
    bias_sum, offset_sum = bias_sum + bias_in_ref[...], offset_sum + offset_in_ref[...]
    product = product + product_in_ref[...]
    product = product.reshape(classes, hh, rows)
    keep = over(iota((classes, hh, rows), 2), ch) == iota((classes, hh, rows), 1)
    head = jnp.sum(jnp.where(keep, product, 0.0), axis=1)
    by_last = (rest(iota((rows, 128), 0), ch) == rest(iota((rows, 128), 1), 16)).astype(F32).astype(BF)
    head = dot_exact(head, by_last)
    bias = jnp.sum(jnp.sum(bias_sum.reshape(hh, ch, ww), axis=0), axis=1, keepdims=True)
    offset = jnp.sum(jnp.sum(offset_sum.reshape(classes, hh, ww), axis=1), axis=1, keepdims=True)
    odd = lax.rem(lax.axis_index("depth"), 2) == 1
    first, last = values[0].astype(F32), values[1].astype(F32)
    a_ref[...] = jnp.where(odd, first, last).astype(BF)
    b_ref[...] = jnp.where(odd, last, first).astype(BF)
    fields = [
        [halo_ref[0], turned_ref[planes - 2]],
        [turned_ref[0], turned_ref[planes - 1]],
        [turned_ref[1], halo_ref[1]],
    ]
    totals = weight_products(shifted_ref, fields, ch, hh, [total_ref[n] for n in range(9)])
    part = over(iota((ch, 256), 1), ch * (STEP + 2))
    for half in range(2):
        rows_ref[half, 27 * ch :] = jnp.zeros((512 - 27 * ch, 128), F32)
        for t in range(27):
            i, j, k = t // 9, t // 3 % 3, t % 3
            value = jnp.where(part == i, totals[3 * k + j], 0.0)
            rows_ref[half, pl.ds(t, ch, stride=27)] = value[:, 128 * half : 128 * half + 128]
    pick = (rest(iota((ch, 256), 1), ch) == iota((ch, 256), 0)).astype(F32).astype(BF)
    sums = sum(dot_nt(pick, part) for part in split(jnp.concatenate([rows_ref[0], rows_ref[1]], axis=1)))
    for q in range(3):
        packed_ref[q * ch : (q + 1) * ch] = sums[:, 128 * q : 128 * q + 128]
    lane = iota((8, 128), 1)
    small = jnp.where(lane < 112, head, jnp.where(lane == 112, bias[:8], jnp.where(lane == 113, bias[8:], offset)))
    low, high = sums[:8, 384:], pltpu.roll(sums[8:, 384:], 48, 1)
    packed_ref[3 * ch :] = jnp.where(lane < 48, low, jnp.where(lane < 96, high, small))


def input_kernel(a_ref, b_ref, shifted_ref, edge_ref, band_ref, out_ref, token_ref, turned_ref, grad_ref, sems):
    token_ref[...] = jnp.zeros_like(token_ref)
    ch, planes, hh, ww = grad_ref.shape
    rows = ch * hh
    unit = (iota((rows, rows), 0) == iota((rows, rows), 1)).astype(F32).astype(BF)
    for i in range(3):
        for k in range(3):
            block = band_ref[:, (3 * i + k) * rows : (3 * i + k + 1) * rows]
            col = (3 * (2 - i) + k) * rows
            turned_ref[:, col : col + rows] = dot_nt(unit, block).astype(BF)
    ends = []
    for x in sorted_halo(a_ref[...].astype(F32), b_ref[...].astype(F32)):
        before, after = moved(x)
        ends.append(jnp.concatenate([after, x, before], axis=0))
    field = [ends[0], edge_ref[0]] + [shifted_ref[d] for d in range(planes - 2)] + [edge_ref[1], ends[1]]
    part, copies = planes // 2, []
    for n in range(2):
        own = range(n * part, (n + 1) * part)
        wide = [jnp.concatenate(field[d : d + 3], axis=0) for d in own]
        grad = dot(turned_ref[...], jnp.concatenate(wide, axis=1)).astype(BF)
        for d in own:
            grad_ref[:, d] = grad[:, (d - n * part) * ww : (d - n * part + 1) * ww].reshape(ch, hh, ww)
        span = pl.ds(n * part, part)
        copies.append(pltpu.make_async_copy(grad_ref.at[:, span], out_ref.at[:, span], sems.at[n]))
        copies[-1].start()
    for copy in copies:
        copy.wait()


def unpack_kernel(scale, token_ref, own_ref, *refs):
    del token_ref
    others, (kernel_ref, bias_ref, head_ref, offset_ref) = refs[:-4], refs[-4:]
    ch = kernel_ref.shape[0]
    total = functools.reduce(jnp.add, [r[...] for r in others], own_ref[...]) * scale
    tail = total[3 * ch :]
    tiles = [total[q * ch : (q + 1) * ch] for q in range(3)]
    tiles.append(jnp.concatenate([tail, pltpu.roll(tail, 80, 1)], axis=0))
    lane = iota((ch, 128), 1)
    for co in range(ch):
        q, off = 27 * co // 128, 27 * co % 128
        value = pltpu.roll(tiles[q], 128 - off, 1) if off else tiles[q]
        if off + 27 > 128:
            value = jnp.where(lane < 128 - off, value, pltpu.roll(tiles[q + 1], 128 - off, 1))
        kernel_ref[co] = value[:, 0:27]
    head_ref[...] = pltpu.roll(tail, 32, 1)[:, 0:16]
    column, row = iota((8, ch), 1), iota((8, ch), 0)
    low = jnp.where(column == row, tail[:, 112:113], 0.0) + jnp.where(column == row + 8, tail[:, 113:114], 0.0)
    bias_ref[...] = jnp.sum(low, axis=0, keepdims=True)
    diagonal = jnp.where(column[:, :8] == row[:, :8], tail[:, 114:115], 0.0)
    offset_ref[...] = jnp.sum(diagonal, axis=0, keepdims=True)


def call(kernel, out_shape, in_spaces, scratch, flops, args, out_spaces=None):
    moved_bytes = sum(a.size * a.dtype.itemsize for a in args)
    return pl.pallas_call(
        kernel,
        out_shape=out_shape,
        in_specs=[pl.BlockSpec(memory_space=s) for s in in_spaces],
        out_specs=jax.tree.map(
            lambda _, s: pl.BlockSpec(memory_space=s), out_shape, out_spaces or jax.tree.map(lambda _: VM, out_shape)
        ),
        scratch_shapes=scratch,
        compiler_params=pltpu.CompilerParams(vmem_limit_bytes=32 << 20),
        cost_estimate=pl.CostEstimate(flops=flops, bytes_accessed=moved_bytes, transcendentals=0),
    )(*args)


def exchange_pairs():
    crops, size = lax.axis_size("dp"), lax.axis_size("depth")
    one, two = [], []
    for c in range(crops):
        for d in range(size):
            one.append((c * size + d, c * size + (d ^ 1)))
            e = ((d + 1) ^ 1) - 1
            if 0 <= e < size:
                two.append((c * size + d, c * size + e))
            elif crops % 2 == 0:
                two.append((c * size + d, (c ^ 1) * size + d))
    return one, two


def exchanged(a, b):
    one, two = exchange_pairs()
    return lax.ppermute(a, ("dp", "depth"), one), lax.ppermute(b, ("dp", "depth"), two)


def reduction_rounds():
    count = lax.axis_size("dp") * lax.axis_size("depth")
    bits = [1 << b for b in range((count - 1).bit_length())]
    bits = bits[-1:] + bits[1:2] + bits[:1] + bits[2:-1] if len(bits) >= 4 else bits
    rounds = []
    for n in range(0, len(bits), 2):
        masks = bits[n : n + 2]
        masks = masks + [sum(masks)] if len(masks) == 2 else masks
        rounds.append([[(i, i ^ m) for i in range(count)] for m in masks])
    return rounds


def body(features, labels, masks, conv_kernel, conv_bias, head_weight, head_bias):
    x, label, mask = features[0, 0], labels[0], masks[0, 0]
    kernel, head = conv_kernel[0], head_weight[0]
    ch, planes, hh, ww = x.shape
    classes = head.shape[0]
    rows = ch * hh
    sds = jax.ShapeDtypeStruct
    size = lax.axis_size("depth")
    pair_flops = 2 * rows * 9 * rows * 2 * ww

    plane = sds((ch, hh, ww), BF)
    inputs = (x, label, mask, kernel.transpose(1, 2, 0), conv_bias, head, head_bias)
    inputs = tuple(pltpu.with_memory_space_constraint(v, pltpu.HBM) for v in inputs)
    shapes = tuple(sds(v.shape, v.dtype) for v in inputs)
    *inputs, end_a, end_b = call(
        load_kernel,
        (*shapes, plane, plane),
        (pltpu.HBM,) * len(inputs),
        [pltpu.SemaphoreType.DMA((len(inputs),))],
        0,
        inputs,
    )
    x, label, mask, kernel, conv_bias, head, head_bias = inputs
    far = exchanged(end_a, end_b)
    inner = planes - 2
    band, mat, mat_t, turn, bias, shifted, turned_x, hidden_in, diff_in, offered_in = call(
        interior_kernel,
        (
            sds((rows, 9 * rows), BF),
            sds((classes * hh, rows), BF),
            sds((rows, classes * hh), BF),
            sds((rows, rows), BF),
            sds((ch, 2 * ww), F32),
            sds((planes, 3 * rows, ww), BF),
            sds((planes, rows, ww), BF),
            sds((inner, rows, ww), BF),
            sds((inner, classes * hh, ww), F32),
            sds((inner, hh, ww), F32),
        ),
        (VM,) * 7,
        [],
        pair_flops * inner // 2,
        (x, label, mask, kernel, conv_bias, head, head_bias),
    )
    peers = [(0, 1), (1, 0)]
    weight_in = lax.ppermute(offered_in, "net", peers)
    halo, hidden_edge, diff_edge, offered_edge = call(
        edge_kernel,
        (
            sds((2, rows, ww), BF),
            sds((2, rows, ww), BF),
            sds((2, classes * hh, ww), F32),
            sds((2, hh, ww), F32),
        ),
        (VM,) * 9,
        [],
        pair_flops,
        (*far, label, mask, head_bias, band, mat, bias, shifted),
    )
    weight_edge = lax.ppermute(offered_edge, "net", peers)
    sums = (
        sds((9, ch, 256), F32),
        sds((rows, ww), F32),
        sds((classes * hh, ww), F32),
        sds((classes * hh, rows), F32),
    )
    grads, *sums, halo = call(
        inner_backward_kernel,
        (sds((inner, 3 * rows, ww), BF), *sums, sds((2, rows, ww), BF)),
        (VM,) * 7,
        [],
        pair_flops * inner // 2,
        (turned_x, weight_in, hidden_in, diff_in, mat_t, halo, turn),
    )
    edge = sds((rows, ww), BF)
    packed, grad_a, grad_b, grad_edge = call(
        edge_backward_kernel,
        (sds((3 * ch + 8, 128), F32), edge, edge, sds((2, 3 * rows, ww), BF)),
        (VM,) * 10,
        [VM((2, 32 * ch, 128), F32)],
        pair_flops,
        (turned_x, halo, weight_edge, hidden_edge, diff_edge, mat_t, *sums),
    )
    rounds, pairs = reduction_rounds(), exchange_pairs()
    for n, masks in enumerate(rounds):
        others = [lax.ppermute(packed, ("dp", "depth"), p) for p in masks]
        if n == 0:
            grad_far = [lax.ppermute(e, ("dp", "depth"), p) for e, p in zip((grad_a, grad_b), pairs)]
        if n < len(rounds) - 1:
            packed = functools.reduce(jnp.add, others, packed)
        if n == len(rounds) - 2:
            packed, band = lax.optimization_barrier((packed, band))
    grad_input, token = call(
        input_kernel,
        (sds((ch, planes, hh, ww), BF), sds((8, 128), F32)),
        (VM,) * 5,
        [VM((rows, 9 * rows), BF), VM((ch, planes, hh, ww), BF), pltpu.SemaphoreType.DMA((2,))],
        pair_flops * planes // 2,
        (*grad_far, grads, grad_edge, band),
        (pltpu.HBM, VM),
    )
    scale = 1.0 / (lax.axis_size("dp") * size * planes * hh * ww)
    grad_kernel, grad_bias, grad_head, grad_offset = call(
        functools.partial(unpack_kernel, scale),
        (sds((ch, ch, 27), F32), sds((1, ch), F32), sds((classes, ch), F32), sds((1, classes), F32)),
        (VM,) * (2 + len(others)),
        [],
        1000,
        (token, packed, *others),
    )
    return (
        grad_input[None, None],
        grad_kernel.transpose(2, 0, 1)[None],
        grad_bias,
        grad_head[None],
        grad_offset,
    )


def solution(mesh):
    in_specs = (
        P("net", "dp", None, "depth", None, None),
        P("dp", "depth", None, None),
        P("net", "dp", "depth", None, None),
        P("net", None, None, None),
        P("net", None),
        P("net", None, None),
        P("net", None),
    )
    out_specs = (
        P("net", "dp", None, "depth", None, None),
        P("net", None, None, None),
        P("net", None),
        P("net", None, None),
        P("net", None),
    )
    return jax.shard_map(body, mesh=mesh, in_specs=in_specs, out_specs=out_specs, check_vma=False)
```

```python
import functools

import jax
import jax.numpy as jnp
from jax import lax
from jax.experimental import pallas as pl
from jax.experimental.pallas import tpu as pltpu
from jax.sharding import PartitionSpec as P

BF = jnp.bfloat16
F32 = jnp.float32
VM = pltpu.VMEM
SM = pltpu.SMEM


def iota(shape, dim):
    return lax.broadcasted_iota(jnp.int32, shape, dim)


def over(x, n):
    return lax.shift_right_logical(x, n.bit_length() - 1) if n & (n - 1) == 0 else x // n


def rest(x, n):
    return lax.bitwise_and(x, n - 1) if n & (n - 1) == 0 else lax.rem(x, n)


def dot(a, b):
    return jnp.dot(a, b, preferred_element_type=F32)


def dot_nt(a, b):
    return lax.dot_general(a, b, (((1,), (1,)), ((), ())), preferred_element_type=F32)


def split(x):
    high = x.astype(BF)
    return high, (x - high.astype(F32)).astype(BF)


def dot_exact(x, ones):
    return sum(dot(part, ones) for part in split(x))


def moved(x):
    y = x.astype(F32)
    lane = iota(y.shape, 1)
    width = y.shape[1]
    before = jnp.where(lane == 0, 0.0, pltpu.roll(y, 1, 1))
    after = jnp.where(lane == width - 1, 0.0, pltpu.roll(y, width - 1, 1))
    return before.astype(BF), after.astype(BF)


def fill_band(kernel_ref, band_ref, ch, hh):
    rows = ch * hh
    unit = (iota((32, 27), 0) == iota((32, 27), 1)).astype(F32).astype(BF)
    by_tap = dot_nt(unit, kernel_ref[...].reshape(ch * ch, 27))
    wide = jnp.broadcast_to(by_tap[:27, None, :], (27, ch, ch * ch))
    wide = jnp.where(over(iota((27, ch, ch * ch), 2), ch) == iota((27, ch, ch * ch), 1), wide, 0.0)
    spread = (over(iota((ch * ch, rows), 1), hh) == rest(iota((ch * ch, rows), 0), ch)).astype(F32).astype(BF)
    wide = dot(wide.reshape(27 * ch, ch * ch).astype(BF), spread).astype(BF)
    masks = [(rest(iota((ch, rows), 1), hh) == h).astype(F32).astype(BF) for h in range(hh)]
    for i in range(3):
        for k in range(3):
            taps = [wide[(9 * i + 3 * j + k) * ch : (9 * i + 3 * j + k + 1) * ch] for j in range(3)]
            col = (3 * i + k) * rows
            for h in range(hh):
                block = masks[h] * taps[1]
                if h > 0:
                    block = block + masks[h - 1] * taps[0]
                if h < hh - 1:
                    block = block + masks[h + 1] * taps[2]
                band_ref[h * ch : (h + 1) * ch, col : col + rows] = block


def head_matrix(head_ref, ch, hh, classes):
    rows = ch * hh
    spread = (rest(iota((ch, rows), 1), ch) == iota((ch, rows), 0)).astype(F32).astype(BF)
    wide = dot(head_ref[...], spread)
    wide = jnp.broadcast_to(wide[:, None, :], (classes, hh, rows))
    keep = over(iota((classes, hh, rows), 2), ch) == iota((classes, hh, rows), 1)
    return jnp.where(keep, wide, 0.0).reshape(classes * hh, rows).astype(BF)


def bias_rows(bias_ref, ch, width):
    square = jnp.broadcast_to(bias_ref[...], (ch, ch))
    column = jnp.sum(jnp.where(iota((ch, ch), 0) == iota((ch, ch), 1), square, 0.0), axis=1, keepdims=True)
    return jnp.broadcast_to(column, (ch, width))


def shifts(x):
    before, after = moved(x)
    return jnp.concatenate([before, x, after], axis=0)


def head_pair(preact, bias, mat, head_bias_ref, label, mask, dims):
    ch, hh, ww, classes = dims
    rows = ch * hh
    preact = (preact.reshape(hh, ch, 2 * ww) + bias[None]).reshape(rows, 2 * ww)
    hidden = jnp.maximum(preact, 0.0).astype(BF)
    logits = dot(mat, hidden).reshape(classes, hh, 2 * ww)
    parts = [logits[c] + head_bias_ref[0:1, c : c + 1] for c in range(classes)]
    total = functools.reduce(jnp.add, [jnp.exp(p) for p in parts])
    log_total = jnp.log(total)
    soft = [jnp.exp(p - log_total) for p in parts]
    hot = [label == c for c in range(classes)]
    chosen = functools.reduce(jnp.add, [jnp.where(o, s, 0.0) for o, s in zip(hot, soft)])
    diffs = [s - jnp.where(o, 1.0, 0.0) for o, s in zip(hot, soft)]
    return hidden, jnp.stack(diffs).reshape(classes * hh, 2 * ww), mask * chosen


def put_pair(ref, first, second, value, ww):
    ref[first] = value[:, :ww]
    ref[second] = value[:, ww:]


def beside(ref, first, second):
    return jnp.concatenate([ref[first], ref[second]], axis=1)


def load_kernel(*refs):
    count = (len(refs) - 3) // 2
    sources, targets, (a_ref, b_ref, sems) = refs[:count], refs[count : 2 * count], refs[2 * count :]
    planes = sources[0].shape[1]
    copies = [pltpu.make_async_copy(s, t, sems.at[n]) for n, (s, t) in enumerate(zip(sources, targets))]
    for copy in copies:
        copy.start()
    copies[0].wait()
    odd = lax.rem(lax.axis_index("depth"), 2)
    a_ref[...] = targets[0][:, (1 - odd) * (planes - 1)]
    b_ref[...] = targets[0][:, odd * (planes - 1)]
    for copy in copies[1:]:
        copy.wait()


def sorted_halo(a, b):
    place, size = lax.axis_index("depth"), lax.axis_size("depth")
    odd = lax.rem(place, 2) == 1
    before, after = jnp.where(odd, a, b), jnp.where(odd, b, a)
    before = jnp.where(place > 0, before, 0.0)
    after = jnp.where(place < size - 1, after, 0.0)
    return before.astype(BF), after.astype(BF)


def turner(ch, hh):
    rows = ch * hh
    row, col = iota((rows, rows), 0), iota((rows, rows), 1)
    return ((over(row, ch) == rest(col, hh)) & (rest(row, ch) == over(col, hh))).astype(F32).astype(BF)


def interior_kernel(
    x_ref, label_ref, mask_ref, kernel_ref, bias_ref, head_ref, head_bias_ref,
    band_ref, mat_ref, mat_t_ref, turner_ref, bias_out_ref,
    shifted_ref, turned_ref, hidden_ref, diff_ref, offered_ref,
):
    ch, planes, hh, ww = x_ref.shape
    classes = head_ref.shape[0]
    rows = ch * hh
    inner = planes - 2
    fill_band(kernel_ref, band_ref, ch, hh)
    mat = head_matrix(head_ref, ch, hh, classes)
    bias = bias_rows(bias_ref, ch, 2 * ww)
    field = [x_ref[:, d].reshape(rows, ww) for d in range(planes)]
    for d in range(planes):
        shifted_ref[d] = shifts(field[d])
    wide = [shifted_ref[d : d + 3].reshape(9 * rows, ww) for d in range(inner)]
    preact = dot(band_ref[...], jnp.concatenate(wide, axis=1))
    for d in range(0, inner, 2):
        hidden, diff, offered = head_pair(
            preact[:, d * ww : (d + 2) * ww], bias, mat, head_bias_ref, beside(label_ref, d + 1, d + 2),
            beside(mask_ref, d + 1, d + 2).astype(F32), (ch, hh, ww, classes),
        )
        put_pair(hidden_ref, d, d + 1, hidden, ww)
        put_pair(diff_ref, d, d + 1, diff, ww)
        put_pair(offered_ref, d, d + 1, offered, ww)
    turn = turner(ch, hh)
    turned = dot(turn, jnp.concatenate(field, axis=1)).astype(BF)
    for d in range(planes):
        turned_ref[d] = turned[:, d * ww : (d + 1) * ww]
    unit = (iota((rows, rows), 0) == iota((rows, rows), 1)).astype(F32).astype(BF)
    mat_ref[...], mat_t_ref[...], turner_ref[...], bias_out_ref[...] = mat, dot_nt(unit, mat).astype(BF), turn, bias


def edge_kernel(
    a_ref, b_ref, label_ref, mask_ref, head_bias_ref, band_ref, mat_ref, bias_ref, shifted_ref,
    halo_ref, hidden_ref, diff_ref, offered_ref,
):
    ch, hh, ww = a_ref.shape
    planes, classes = label_ref.shape[0], mat_ref.shape[0] // hh
    rows = ch * hh
    before, after = sorted_halo(a_ref[...].reshape(rows, ww).astype(F32), b_ref[...].reshape(rows, ww).astype(F32))
    left = jnp.concatenate([shifts(before), shifted_ref[0:2].reshape(6 * rows, ww)], axis=0)
    right = jnp.concatenate([shifted_ref[planes - 2 : planes].reshape(6 * rows, ww), shifts(after)], axis=0)
    preact = dot(band_ref[...], jnp.concatenate([left, right], axis=1))
    hidden, diff, offered = head_pair(
        preact, bias_ref[...], mat_ref[...], head_bias_ref, beside(label_ref, 0, planes - 1),
        beside(mask_ref, 0, planes - 1).astype(F32), (ch, hh, ww, classes),
    )
    put_pair(hidden_ref, 0, 1, hidden, ww)
    put_pair(diff_ref, 0, 1, diff, ww)
    put_pair(offered_ref, 0, 1, offered, ww)
    halo_ref[0], halo_ref[1] = before, after


def backward_planes(diff_ref, weight_ref, hidden_ref, mat_t_ref, shifted_ref):
    count, rows, ww = hidden_ref.shape
    hh = weight_ref.shape[1]
    classes = diff_ref.shape[1] // hh
    offset_sum, halves = 0.0, []
    for d in range(count):
        grad = (diff_ref[d].reshape(classes, hh, ww) * weight_ref[d][None]).reshape(classes * hh, ww)
        offset_sum = offset_sum + grad
        halves.append(grad.astype(BF))
    halves = jnp.concatenate(halves, axis=1)
    hiddens = jnp.concatenate([hidden_ref[d] for d in range(count)], axis=1)
    pre = jnp.where(hiddens.astype(F32) > 0.0, dot(mat_t_ref[...], halves), 0.0)
    bias_sum = sum(pre[:, d * ww : (d + 1) * ww] for d in range(count))
    values = [pre[:, d * ww : (d + 1) * ww].astype(BF) for d in range(count)]
    for d in range(count):
        before, after = moved(values[d])
        shifted_ref[d] = jnp.concatenate([after, values[d], before], axis=0)
    return values, bias_sum, offset_sum, dot_nt(halves, hiddens)


STEP = 3


def weight_products(shifted_ref, fields, ch, hh, totals):
    count, rows3, ww = shifted_ref.shape
    rows = rows3 // 3
    span = STEP + 2
    spot = rest(over(iota((ch, 256), 1), ch), span)
    grads = [shifted_ref[d] for d in range(count)]
    for h0 in range(0, hh, STEP):
        step = min(STEP, hh - h0)
        left = [g[k * rows + h0 * ch : k * rows + (h0 + step) * ch] for k in range(3) for g in grads]
        left = [jnp.concatenate(left[k * count : (k + 1) * count], axis=1) for k in range(3)]
        low, high = max(h0 - 1, 0), min(h0 + span - 1, hh)
        right = []
        for i in range(3):
            if h0 == 0:
                right.append(jnp.zeros((ch, count * ww), BF))
            right.append(jnp.concatenate([f[low * ch : high * ch] for f in fields[i]], axis=1))
            if h0 + span - 1 > hh:
                right.append(jnp.zeros(((h0 + span - 1 - hh) * ch, count * ww), BF))
        right.append(jnp.zeros((256 - 3 * span * ch, count * ww), BF))
        product = dot_nt(jnp.concatenate(left, axis=0), jnp.concatenate(right, axis=0))
        for k in range(3):
            for j in range(3):
                total = jnp.zeros((ch, 256), F32)
                for h in range(step):
                    r = (k * step + h) * ch
                    total = jnp.where(spot == h + j, product[r : r + ch], total)
                totals[3 * k + j] = totals[3 * k + j] + total
    return totals


def inner_backward_kernel(
    turned_ref, weight_ref, hidden_ref, diff_ref, mat_t_ref, halo_ref, turner_ref,
    shifted_ref, total_ref, bias_ref, offset_ref, product_ref, halo_turned_ref,
):
    inner, rows, ww = hidden_ref.shape
    put_pair(halo_turned_ref, 0, 1, dot(turner_ref[...], beside(halo_ref, 0, 1)).astype(BF), ww)
    hh = weight_ref.shape[1]
    _, bias_ref[...], offset_ref[...], product_ref[...] = backward_planes(
        diff_ref, weight_ref, hidden_ref, mat_t_ref, shifted_ref
    )
    fields = [[turned_ref[d + i] for d in range(inner)] for i in range(3)]
    totals = weight_products(shifted_ref, fields, rows // hh, hh, [0.0] * 9)
    for n in range(9):
        total_ref[n] = totals[n]


def edge_backward_kernel(
    turned_ref, halo_ref, weight_ref, hidden_ref, diff_ref, mat_t_ref, total_ref, bias_in_ref, offset_in_ref, product_in_ref,
    packed_ref, a_ref, b_ref, shifted_ref, rows_ref,
):
    planes, rows, ww = turned_ref.shape
    hh = weight_ref.shape[1]
    ch, classes = rows // hh, diff_ref.shape[1] // hh
    values, bias_sum, offset_sum, product = backward_planes(diff_ref, weight_ref, hidden_ref, mat_t_ref, shifted_ref)
    bias_sum, offset_sum = bias_sum + bias_in_ref[...], offset_sum + offset_in_ref[...]
    product = product + product_in_ref[...]
    product = product.reshape(classes, hh, rows)
    keep = over(iota((classes, hh, rows), 2), ch) == iota((classes, hh, rows), 1)
    head = jnp.sum(jnp.where(keep, product, 0.0), axis=1)
    by_last = (rest(iota((rows, 128), 0), ch) == rest(iota((rows, 128), 1), 16)).astype(F32).astype(BF)
    head = dot_exact(head, by_last)
    bias = jnp.sum(jnp.sum(bias_sum.reshape(hh, ch, ww), axis=0), axis=1, keepdims=True)
    offset = jnp.sum(jnp.sum(offset_sum.reshape(classes, hh, ww), axis=1), axis=1, keepdims=True)
    odd = lax.rem(lax.axis_index("depth"), 2) == 1
    first, last = values[0].astype(F32), values[1].astype(F32)
    a_ref[...] = jnp.where(odd, first, last).astype(BF)
    b_ref[...] = jnp.where(odd, last, first).astype(BF)
    fields = [
        [halo_ref[0], turned_ref[planes - 2]],
        [turned_ref[0], turned_ref[planes - 1]],
        [turned_ref[1], halo_ref[1]],
    ]
    totals = weight_products(shifted_ref, fields, ch, hh, [total_ref[n] for n in range(9)])
    part = over(iota((ch, 256), 1), ch * (STEP + 2))
    for half in range(2):
        for t in range(27):
            i, j, k = t // 9, t // 3 % 3, t % 3
            value = jnp.where(part == i, totals[3 * k + j], 0.0)
            rows_ref[half, pl.ds(t, ch, stride=27)] = value[:, 128 * half : 128 * half + 128]
    pick = (rest(iota((ch, 256), 1), ch) == iota((ch, 256), 0)).astype(F32).astype(BF)
    sums = sum(dot_nt(pick, part) for part in split(jnp.concatenate([rows_ref[0], rows_ref[1]], axis=1)))
    for q in range(3):
        packed_ref[q * ch : (q + 1) * ch] = sums[:, 128 * q : 128 * q + 128]
    lane = iota((8, 128), 1)
    small = jnp.where(lane < 112, head, jnp.where(lane == 112, bias[:8], jnp.where(lane == 113, bias[8:], offset)))
    last = jnp.concatenate([sums[:, 384:], jnp.zeros((ch, 80), F32)], axis=1)
    low, high = last[:8], pltpu.roll(last[8:], 48, 1)
    packed_ref[3 * ch :] = jnp.where(lane < 48, low, jnp.where(lane < 96, high, small))


def input_kernel(a_ref, b_ref, shifted_ref, edge_ref, band_ref, out_ref, token_ref, turned_ref, grad_ref, sems):
    token_ref[...] = jnp.zeros_like(token_ref)
    ch, planes, hh, ww = grad_ref.shape
    rows = ch * hh
    unit = (iota((rows, rows), 0) == iota((rows, rows), 1)).astype(F32).astype(BF)
    for i in range(3):
        for k in range(3):
            block = band_ref[:, (3 * i + k) * rows : (3 * i + k + 1) * rows]
            col = (3 * (2 - i) + k) * rows
            turned_ref[:, col : col + rows] = dot_nt(unit, block).astype(BF)
    ends = []
    for x in sorted_halo(a_ref[...].astype(F32), b_ref[...].astype(F32)):
        before, after = moved(x)
        ends.append(jnp.concatenate([after, x, before], axis=0))
    field = [ends[0], edge_ref[0]] + [shifted_ref[d] for d in range(planes - 2)] + [edge_ref[1], ends[1]]
    part, copies = planes // 2, []
    for n in range(2):
        own = range(n * part, (n + 1) * part)
        wide = [jnp.concatenate(field[d : d + 3], axis=0) for d in own]
        grad = dot(turned_ref[...], jnp.concatenate(wide, axis=1)).astype(BF)
        for d in own:
            grad_ref[:, d] = grad[:, (d - n * part) * ww : (d - n * part + 1) * ww].reshape(ch, hh, ww)
        span = pl.ds(n * part, part)
        copies.append(pltpu.make_async_copy(grad_ref.at[:, span], out_ref.at[:, span], sems.at[n]))
        copies[-1].start()
    for copy in copies:
        copy.wait()


def unpack_kernel(scale, token_ref, own_ref, *refs):
    del token_ref
    others, (kernel_ref, bias_ref, head_ref, offset_ref) = refs[:-4], refs[-4:]
    ch = kernel_ref.shape[0]
    total = functools.reduce(jnp.add, [r[...] for r in others], own_ref[...]) * scale
    tail = total[3 * ch :]
    tiles = [total[q * ch : (q + 1) * ch] for q in range(3)]
    tiles.append(jnp.concatenate([tail, pltpu.roll(tail, 80, 1)], axis=0))
    lane = iota((ch, 128), 1)
    for co in range(ch):
        q, off = 27 * co // 128, 27 * co % 128
        value = pltpu.roll(tiles[q], 128 - off, 1) if off else tiles[q]
        if off + 27 > 128:
            value = jnp.where(lane < 128 - off, value, pltpu.roll(tiles[q + 1], 128 - off, 1))
        kernel_ref[co] = value[:, 0:27]
    head_ref[...] = pltpu.roll(tail, 32, 1)[:, 0:16]
    column, row = iota((8, ch), 1), iota((8, ch), 0)
    low = jnp.where(column == row, tail[:, 112:113], 0.0) + jnp.where(column == row + 8, tail[:, 113:114], 0.0)
    bias_ref[...] = jnp.sum(low, axis=0, keepdims=True)
    diagonal = jnp.where(column[:, :8] == row[:, :8], tail[:, 114:115], 0.0)
    offset_ref[...] = jnp.sum(diagonal, axis=0, keepdims=True)


def call(kernel, out_shape, in_spaces, scratch, flops, args, out_spaces=None):
    moved_bytes = sum(a.size * a.dtype.itemsize for a in args)
    return pl.pallas_call(
        kernel,
        out_shape=out_shape,
        in_specs=[pl.BlockSpec(memory_space=s) for s in in_spaces],
        out_specs=jax.tree.map(
            lambda _, s: pl.BlockSpec(memory_space=s), out_shape, out_spaces or jax.tree.map(lambda _: VM, out_shape)
        ),
        scratch_shapes=scratch,
        compiler_params=pltpu.CompilerParams(vmem_limit_bytes=32 << 20),
        cost_estimate=pl.CostEstimate(flops=flops, bytes_accessed=moved_bytes, transcendentals=0),
    )(*args)


def exchange_pairs():
    crops, size = lax.axis_size("dp"), lax.axis_size("depth")
    one, two = [], []
    for c in range(crops):
        for d in range(size):
            one.append((c * size + d, c * size + (d ^ 1)))
            e = ((d + 1) ^ 1) - 1
            if 0 <= e < size:
                two.append((c * size + d, c * size + e))
            elif crops % 2 == 0:
                two.append((c * size + d, (c ^ 1) * size + d))
    return one, two


def exchanged(a, b):
    one, two = exchange_pairs()
    return lax.ppermute(a, ("dp", "depth"), one), lax.ppermute(b, ("dp", "depth"), two)


def reduction_rounds():
    count = lax.axis_size("dp") * lax.axis_size("depth")
    bits = [1 << b for b in range((count - 1).bit_length())]
    bits = bits[-1:] + bits[1:2] + bits[:1] + bits[2:-1] if len(bits) >= 4 else bits
    rounds = []
    for n in range(0, len(bits), 2):
        masks = bits[n : n + 2]
        masks = masks + [sum(masks)] if len(masks) == 2 else masks
        rounds.append([[(i, i ^ m) for i in range(count)] for m in masks])
    return rounds


def body(features, labels, masks, conv_kernel, conv_bias, head_weight, head_bias):
    x, label, mask = features[0, 0], labels[0], masks[0, 0]
    kernel, head = conv_kernel[0], head_weight[0]
    ch, planes, hh, ww = x.shape
    classes = head.shape[0]
    rows = ch * hh
    sds = jax.ShapeDtypeStruct
    size = lax.axis_size("depth")
    pair_flops = 2 * rows * 9 * rows * 2 * ww

    plane = sds((ch, hh, ww), BF)
    inputs = (x, label, mask, kernel.transpose(1, 2, 0), conv_bias, head, head_bias)
    inputs = tuple(pltpu.with_memory_space_constraint(v, pltpu.HBM) for v in inputs)
    shapes = tuple(sds(v.shape, v.dtype) for v in inputs)
    *inputs, end_a, end_b = call(
        load_kernel,
        (*shapes, plane, plane),
        (pltpu.HBM,) * len(inputs),
        [pltpu.SemaphoreType.DMA((len(inputs),))],
        0,
        inputs,
    )
    x, label, mask, kernel, conv_bias, head, head_bias = inputs
    far = exchanged(end_a, end_b)
    inner = planes - 2
    band, mat, mat_t, turn, bias, shifted, turned_x, hidden_in, diff_in, offered_in = call(
        interior_kernel,
        (
            sds((rows, 9 * rows), BF),
            sds((classes * hh, rows), BF),
            sds((rows, classes * hh), BF),
            sds((rows, rows), BF),
            sds((ch, 2 * ww), F32),
            sds((planes, 3 * rows, ww), BF),
            sds((planes, rows, ww), BF),
            sds((inner, rows, ww), BF),
            sds((inner, classes * hh, ww), F32),
            sds((inner, hh, ww), F32),
        ),
        (VM,) * 7,
        [],
        pair_flops * inner // 2,
        (x, label, mask, kernel, conv_bias, head, head_bias),
    )
    peers = [(0, 1), (1, 0)]
    weight_in = lax.ppermute(offered_in, "net", peers)
    halo, hidden_edge, diff_edge, offered_edge = call(
        edge_kernel,
        (
            sds((2, rows, ww), BF),
            sds((2, rows, ww), BF),
            sds((2, classes * hh, ww), F32),
            sds((2, hh, ww), F32),
        ),
        (VM,) * 9,
        [],
        pair_flops,
        (*far, label, mask, head_bias, band, mat, bias, shifted),
    )
    weight_edge = lax.ppermute(offered_edge, "net", peers)
    sums = (
        sds((9, ch, 256), F32),
        sds((rows, ww), F32),
        sds((classes * hh, ww), F32),
        sds((classes * hh, rows), F32),
    )
    grads, *sums, halo = call(
        inner_backward_kernel,
        (sds((inner, 3 * rows, ww), BF), *sums, sds((2, rows, ww), BF)),
        (VM,) * 7,
        [],
        pair_flops * inner // 2,
        (turned_x, weight_in, hidden_in, diff_in, mat_t, halo, turn),
    )
    edge = sds((rows, ww), BF)
    packed, grad_a, grad_b, grad_edge = call(
        edge_backward_kernel,
        (sds((3 * ch + 8, 128), F32), edge, edge, sds((2, 3 * rows, ww), BF)),
        (VM,) * 10,
        [VM((2, 27 * ch, 128), F32)],
        pair_flops,
        (turned_x, halo, weight_edge, hidden_edge, diff_edge, mat_t, *sums),
    )
    rounds, pairs = reduction_rounds(), exchange_pairs()
    for n, masks in enumerate(rounds):
        others = [lax.ppermute(packed, ("dp", "depth"), p) for p in masks]
        if n == 0:
            grad_far = [lax.ppermute(e, ("dp", "depth"), p) for e, p in zip((grad_a, grad_b), pairs)]
        if n < len(rounds) - 1:
            packed = functools.reduce(jnp.add, others, packed)
        if n == len(rounds) - 2:
            packed, band = lax.optimization_barrier((packed, band))
    grad_input, token = call(
        input_kernel,
        (sds((ch, planes, hh, ww), BF), sds((8, 128), F32)),
        (VM,) * 5,
        [VM((rows, 9 * rows), BF), VM((ch, planes, hh, ww), BF), pltpu.SemaphoreType.DMA((2,))],
        pair_flops * planes // 2,
        (*grad_far, grads, grad_edge, band),
        (pltpu.HBM, VM),
    )
    scale = 1.0 / (lax.axis_size("dp") * size * planes * hh * ww)
    grad_kernel, grad_bias, grad_head, grad_offset = call(
        functools.partial(unpack_kernel, scale),
        (sds((ch, ch, 27), F32), sds((1, ch), F32), sds((classes, ch), F32), sds((1, classes), F32)),
        (VM,) * (2 + len(others)),
        [],
        1000,
        (token, packed, *others),
    )
    return (
        grad_input[None, None],
        grad_kernel.transpose(2, 0, 1)[None],
        grad_bias,
        grad_head[None],
        grad_offset,
    )


def solution(mesh):
    in_specs = (
        P("net", "dp", None, "depth", None, None),
        P("dp", "depth", None, None),
        P("net", "dp", "depth", None, None),
        P("net", None, None, None),
        P("net", None),
        P("net", None, None),
        P("net", None),
    )
    out_specs = (
        P("net", "dp", None, "depth", None, None),
        P("net", None, None, None),
        P("net", None),
        P("net", None, None),
        P("net", None),
    )
    return jax.shard_map(body, mesh=mesh, in_specs=in_specs, out_specs=out_specs, check_vma=False)
```

```python
import functools

import jax
import jax.numpy as jnp
from jax import lax
from jax.experimental import pallas as pl
from jax.experimental.pallas import tpu as pltpu
from jax.sharding import PartitionSpec as P

BF = jnp.bfloat16
F32 = jnp.float32
VM = pltpu.VMEM
SM = pltpu.SMEM


def iota(shape, dim):
    return lax.broadcasted_iota(jnp.int32, shape, dim)


def over(x, n):
    return lax.shift_right_logical(x, n.bit_length() - 1) if n & (n - 1) == 0 else x // n


def rest(x, n):
    return lax.bitwise_and(x, n - 1) if n & (n - 1) == 0 else lax.rem(x, n)


def dot(a, b):
    return jnp.dot(a, b, preferred_element_type=F32)


def dot_nt(a, b):
    return lax.dot_general(a, b, (((1,), (1,)), ((), ())), preferred_element_type=F32)


def split(x):
    high = x.astype(BF)
    return high, (x - high.astype(F32)).astype(BF)


def dot_exact(x, ones):
    return sum(dot(part, ones) for part in split(x))


def moved(x):
    y = x.astype(F32)
    lane = iota(y.shape, 1)
    width = y.shape[1]
    before = jnp.where(lane == 0, 0.0, pltpu.roll(y, 1, 1))
    after = jnp.where(lane == width - 1, 0.0, pltpu.roll(y, width - 1, 1))
    return before.astype(BF), after.astype(BF)


def fill_band(kernel_ref, band_ref, ch, hh):
    rows = ch * hh
    unit = (iota((32, 27), 0) == iota((32, 27), 1)).astype(F32).astype(BF)
    by_tap = dot_nt(unit, kernel_ref[...].reshape(ch * ch, 27))
    wide = jnp.broadcast_to(by_tap[:27, None, :], (27, ch, ch * ch))
    wide = jnp.where(over(iota((27, ch, ch * ch), 2), ch) == iota((27, ch, ch * ch), 1), wide, 0.0)
    spread = (over(iota((ch * ch, rows), 1), hh) == rest(iota((ch * ch, rows), 0), ch)).astype(F32).astype(BF)
    wide = dot(wide.reshape(27 * ch, ch * ch).astype(BF), spread).astype(BF)
    masks = [(rest(iota((ch, rows), 1), hh) == h).astype(F32).astype(BF) for h in range(hh)]
    for i in range(3):
        for k in range(3):
            taps = [wide[(9 * i + 3 * j + k) * ch : (9 * i + 3 * j + k + 1) * ch] for j in range(3)]
            col = (3 * i + k) * rows
            for h in range(hh):
                block = masks[h] * taps[1]
                if h > 0:
                    block = block + masks[h - 1] * taps[0]
                if h < hh - 1:
                    block = block + masks[h + 1] * taps[2]
                band_ref[h * ch : (h + 1) * ch, col : col + rows] = block


def head_matrix(head_ref, ch, hh, classes):
    rows = ch * hh
    spread = (rest(iota((ch, rows), 1), ch) == iota((ch, rows), 0)).astype(F32).astype(BF)
    wide = dot(head_ref[...], spread)
    wide = jnp.broadcast_to(wide[:, None, :], (classes, hh, rows))
    keep = over(iota((classes, hh, rows), 2), ch) == iota((classes, hh, rows), 1)
    return jnp.where(keep, wide, 0.0).reshape(classes * hh, rows).astype(BF)


def bias_rows(bias_ref, ch, width):
    square = jnp.broadcast_to(bias_ref[...], (ch, ch))
    column = jnp.sum(jnp.where(iota((ch, ch), 0) == iota((ch, ch), 1), square, 0.0), axis=1, keepdims=True)
    return jnp.broadcast_to(column, (ch, width))


def shifts(x):
    before, after = moved(x)
    return jnp.concatenate([before, x, after], axis=0)


def head_pair(preact, bias, mat, head_bias_ref, label, mask, dims):
    ch, hh, ww, classes = dims
    rows = ch * hh
    preact = (preact.reshape(hh, ch, 2 * ww) + bias[None]).reshape(rows, 2 * ww)
    hidden = jnp.maximum(preact, 0.0).astype(BF)
    logits = dot(mat, hidden).reshape(classes, hh, 2 * ww)
    parts = [logits[c] + head_bias_ref[0:1, c : c + 1] for c in range(classes)]
    total = functools.reduce(jnp.add, [jnp.exp(p) for p in parts])
    log_total = jnp.log(total)
    soft = [jnp.exp(p - log_total) for p in parts]
    hot = [label == c for c in range(classes)]
    chosen = functools.reduce(jnp.add, [jnp.where(o, s, 0.0) for o, s in zip(hot, soft)])
    diffs = [s - jnp.where(o, 1.0, 0.0) for o, s in zip(hot, soft)]
    return hidden, jnp.stack(diffs).reshape(classes * hh, 2 * ww), mask * chosen


def put_pair(ref, first, second, value, ww):
    ref[first] = value[:, :ww]
    ref[second] = value[:, ww:]


def beside(ref, first, second):
    return jnp.concatenate([ref[first], ref[second]], axis=1)


PARTS = 4


def load_kernel(*refs):
    count = (len(refs) - 3) // 2
    sources, targets, (a_ref, b_ref, sems) = refs[:count], refs[count : 2 * count], refs[2 * count :]
    planes = sources[0].shape[1]
    part = sources[0].shape[0] // PARTS
    spans = [pl.ds(n * part, part) for n in range(PARTS)]
    pairs = [(sources[0].at[span], targets[0].at[span]) for span in spans] + list(zip(sources[1:], targets[1:]))
    copies = [pltpu.make_async_copy(s, t, sems.at[n]) for n, (s, t) in enumerate(pairs)]
    for copy in copies:
        copy.start()
    for copy in copies[:PARTS]:
        copy.wait()
    odd = lax.rem(lax.axis_index("depth"), 2)
    a_ref[...] = targets[0][:, (1 - odd) * (planes - 1)]
    b_ref[...] = targets[0][:, odd * (planes - 1)]
    for copy in copies[PARTS:]:
        copy.wait()


def sorted_halo(a, b):
    place, size = lax.axis_index("depth"), lax.axis_size("depth")
    odd = lax.rem(place, 2) == 1
    before, after = jnp.where(odd, a, b), jnp.where(odd, b, a)
    before = jnp.where(place > 0, before, 0.0)
    after = jnp.where(place < size - 1, after, 0.0)
    return before.astype(BF), after.astype(BF)


def turner(ch, hh):
    rows = ch * hh
    row, col = iota((rows, rows), 0), iota((rows, rows), 1)
    return ((over(row, ch) == rest(col, hh)) & (rest(row, ch) == over(col, hh))).astype(F32).astype(BF)


def interior_kernel(
    x_ref, label_ref, mask_ref, kernel_ref, bias_ref, head_ref, head_bias_ref,
    band_ref, mat_ref, mat_t_ref, turner_ref, bias_out_ref,
    shifted_ref, turned_ref, hidden_ref, diff_ref, offered_ref,
):
    ch, planes, hh, ww = x_ref.shape
    classes = head_ref.shape[0]
    rows = ch * hh
    inner = planes - 2
    fill_band(kernel_ref, band_ref, ch, hh)
    mat = head_matrix(head_ref, ch, hh, classes)
    bias = bias_rows(bias_ref, ch, 2 * ww)
    field = [x_ref[:, d].reshape(rows, ww) for d in range(planes)]
    for d in range(planes):
        shifted_ref[d] = shifts(field[d])
    wide = [shifted_ref[d : d + 3].reshape(9 * rows, ww) for d in range(inner)]
    preact = dot(band_ref[...], jnp.concatenate(wide, axis=1))
    for d in range(0, inner, 2):
        hidden, diff, offered = head_pair(
            preact[:, d * ww : (d + 2) * ww], bias, mat, head_bias_ref, beside(label_ref, d + 1, d + 2),
            beside(mask_ref, d + 1, d + 2).astype(F32), (ch, hh, ww, classes),
        )
        put_pair(hidden_ref, d, d + 1, hidden, ww)
        put_pair(diff_ref, d, d + 1, diff, ww)
        put_pair(offered_ref, d, d + 1, offered, ww)
    turn = turner(ch, hh)
    turned = dot(turn, jnp.concatenate(field, axis=1)).astype(BF)
    for d in range(planes):
        turned_ref[d] = turned[:, d * ww : (d + 1) * ww]
    unit = (iota((rows, rows), 0) == iota((rows, rows), 1)).astype(F32).astype(BF)
    mat_ref[...], mat_t_ref[...], turner_ref[...], bias_out_ref[...] = mat, dot_nt(unit, mat).astype(BF), turn, bias


def edge_kernel(
    a_ref, b_ref, label_ref, mask_ref, head_bias_ref, band_ref, mat_ref, bias_ref, shifted_ref,
    halo_ref, hidden_ref, diff_ref, offered_ref,
):
    ch, hh, ww = a_ref.shape
    planes, classes = label_ref.shape[0], mat_ref.shape[0] // hh
    rows = ch * hh
    before, after = sorted_halo(a_ref[...].reshape(rows, ww).astype(F32), b_ref[...].reshape(rows, ww).astype(F32))
    left = jnp.concatenate([shifts(before), shifted_ref[0:2].reshape(6 * rows, ww)], axis=0)
    right = jnp.concatenate([shifted_ref[planes - 2 : planes].reshape(6 * rows, ww), shifts(after)], axis=0)
    preact = dot(band_ref[...], jnp.concatenate([left, right], axis=1))
    hidden, diff, offered = head_pair(
        preact, bias_ref[...], mat_ref[...], head_bias_ref, beside(label_ref, 0, planes - 1),
        beside(mask_ref, 0, planes - 1).astype(F32), (ch, hh, ww, classes),
    )
    put_pair(hidden_ref, 0, 1, hidden, ww)
    put_pair(diff_ref, 0, 1, diff, ww)
    put_pair(offered_ref, 0, 1, offered, ww)
    halo_ref[0], halo_ref[1] = before, after


def backward_planes(diff_ref, weight_ref, hidden_ref, mat_t_ref, shifted_ref):
    count, rows, ww = hidden_ref.shape
    hh = weight_ref.shape[1]
    classes = diff_ref.shape[1] // hh
    offset_sum, halves = 0.0, []
    for d in range(count):
        grad = (diff_ref[d].reshape(classes, hh, ww) * weight_ref[d][None]).reshape(classes * hh, ww)
        offset_sum = offset_sum + grad
        halves.append(grad.astype(BF))
    halves = jnp.concatenate(halves, axis=1)
    hiddens = jnp.concatenate([hidden_ref[d] for d in range(count)], axis=1)
    pre = jnp.where(hiddens.astype(F32) > 0.0, dot(mat_t_ref[...], halves), 0.0)
    bias_sum = sum(pre[:, d * ww : (d + 1) * ww] for d in range(count))
    values = [pre[:, d * ww : (d + 1) * ww].astype(BF) for d in range(count)]
    for d in range(count):
        before, after = moved(values[d])
        shifted_ref[d] = jnp.concatenate([after, values[d], before], axis=0)
    return values, bias_sum, offset_sum, dot_nt(halves, hiddens)


STEP = 3


def weight_products(shifted_ref, fields, ch, hh, totals):
    count, rows3, ww = shifted_ref.shape
    rows = rows3 // 3
    span = STEP + 2
    spot = rest(over(iota((ch, 256), 1), ch), span)
    grads = [shifted_ref[d] for d in range(count)]
    for h0 in range(0, hh, STEP):
        step = min(STEP, hh - h0)
        left = [g[k * rows + h0 * ch : k * rows + (h0 + step) * ch] for k in range(3) for g in grads]
        left = [jnp.concatenate(left[k * count : (k + 1) * count], axis=1) for k in range(3)]
        low, high = max(h0 - 1, 0), min(h0 + span - 1, hh)
        right = []
        for i in range(3):
            if h0 == 0:
                right.append(jnp.zeros((ch, count * ww), BF))
            right.append(jnp.concatenate([f[low * ch : high * ch] for f in fields[i]], axis=1))
            if h0 + span - 1 > hh:
                right.append(jnp.zeros(((h0 + span - 1 - hh) * ch, count * ww), BF))
        right.append(jnp.zeros((256 - 3 * span * ch, count * ww), BF))
        product = dot_nt(jnp.concatenate(left, axis=0), jnp.concatenate(right, axis=0))
        for k in range(3):
            for j in range(3):
                total = jnp.zeros((ch, 256), F32)
                for h in range(step):
                    r = (k * step + h) * ch
                    total = jnp.where(spot == h + j, product[r : r + ch], total)
                totals[3 * k + j] = totals[3 * k + j] + total
    return totals


def inner_backward_kernel(
    turned_ref, weight_ref, hidden_ref, diff_ref, mat_t_ref, halo_ref, turner_ref,
    shifted_ref, total_ref, bias_ref, offset_ref, product_ref, halo_turned_ref,
):
    inner, rows, ww = hidden_ref.shape
    put_pair(halo_turned_ref, 0, 1, dot(turner_ref[...], beside(halo_ref, 0, 1)).astype(BF), ww)
    hh = weight_ref.shape[1]
    _, bias_ref[...], offset_ref[...], product_ref[...] = backward_planes(
        diff_ref, weight_ref, hidden_ref, mat_t_ref, shifted_ref
    )
    fields = [[turned_ref[d + i] for d in range(inner)] for i in range(3)]
    totals = weight_products(shifted_ref, fields, rows // hh, hh, [0.0] * 9)
    for n in range(9):
        total_ref[n] = totals[n]


def edge_backward_kernel(
    turned_ref, halo_ref, weight_ref, hidden_ref, diff_ref, mat_t_ref, total_ref, bias_in_ref, offset_in_ref, product_in_ref,
    packed_ref, a_ref, b_ref, shifted_ref, rows_ref,
):
    planes, rows, ww = turned_ref.shape
    hh = weight_ref.shape[1]
    ch, classes = rows // hh, diff_ref.shape[1] // hh
    values, bias_sum, offset_sum, product = backward_planes(diff_ref, weight_ref, hidden_ref, mat_t_ref, shifted_ref)
    bias_sum, offset_sum = bias_sum + bias_in_ref[...], offset_sum + offset_in_ref[...]
    product = product + product_in_ref[...]
    product = product.reshape(classes, hh, rows)
    keep = over(iota((classes, hh, rows), 2), ch) == iota((classes, hh, rows), 1)
    head = jnp.sum(jnp.where(keep, product, 0.0), axis=1)
    by_last = (rest(iota((rows, 128), 0), ch) == rest(iota((rows, 128), 1), 16)).astype(F32).astype(BF)
    head = dot_exact(head, by_last)
    bias = jnp.sum(jnp.sum(bias_sum.reshape(hh, ch, ww), axis=0), axis=1, keepdims=True)
    offset = jnp.sum(jnp.sum(offset_sum.reshape(classes, hh, ww), axis=1), axis=1, keepdims=True)
    odd = lax.rem(lax.axis_index("depth"), 2) == 1
    first, last = values[0].astype(F32), values[1].astype(F32)
    a_ref[...] = jnp.where(odd, first, last).astype(BF)
    b_ref[...] = jnp.where(odd, last, first).astype(BF)
    fields = [
        [halo_ref[0], turned_ref[planes - 2]],
        [turned_ref[0], turned_ref[planes - 1]],
        [turned_ref[1], halo_ref[1]],
    ]
    totals = weight_products(shifted_ref, fields, ch, hh, [total_ref[n] for n in range(9)])
    part = over(iota((ch, 256), 1), ch * (STEP + 2))
    for half in range(2):
        for t in range(27):
            i, j, k = t // 9, t // 3 % 3, t % 3
            value = jnp.where(part == i, totals[3 * k + j], 0.0)
            rows_ref[half, pl.ds(t, ch, stride=27)] = value[:, 128 * half : 128 * half + 128]
    pick = (rest(iota((ch, 256), 1), ch) == iota((ch, 256), 0)).astype(F32).astype(BF)
    sums = sum(dot_nt(pick, part) for part in split(jnp.concatenate([rows_ref[0], rows_ref[1]], axis=1)))
    for q in range(3):
        packed_ref[q * ch : (q + 1) * ch] = sums[:, 128 * q : 128 * q + 128]
    lane = iota((8, 128), 1)
    small = jnp.where(lane < 112, head, jnp.where(lane == 112, bias[:8], jnp.where(lane == 113, bias[8:], offset)))
    last = jnp.concatenate([sums[:, 384:], jnp.zeros((ch, 80), F32)], axis=1)
    low, high = last[:8], pltpu.roll(last[8:], 48, 1)
    packed_ref[3 * ch :] = jnp.where(lane < 48, low, jnp.where(lane < 96, high, small))


def input_kernel(a_ref, b_ref, shifted_ref, edge_ref, band_ref, out_ref, token_ref, turned_ref, grad_ref, sems):
    token_ref[...] = jnp.zeros_like(token_ref)
    ch, planes, hh, ww = grad_ref.shape
    rows = ch * hh
    unit = (iota((rows, rows), 0) == iota((rows, rows), 1)).astype(F32).astype(BF)
    for i in range(3):
        for k in range(3):
            block = band_ref[:, (3 * i + k) * rows : (3 * i + k + 1) * rows]
            col = (3 * (2 - i) + k) * rows
            turned_ref[:, col : col + rows] = dot_nt(unit, block).astype(BF)
    ends = []
    for x in sorted_halo(a_ref[...].astype(F32), b_ref[...].astype(F32)):
        before, after = moved(x)
        ends.append(jnp.concatenate([after, x, before], axis=0))
    field = [ends[0], edge_ref[0]] + [shifted_ref[d] for d in range(planes - 2)] + [edge_ref[1], ends[1]]
    part, copies = planes // 2, []
    for n in range(2):
        own = range(n * part, (n + 1) * part)
        wide = [jnp.concatenate(field[d : d + 3], axis=0) for d in own]
        grad = dot(turned_ref[...], jnp.concatenate(wide, axis=1)).astype(BF)
        for d in own:
            grad_ref[:, d] = grad[:, (d - n * part) * ww : (d - n * part + 1) * ww].reshape(ch, hh, ww)
        span = pl.ds(n * part, part)
        copies.append(pltpu.make_async_copy(grad_ref.at[:, span], out_ref.at[:, span], sems.at[n]))
        copies[-1].start()
    for copy in copies:
        copy.wait()


def unpack_kernel(scale, token_ref, own_ref, *refs):
    del token_ref
    others, (kernel_ref, bias_ref, head_ref, offset_ref) = refs[:-4], refs[-4:]
    ch = kernel_ref.shape[0]
    total = functools.reduce(jnp.add, [r[...] for r in others], own_ref[...]) * scale
    tail = total[3 * ch :]
    tiles = [total[q * ch : (q + 1) * ch] for q in range(3)]
    tiles.append(jnp.concatenate([tail, pltpu.roll(tail, 80, 1)], axis=0))
    lane = iota((ch, 128), 1)
    for co in range(ch):
        q, off = 27 * co // 128, 27 * co % 128
        value = pltpu.roll(tiles[q], 128 - off, 1) if off else tiles[q]
        if off + 27 > 128:
            value = jnp.where(lane < 128 - off, value, pltpu.roll(tiles[q + 1], 128 - off, 1))
        kernel_ref[co] = value[:, 0:27]
    head_ref[...] = pltpu.roll(tail, 32, 1)[:, 0:16]
    column, row = iota((8, ch), 1), iota((8, ch), 0)
    low = jnp.where(column == row, tail[:, 112:113], 0.0) + jnp.where(column == row + 8, tail[:, 113:114], 0.0)
    bias_ref[...] = jnp.sum(low, axis=0, keepdims=True)
    diagonal = jnp.where(column[:, :8] == row[:, :8], tail[:, 114:115], 0.0)
    offset_ref[...] = jnp.sum(diagonal, axis=0, keepdims=True)


def call(kernel, out_shape, in_spaces, scratch, flops, args, out_spaces=None):
    moved_bytes = sum(a.size * a.dtype.itemsize for a in args)
    return pl.pallas_call(
        kernel,
        out_shape=out_shape,
        in_specs=[pl.BlockSpec(memory_space=s) for s in in_spaces],
        out_specs=jax.tree.map(
            lambda _, s: pl.BlockSpec(memory_space=s), out_shape, out_spaces or jax.tree.map(lambda _: VM, out_shape)
        ),
        scratch_shapes=scratch,
        compiler_params=pltpu.CompilerParams(vmem_limit_bytes=32 << 20),
        cost_estimate=pl.CostEstimate(flops=flops, bytes_accessed=moved_bytes, transcendentals=0),
    )(*args)


def exchange_pairs():
    crops, size = lax.axis_size("dp"), lax.axis_size("depth")
    one, two = [], []
    for c in range(crops):
        for d in range(size):
            one.append((c * size + d, c * size + (d ^ 1)))
            e = ((d + 1) ^ 1) - 1
            if 0 <= e < size:
                two.append((c * size + d, c * size + e))
            elif crops % 2 == 0:
                two.append((c * size + d, (c ^ 1) * size + d))
    return one, two


def exchanged(a, b):
    one, two = exchange_pairs()
    return lax.ppermute(a, ("dp", "depth"), one), lax.ppermute(b, ("dp", "depth"), two)


def reduction_rounds():
    count = lax.axis_size("dp") * lax.axis_size("depth")
    bits = [1 << b for b in range((count - 1).bit_length())]
    bits = bits[-1:] + bits[1:2] + bits[:1] + bits[2:-1] if len(bits) >= 4 else bits
    rounds = []
    for n in range(0, len(bits), 2):
        masks = bits[n : n + 2]
        masks = masks + [sum(masks)] if len(masks) == 2 else masks
        rounds.append([[(i, i ^ m) for i in range(count)] for m in masks])
    return rounds


def body(features, labels, masks, conv_kernel, conv_bias, head_weight, head_bias):
    x, label, mask = features[0, 0], labels[0], masks[0, 0]
    kernel, head = conv_kernel[0], head_weight[0]
    ch, planes, hh, ww = x.shape
    classes = head.shape[0]
    rows = ch * hh
    sds = jax.ShapeDtypeStruct
    size = lax.axis_size("depth")
    pair_flops = 2 * rows * 9 * rows * 2 * ww

    plane = sds((ch, hh, ww), BF)
    inputs = (x, label, mask, kernel.transpose(1, 2, 0), conv_bias, head, head_bias)
    inputs = tuple(pltpu.with_memory_space_constraint(v, pltpu.HBM) for v in inputs)
    shapes = tuple(sds(v.shape, v.dtype) for v in inputs)
    *inputs, end_a, end_b = call(
        load_kernel,
        (*shapes, plane, plane),
        (pltpu.HBM,) * len(inputs),
        [pltpu.SemaphoreType.DMA((len(inputs) - 1 + PARTS,))],
        0,
        inputs,
    )
    x, label, mask, kernel, conv_bias, head, head_bias = inputs
    far = exchanged(end_a, end_b)
    inner = planes - 2
    band, mat, mat_t, turn, bias, shifted, turned_x, hidden_in, diff_in, offered_in = call(
        interior_kernel,
        (
            sds((rows, 9 * rows), BF),
            sds((classes * hh, rows), BF),
            sds((rows, classes * hh), BF),
            sds((rows, rows), BF),
            sds((ch, 2 * ww), F32),
            sds((planes, 3 * rows, ww), BF),
            sds((planes, rows, ww), BF),
            sds((inner, rows, ww), BF),
            sds((inner, classes * hh, ww), F32),
            sds((inner, hh, ww), F32),
        ),
        (VM,) * 7,
        [],
        pair_flops * inner // 2,
        (x, label, mask, kernel, conv_bias, head, head_bias),
    )
    peers = [(0, 1), (1, 0)]
    weight_in = lax.ppermute(offered_in, "net", peers)
    halo, hidden_edge, diff_edge, offered_edge = call(
        edge_kernel,
        (
            sds((2, rows, ww), BF),
            sds((2, rows, ww), BF),
            sds((2, classes * hh, ww), F32),
            sds((2, hh, ww), F32),
        ),
        (VM,) * 9,
        [],
        pair_flops,
        (*far, label, mask, head_bias, band, mat, bias, shifted),
    )
    weight_edge = lax.ppermute(offered_edge, "net", peers)
    sums = (
        sds((9, ch, 256), F32),
        sds((rows, ww), F32),
        sds((classes * hh, ww), F32),
        sds((classes * hh, rows), F32),
    )
    grads, *sums, halo = call(
        inner_backward_kernel,
        (sds((inner, 3 * rows, ww), BF), *sums, sds((2, rows, ww), BF)),
        (VM,) * 7,
        [],
        pair_flops * inner // 2,
        (turned_x, weight_in, hidden_in, diff_in, mat_t, halo, turn),
    )
    edge = sds((rows, ww), BF)
    packed, grad_a, grad_b, grad_edge = call(
        edge_backward_kernel,
        (sds((3 * ch + 8, 128), F32), edge, edge, sds((2, 3 * rows, ww), BF)),
        (VM,) * 10,
        [VM((2, 27 * ch, 128), F32)],
        pair_flops,
        (turned_x, halo, weight_edge, hidden_edge, diff_edge, mat_t, *sums),
    )
    rounds, pairs = reduction_rounds(), exchange_pairs()
    for n, masks in enumerate(rounds):
        others = [lax.ppermute(packed, ("dp", "depth"), p) for p in masks]
        if n == 0:
            grad_far = [lax.ppermute(e, ("dp", "depth"), p) for e, p in zip((grad_a, grad_b), pairs)]
        if n < len(rounds) - 1:
            packed = functools.reduce(jnp.add, others, packed)
        if n == len(rounds) - 2:
            packed, band = lax.optimization_barrier((packed, band))
    grad_input, token = call(
        input_kernel,
        (sds((ch, planes, hh, ww), BF), sds((8, 128), F32)),
        (VM,) * 5,
        [VM((rows, 9 * rows), BF), VM((ch, planes, hh, ww), BF), pltpu.SemaphoreType.DMA((2,))],
        pair_flops * planes // 2,
        (*grad_far, grads, grad_edge, band),
        (pltpu.HBM, VM),
    )
    scale = 1.0 / (lax.axis_size("dp") * size * planes * hh * ww)
    grad_kernel, grad_bias, grad_head, grad_offset = call(
        functools.partial(unpack_kernel, scale),
        (sds((ch, ch, 27), F32), sds((1, ch), F32), sds((classes, ch), F32), sds((1, classes), F32)),
        (VM,) * (2 + len(others)),
        [],
        1000,
        (token, packed, *others),
    )
    return (
        grad_input[None, None],
        grad_kernel.transpose(2, 0, 1)[None],
        grad_bias,
        grad_head[None],
        grad_offset,
    )


def solution(mesh):
    in_specs = (
        P("net", "dp", None, "depth", None, None),
        P("dp", "depth", None, None),
        P("net", "dp", "depth", None, None),
        P("net", None, None, None),
        P("net", None),
        P("net", None, None),
        P("net", None),
    )
    out_specs = (
        P("net", "dp", None, "depth", None, None),
        P("net", None, None, None),
        P("net", None),
        P("net", None, None),
        P("net", None),
    )
    return jax.shard_map(body, mesh=mesh, in_specs=in_specs, out_specs=out_specs, check_vma=False)
```

```python
import functools

import jax
import jax.numpy as jnp
from jax import lax
from jax.experimental import pallas as pl
from jax.experimental.pallas import tpu as pltpu
from jax.sharding import PartitionSpec as P

BF = jnp.bfloat16
F32 = jnp.float32
VM = pltpu.VMEM
SM = pltpu.SMEM


def iota(shape, dim):
    return lax.broadcasted_iota(jnp.int32, shape, dim)


def over(x, n):
    return lax.shift_right_logical(x, n.bit_length() - 1) if n & (n - 1) == 0 else x // n


def rest(x, n):
    return lax.bitwise_and(x, n - 1) if n & (n - 1) == 0 else lax.rem(x, n)


def dot(a, b):
    return jnp.dot(a, b, preferred_element_type=F32)


def dot_nt(a, b):
    return lax.dot_general(a, b, (((1,), (1,)), ((), ())), preferred_element_type=F32)


def split(x):
    high = x.astype(BF)
    return high, (x - high.astype(F32)).astype(BF)


def dot_exact(x, ones):
    return sum(dot(part, ones) for part in split(x))


def moved(x):
    y = x.astype(F32)
    lane = iota(y.shape, 1)
    width = y.shape[1]
    before = jnp.where(lane == 0, 0.0, pltpu.roll(y, 1, 1))
    after = jnp.where(lane == width - 1, 0.0, pltpu.roll(y, width - 1, 1))
    return before.astype(BF), after.astype(BF)


def fill_band(kernel_ref, band_ref, ch, hh):
    rows = ch * hh
    unit = (iota((32, 27), 0) == iota((32, 27), 1)).astype(F32).astype(BF)
    by_tap = dot_nt(unit, kernel_ref[...].reshape(ch * ch, 27))
    wide = jnp.broadcast_to(by_tap[:27, None, :], (27, ch, ch * ch))
    wide = jnp.where(over(iota((27, ch, ch * ch), 2), ch) == iota((27, ch, ch * ch), 1), wide, 0.0)
    spread = (over(iota((ch * ch, rows), 1), hh) == rest(iota((ch * ch, rows), 0), ch)).astype(F32).astype(BF)
    wide = dot(wide.reshape(27 * ch, ch * ch).astype(BF), spread).astype(BF)
    masks = [(rest(iota((ch, rows), 1), hh) == h).astype(F32).astype(BF) for h in range(hh)]
    for i in range(3):
        for k in range(3):
            taps = [wide[(9 * i + 3 * j + k) * ch : (9 * i + 3 * j + k + 1) * ch] for j in range(3)]
            col = (3 * i + k) * rows
            for h in range(hh):
                block = masks[h] * taps[1]
                if h > 0:
                    block = block + masks[h - 1] * taps[0]
                if h < hh - 1:
                    block = block + masks[h + 1] * taps[2]
                band_ref[h * ch : (h + 1) * ch, col : col + rows] = block


def head_matrix(head_ref, ch, hh, classes):
    rows = ch * hh
    spread = (rest(iota((ch, rows), 1), ch) == iota((ch, rows), 0)).astype(F32).astype(BF)
    wide = dot(head_ref[...], spread)
    wide = jnp.broadcast_to(wide[:, None, :], (classes, hh, rows))
    keep = over(iota((classes, hh, rows), 2), ch) == iota((classes, hh, rows), 1)
    return jnp.where(keep, wide, 0.0).reshape(classes * hh, rows).astype(BF)


def bias_rows(bias_ref, ch, width):
    square = jnp.broadcast_to(bias_ref[...], (ch, ch))
    column = jnp.sum(jnp.where(iota((ch, ch), 0) == iota((ch, ch), 1), square, 0.0), axis=1, keepdims=True)
    return jnp.broadcast_to(column, (ch, width))


def shifts(x):
    before, after = moved(x)
    return jnp.concatenate([before, x, after], axis=0)


def head_pair(preact, bias, mat, head_bias_ref, label, mask, dims):
    ch, hh, ww, classes = dims
    rows = ch * hh
    preact = (preact.reshape(hh, ch, 2 * ww) + bias[None]).reshape(rows, 2 * ww)
    hidden = jnp.maximum(preact, 0.0).astype(BF)
    logits = dot(mat, hidden).reshape(classes, hh, 2 * ww)
    parts = [logits[c] + head_bias_ref[0:1, c : c + 1] for c in range(classes)]
    total = functools.reduce(jnp.add, [jnp.exp(p) for p in parts])
    log_total = jnp.log(total)
    soft = [jnp.exp(p - log_total) for p in parts]
    hot = [label == c for c in range(classes)]
    chosen = functools.reduce(jnp.add, [jnp.where(o, s, 0.0) for o, s in zip(hot, soft)])
    diffs = [s - jnp.where(o, 1.0, 0.0) for o, s in zip(hot, soft)]
    return hidden, jnp.stack(diffs).reshape(classes * hh, 2 * ww), mask * chosen


def put_pair(ref, first, second, value, ww):
    ref[first] = value[:, :ww]
    ref[second] = value[:, ww:]


def beside(ref, first, second):
    return jnp.concatenate([ref[first], ref[second]], axis=1)


def load_kernel(*refs):
    count = (len(refs) - 3) // 2
    sources, targets, (a_ref, b_ref, sems) = refs[:count], refs[count : 2 * count], refs[2 * count :]
    planes = sources[0].shape[1]
    copies = [pltpu.make_async_copy(s, t, sems.at[n]) for n, (s, t) in enumerate(zip(sources, targets))]
    for copy in copies:
        copy.start()
    copies[0].wait()
    odd = lax.rem(lax.axis_index("depth"), 2)
    a_ref[...] = targets[0][:, (1 - odd) * (planes - 1)]
    b_ref[...] = targets[0][:, odd * (planes - 1)]
    for copy in copies[1:]:
        copy.wait()


def sorted_halo(a, b):
    place, size = lax.axis_index("depth"), lax.axis_size("depth")
    odd = lax.rem(place, 2) == 1
    before, after = jnp.where(odd, a, b), jnp.where(odd, b, a)
    before = jnp.where(place > 0, before, 0.0)
    after = jnp.where(place < size - 1, after, 0.0)
    return before.astype(BF), after.astype(BF)


def turner(ch, hh):
    rows = ch * hh
    row, col = iota((rows, rows), 0), iota((rows, rows), 1)
    return ((over(row, ch) == rest(col, hh)) & (rest(row, ch) == over(col, hh))).astype(F32).astype(BF)


def interior_kernel(
    x_ref, label_ref, mask_ref, kernel_ref, bias_ref, head_ref, head_bias_ref,
    band_ref, mat_ref, mat_t_ref, turner_ref, bias_out_ref,
    shifted_ref, turned_ref, hidden_ref, diff_ref, offered_ref,
):
    ch, planes, hh, ww = x_ref.shape
    classes = head_ref.shape[0]
    rows = ch * hh
    inner = planes - 2
    fill_band(kernel_ref, band_ref, ch, hh)
    mat = head_matrix(head_ref, ch, hh, classes)
    bias = bias_rows(bias_ref, ch, 2 * ww)
    field = [x_ref[:, d].reshape(rows, ww) for d in range(planes)]
    for d in range(planes):
        shifted_ref[d] = shifts(field[d])
    wide = [shifted_ref[d : d + 3].reshape(9 * rows, ww) for d in range(inner)]
    preact = dot(band_ref[...], jnp.concatenate(wide, axis=1))
    for d in range(0, inner, 2):
        hidden, diff, offered = head_pair(
            preact[:, d * ww : (d + 2) * ww], bias, mat, head_bias_ref, beside(label_ref, d + 1, d + 2),
            beside(mask_ref, d + 1, d + 2).astype(F32), (ch, hh, ww, classes),
        )
        put_pair(hidden_ref, d, d + 1, hidden, ww)
        put_pair(diff_ref, d, d + 1, diff, ww)
        put_pair(offered_ref, d, d + 1, offered, ww)
    turn = turner(ch, hh)
    turned = dot(turn, jnp.concatenate(field, axis=1)).astype(BF)
    for d in range(planes):
        turned_ref[d] = turned[:, d * ww : (d + 1) * ww]
    unit = (iota((rows, rows), 0) == iota((rows, rows), 1)).astype(F32).astype(BF)
    mat_ref[...], mat_t_ref[...], turner_ref[...], bias_out_ref[...] = mat, dot_nt(unit, mat).astype(BF), turn, bias


def edge_kernel(
    a_ref, b_ref, label_ref, mask_ref, head_bias_ref, band_ref, mat_ref, bias_ref, shifted_ref,
    halo_ref, hidden_ref, diff_ref, offered_ref,
):
    ch, hh, ww = a_ref.shape
    planes, classes = label_ref.shape[0], mat_ref.shape[0] // hh
    rows = ch * hh
    before, after = sorted_halo(a_ref[...].reshape(rows, ww).astype(F32), b_ref[...].reshape(rows, ww).astype(F32))
    left = jnp.concatenate([shifts(before), shifted_ref[0:2].reshape(6 * rows, ww)], axis=0)
    right = jnp.concatenate([shifted_ref[planes - 2 : planes].reshape(6 * rows, ww), shifts(after)], axis=0)
    preact = dot(band_ref[...], jnp.concatenate([left, right], axis=1))
    hidden, diff, offered = head_pair(
        preact, bias_ref[...], mat_ref[...], head_bias_ref, beside(label_ref, 0, planes - 1),
        beside(mask_ref, 0, planes - 1).astype(F32), (ch, hh, ww, classes),
    )
    put_pair(hidden_ref, 0, 1, hidden, ww)
    put_pair(diff_ref, 0, 1, diff, ww)
    put_pair(offered_ref, 0, 1, offered, ww)
    halo_ref[0], halo_ref[1] = before, after


def backward_planes(diff_ref, weight_ref, hidden_ref, mat_t_ref, shifted_ref):
    count, rows, ww = hidden_ref.shape
    hh = weight_ref.shape[1]
    classes = diff_ref.shape[1] // hh
    offset_sum, halves = 0.0, []
    for d in range(count):
        grad = (diff_ref[d].reshape(classes, hh, ww) * weight_ref[d][None]).reshape(classes * hh, ww)
        offset_sum = offset_sum + grad
        halves.append(grad.astype(BF))
    halves = jnp.concatenate(halves, axis=1)
    hiddens = jnp.concatenate([hidden_ref[d] for d in range(count)], axis=1)
    pre = jnp.where(hiddens.astype(F32) > 0.0, dot(mat_t_ref[...], halves), 0.0)
    bias_sum = sum(pre[:, d * ww : (d + 1) * ww] for d in range(count))
    values = [pre[:, d * ww : (d + 1) * ww].astype(BF) for d in range(count)]
    for d in range(count):
        before, after = moved(values[d])
        shifted_ref[d] = jnp.concatenate([after, values[d], before], axis=0)
    return values, bias_sum, offset_sum, dot_nt(halves, hiddens)


STEP = 2


def weight_products(shifted_ref, fields, ch, hh, totals):
    count, rows3, ww = shifted_ref.shape
    rows = rows3 // 3
    span = STEP + 2
    spot = rest(over(iota((ch, 256), 1), ch), span)
    grads = [shifted_ref[d] for d in range(count)]
    for h0 in range(0, hh, STEP):
        step = min(STEP, hh - h0)
        left = [g[k * rows + h0 * ch : k * rows + (h0 + step) * ch] for k in range(3) for g in grads]
        left = [jnp.concatenate(left[k * count : (k + 1) * count], axis=1) for k in range(3)]
        low, high = max(h0 - 1, 0), min(h0 + span - 1, hh)
        right = []
        for i in range(3):
            if h0 == 0:
                right.append(jnp.zeros((ch, count * ww), BF))
            right.append(jnp.concatenate([f[low * ch : high * ch] for f in fields[i]], axis=1))
            if h0 + span - 1 > hh:
                right.append(jnp.zeros(((h0 + span - 1 - hh) * ch, count * ww), BF))
        right.append(jnp.zeros((256 - 3 * span * ch, count * ww), BF))
        product = dot_nt(jnp.concatenate(left, axis=0), jnp.concatenate(right, axis=0))
        for k in range(3):
            for j in range(3):
                total = jnp.zeros((ch, 256), F32)
                for h in range(step):
                    r = (k * step + h) * ch
                    total = jnp.where(spot == h + j, product[r : r + ch], total)
                totals[3 * k + j] = totals[3 * k + j] + total
    return totals


def inner_backward_kernel(
    turned_ref, weight_ref, hidden_ref, diff_ref, mat_t_ref, halo_ref, turner_ref,
    shifted_ref, total_ref, bias_ref, offset_ref, product_ref, halo_turned_ref,
):
    inner, rows, ww = hidden_ref.shape
    put_pair(halo_turned_ref, 0, 1, dot(turner_ref[...], beside(halo_ref, 0, 1)).astype(BF), ww)
    hh = weight_ref.shape[1]
    _, bias_ref[...], offset_ref[...], product_ref[...] = backward_planes(
        diff_ref, weight_ref, hidden_ref, mat_t_ref, shifted_ref
    )
    fields = [[turned_ref[d + i] for d in range(inner)] for i in range(3)]
    totals = weight_products(shifted_ref, fields, rows // hh, hh, [0.0] * 9)
    for n in range(9):
        total_ref[n] = totals[n]


def edge_backward_kernel(
    turned_ref, halo_ref, weight_ref, hidden_ref, diff_ref, mat_t_ref, total_ref, bias_in_ref, offset_in_ref, product_in_ref,
    packed_ref, a_ref, b_ref, shifted_ref, rows_ref,
):
    planes, rows, ww = turned_ref.shape
    hh = weight_ref.shape[1]
    ch, classes = rows // hh, diff_ref.shape[1] // hh
    values, bias_sum, offset_sum, product = backward_planes(diff_ref, weight_ref, hidden_ref, mat_t_ref, shifted_ref)
    bias_sum, offset_sum = bias_sum + bias_in_ref[...], offset_sum + offset_in_ref[...]
    product = product + product_in_ref[...]
    product = product.reshape(classes, hh, rows)
    keep = over(iota((classes, hh, rows), 2), ch) == iota((classes, hh, rows), 1)
    head = jnp.sum(jnp.where(keep, product, 0.0), axis=1)
    by_last = (rest(iota((rows, 128), 0), ch) == rest(iota((rows, 128), 1), 16)).astype(F32).astype(BF)
    head = dot_exact(head, by_last)
    bias = jnp.sum(jnp.sum(bias_sum.reshape(hh, ch, ww), axis=0), axis=1, keepdims=True)
    offset = jnp.sum(jnp.sum(offset_sum.reshape(classes, hh, ww), axis=1), axis=1, keepdims=True)
    odd = lax.rem(lax.axis_index("depth"), 2) == 1
    first, last = values[0].astype(F32), values[1].astype(F32)
    a_ref[...] = jnp.where(odd, first, last).astype(BF)
    b_ref[...] = jnp.where(odd, last, first).astype(BF)
    fields = [
        [halo_ref[0], turned_ref[planes - 2]],
        [turned_ref[0], turned_ref[planes - 1]],
        [turned_ref[1], halo_ref[1]],
    ]
    totals = weight_products(shifted_ref, fields, ch, hh, [total_ref[n] for n in range(9)])
    part = over(iota((ch, 256), 1), ch * (STEP + 2))
    for half in range(2):
        for t in range(27):
            i, j, k = t // 9, t // 3 % 3, t % 3
            value = jnp.where(part == i, totals[3 * k + j], 0.0)
            rows_ref[half, pl.ds(t, ch, stride=27)] = value[:, 128 * half : 128 * half + 128]
    pick = (rest(iota((ch, 256), 1), ch) == iota((ch, 256), 0)).astype(F32).astype(BF)
    sums = sum(dot_nt(pick, part) for part in split(jnp.concatenate([rows_ref[0], rows_ref[1]], axis=1)))
    for q in range(3):
        packed_ref[q * ch : (q + 1) * ch] = sums[:, 128 * q : 128 * q + 128]
    lane = iota((8, 128), 1)
    small = jnp.where(lane < 112, head, jnp.where(lane == 112, bias[:8], jnp.where(lane == 113, bias[8:], offset)))
    last = jnp.concatenate([sums[:, 384:], jnp.zeros((ch, 80), F32)], axis=1)
    low, high = last[:8], pltpu.roll(last[8:], 48, 1)
    packed_ref[3 * ch :] = jnp.where(lane < 48, low, jnp.where(lane < 96, high, small))


def input_kernel(a_ref, b_ref, shifted_ref, edge_ref, band_ref, out_ref, token_ref, turned_ref, grad_ref, sems):
    token_ref[...] = jnp.zeros_like(token_ref)
    ch, planes, hh, ww = grad_ref.shape
    rows = ch * hh
    unit = (iota((rows, rows), 0) == iota((rows, rows), 1)).astype(F32).astype(BF)
    for i in range(3):
        for k in range(3):
            block = band_ref[:, (3 * i + k) * rows : (3 * i + k + 1) * rows]
            col = (3 * (2 - i) + k) * rows
            turned_ref[:, col : col + rows] = dot_nt(unit, block).astype(BF)
    ends = []
    for x in sorted_halo(a_ref[...].astype(F32), b_ref[...].astype(F32)):
        before, after = moved(x)
        ends.append(jnp.concatenate([after, x, before], axis=0))
    field = [ends[0], edge_ref[0]] + [shifted_ref[d] for d in range(planes - 2)] + [edge_ref[1], ends[1]]
    part, copies = planes // 2, []
    for n in range(2):
        own = range(n * part, (n + 1) * part)
        wide = [jnp.concatenate(field[d : d + 3], axis=0) for d in own]
        grad = dot(turned_ref[...], jnp.concatenate(wide, axis=1)).astype(BF)
        for d in own:
            grad_ref[:, d] = grad[:, (d - n * part) * ww : (d - n * part + 1) * ww].reshape(ch, hh, ww)
        span = pl.ds(n * part, part)
        copies.append(pltpu.make_async_copy(grad_ref.at[:, span], out_ref.at[:, span], sems.at[n]))
        copies[-1].start()
    for copy in copies:
        copy.wait()


def unpack_kernel(scale, token_ref, own_ref, *refs):
    del token_ref
    others, (kernel_ref, bias_ref, head_ref, offset_ref) = refs[:-4], refs[-4:]
    ch = kernel_ref.shape[0]
    total = functools.reduce(jnp.add, [r[...] for r in others], own_ref[...]) * scale
    tail = total[3 * ch :]
    tiles = [total[q * ch : (q + 1) * ch] for q in range(3)]
    tiles.append(jnp.concatenate([tail, pltpu.roll(tail, 80, 1)], axis=0))
    lane = iota((ch, 128), 1)
    for co in range(ch):
        q, off = 27 * co // 128, 27 * co % 128
        value = pltpu.roll(tiles[q], 128 - off, 1) if off else tiles[q]
        if off + 27 > 128:
            value = jnp.where(lane < 128 - off, value, pltpu.roll(tiles[q + 1], 128 - off, 1))
        kernel_ref[co] = value[:, 0:27]
    head_ref[...] = pltpu.roll(tail, 32, 1)[:, 0:16]
    column, row = iota((8, ch), 1), iota((8, ch), 0)
    low = jnp.where(column == row, tail[:, 112:113], 0.0) + jnp.where(column == row + 8, tail[:, 113:114], 0.0)
    bias_ref[...] = jnp.sum(low, axis=0, keepdims=True)
    diagonal = jnp.where(column[:, :8] == row[:, :8], tail[:, 114:115], 0.0)
    offset_ref[...] = jnp.sum(diagonal, axis=0, keepdims=True)


def call(kernel, out_shape, in_spaces, scratch, flops, args, out_spaces=None):
    moved_bytes = sum(a.size * a.dtype.itemsize for a in args)
    return pl.pallas_call(
        kernel,
        out_shape=out_shape,
        in_specs=[pl.BlockSpec(memory_space=s) for s in in_spaces],
        out_specs=jax.tree.map(
            lambda _, s: pl.BlockSpec(memory_space=s), out_shape, out_spaces or jax.tree.map(lambda _: VM, out_shape)
        ),
        scratch_shapes=scratch,
        compiler_params=pltpu.CompilerParams(vmem_limit_bytes=32 << 20),
        cost_estimate=pl.CostEstimate(flops=flops, bytes_accessed=moved_bytes, transcendentals=0),
    )(*args)


def exchange_pairs():
    crops, size = lax.axis_size("dp"), lax.axis_size("depth")
    one, two = [], []
    for c in range(crops):
        for d in range(size):
            one.append((c * size + d, c * size + (d ^ 1)))
            e = ((d + 1) ^ 1) - 1
            if 0 <= e < size:
                two.append((c * size + d, c * size + e))
            elif crops % 2 == 0:
                two.append((c * size + d, (c ^ 1) * size + d))
    return one, two


def exchanged(a, b):
    one, two = exchange_pairs()
    return lax.ppermute(a, ("dp", "depth"), one), lax.ppermute(b, ("dp", "depth"), two)


def reduction_rounds():
    count = lax.axis_size("dp") * lax.axis_size("depth")
    bits = [1 << b for b in range((count - 1).bit_length())]
    bits = bits[-1:] + bits[1:2] + bits[:1] + bits[2:-1] if len(bits) >= 4 else bits
    rounds = []
    for n in range(0, len(bits), 2):
        masks = bits[n : n + 2]
        masks = masks + [sum(masks)] if len(masks) == 2 else masks
        rounds.append([[(i, i ^ m) for i in range(count)] for m in masks])
    return rounds


def body(features, labels, masks, conv_kernel, conv_bias, head_weight, head_bias):
    x, label, mask = features[0, 0], labels[0], masks[0, 0]
    kernel, head = conv_kernel[0], head_weight[0]
    ch, planes, hh, ww = x.shape
    classes = head.shape[0]
    rows = ch * hh
    sds = jax.ShapeDtypeStruct
    size = lax.axis_size("depth")
    pair_flops = 2 * rows * 9 * rows * 2 * ww

    plane = sds((ch, hh, ww), BF)
    inputs = (x, label, mask, kernel.transpose(1, 2, 0), conv_bias, head, head_bias)
    inputs = tuple(pltpu.with_memory_space_constraint(v, pltpu.HBM) for v in inputs)
    shapes = tuple(sds(v.shape, v.dtype) for v in inputs)
    *inputs, end_a, end_b = call(
        load_kernel,
        (*shapes, plane, plane),
        (pltpu.HBM,) * len(inputs),
        [pltpu.SemaphoreType.DMA((len(inputs),))],
        0,
        inputs,
    )
    x, label, mask, kernel, conv_bias, head, head_bias = inputs
    far = exchanged(end_a, end_b)
    inner = planes - 2
    band, mat, mat_t, turn, bias, shifted, turned_x, hidden_in, diff_in, offered_in = call(
        interior_kernel,
        (
            sds((rows, 9 * rows), BF),
            sds((classes * hh, rows), BF),
            sds((rows, classes * hh), BF),
            sds((rows, rows), BF),
            sds((ch, 2 * ww), F32),
            sds((planes, 3 * rows, ww), BF),
            sds((planes, rows, ww), BF),
            sds((inner, rows, ww), BF),
            sds((inner, classes * hh, ww), F32),
            sds((inner, hh, ww), F32),
        ),
        (VM,) * 7,
        [],
        pair_flops * inner // 2,
        (x, label, mask, kernel, conv_bias, head, head_bias),
    )
    peers = [(0, 1), (1, 0)]
    weight_in = lax.ppermute(offered_in, "net", peers)
    halo, hidden_edge, diff_edge, offered_edge = call(
        edge_kernel,
        (
            sds((2, rows, ww), BF),
            sds((2, rows, ww), BF),
            sds((2, classes * hh, ww), F32),
            sds((2, hh, ww), F32),
        ),
        (VM,) * 9,
        [],
        pair_flops,
        (*far, label, mask, head_bias, band, mat, bias, shifted),
    )
    weight_edge = lax.ppermute(offered_edge, "net", peers)
    sums = (
        sds((9, ch, 256), F32),
        sds((rows, ww), F32),
        sds((classes * hh, ww), F32),
        sds((classes * hh, rows), F32),
    )
    grads, *sums, halo = call(
        inner_backward_kernel,
        (sds((inner, 3 * rows, ww), BF), *sums, sds((2, rows, ww), BF)),
        (VM,) * 7,
        [],
        pair_flops * inner // 2,
        (turned_x, weight_in, hidden_in, diff_in, mat_t, halo, turn),
    )
    edge = sds((rows, ww), BF)
    packed, grad_a, grad_b, grad_edge = call(
        edge_backward_kernel,
        (sds((3 * ch + 8, 128), F32), edge, edge, sds((2, 3 * rows, ww), BF)),
        (VM,) * 10,
        [VM((2, 27 * ch, 128), F32)],
        pair_flops,
        (turned_x, halo, weight_edge, hidden_edge, diff_edge, mat_t, *sums),
    )
    rounds, pairs = reduction_rounds(), exchange_pairs()
    for n, masks in enumerate(rounds):
        others = [lax.ppermute(packed, ("dp", "depth"), p) for p in masks]
        if n == 0:
            grad_far = [lax.ppermute(e, ("dp", "depth"), p) for e, p in zip((grad_a, grad_b), pairs)]
        if n < len(rounds) - 1:
            packed = functools.reduce(jnp.add, others, packed)
        if n == len(rounds) - 2:
            packed, band = lax.optimization_barrier((packed, band))
    grad_input, token = call(
        input_kernel,
        (sds((ch, planes, hh, ww), BF), sds((8, 128), F32)),
        (VM,) * 5,
        [VM((rows, 9 * rows), BF), VM((ch, planes, hh, ww), BF), pltpu.SemaphoreType.DMA((2,))],
        pair_flops * planes // 2,
        (*grad_far, grads, grad_edge, band),
        (pltpu.HBM, VM),
    )
    scale = 1.0 / (lax.axis_size("dp") * size * planes * hh * ww)
    grad_kernel, grad_bias, grad_head, grad_offset = call(
        functools.partial(unpack_kernel, scale),
        (sds((ch, ch, 27), F32), sds((1, ch), F32), sds((classes, ch), F32), sds((1, classes), F32)),
        (VM,) * (2 + len(others)),
        [],
        1000,
        (token, packed, *others),
    )
    return (
        grad_input[None, None],
        grad_kernel.transpose(2, 0, 1)[None],
        grad_bias,
        grad_head[None],
        grad_offset,
    )


def solution(mesh):
    in_specs = (
        P("net", "dp", None, "depth", None, None),
        P("dp", "depth", None, None),
        P("net", "dp", "depth", None, None),
        P("net", None, None, None),
        P("net", None),
        P("net", None, None),
        P("net", None),
    )
    out_specs = (
        P("net", "dp", None, "depth", None, None),
        P("net", None, None, None),
        P("net", None),
        P("net", None, None),
        P("net", None),
    )
    return jax.shard_map(body, mesh=mesh, in_specs=in_specs, out_specs=out_specs, check_vma=False)
```
